128 devices in a mesh: row: 8 (over y_lo, z), col: 16 (over y_hi, x, core).
Axes of the slice: x: 4, y: 4 (y_hi: 2, y_lo: 2; y = y_hi * 2 + y_lo), z: 4, core: 2. Of those that a mesh axis runs over, the one named last changes fastest.
Arguments:
- embedding: float32 [16384, 256], P(('row', 'col')), may hold values from -6 to 6
- seed_cluster: int32 [16384], P(('row', 'col')), may hold values from 0 to 127
Outputs:
- log_member: float32 [16384, 128], P(('row', 'col'))
The draws below stay inside these ranges and needn't reach their ends.
All inputs are finite; a program needn't handle non-finite values.
Results may differ from the reference program's by a relative error of at most 0.0003.
Values sent between devices are 32-bit elements; how exact they have to be, the bound alone decides.
No kernel may reach another device: no remote copies, remote signals or barrier semaphores. Data moves between devices by JAX's collectives and lax.ppermute only.
A program may use at most 64 MiB of HBM per device.

```python
import jax
import jax.numpy as jnp
from jax import lax

FEATURES = 256
CLUSTER_COUNT = 128
POINTS_DEV = 128
SWEEPS = 2
POINTS = 16384
N_COL = 16


def set_ends(result, own_key, smallest, top_value):
    longest = result.shape.index(max(result.shape))
    spots = []
    for shift in (0, 1):
        where = [jax.random.randint(jax.random.fold_in(own_key, axis), (), 0, length) for axis, length in enumerate(result.shape)]
        where[longest] = (where[longest] + shift) % result.shape[longest]
        spots.append(tuple(where))
    return result.at[spots[0]].set(smallest).at[spots[1]].set(top_value)


def block_scale(rng, dims, shards, least, top_value):
    level = 1.0
    for axis_at, parts in shards:
        steps = jax.random.uniform(jax.random.fold_in(jax.random.fold_in(rng, 6), axis_at), (parts,), jnp.float32, least / len(shards), top_value / len(shards))
        level = level * jnp.repeat(jnp.exp(steps), dims[axis_at] // parts).reshape((-1,) + (1,) * (len(dims) - 1 - axis_at))
    return level


def centred(stream_key, shape, spread, limit, shards=(), kind=jnp.bfloat16):
    entries = spread * jax.random.normal(stream_key, shape, jnp.float32)
    if shards:
        entries = entries * block_scale(stream_key, shape, shards, -0.22, 0.18)
    return jnp.clip(entries, -limit, limit).astype(kind)


def setup_inputs(seed: int = 0) -> dict:
    streams_of = jax.random.split(jax.random.key(seed), 3)
    return {
        "embedding": centred(streams_of[0], (POINTS, FEATURES), 1.0, 6.0, ((0, 128),), jnp.float32),
        "seed_cluster": set_ends(jax.random.randint(streams_of[1], (POINTS,), 0, CLUSTER_COUNT), jax.random.fold_in(streams_of[1], 1), 0, CLUSTER_COUNT - 1).astype(jnp.int32),
    }


ANNEAL_TEMP_VALUE = 0.02

def reference(embedding, seed_cluster):
    total = embedding.shape[0]
    squared_norms = lax.optimization_barrier(jnp.sum(embedding * embedding, axis=1))
    cluster_labels = jnp.arange(CLUSTER_COUNT, dtype=jnp.int32)
    member = 0.5 * (seed_cluster[:, None] == cluster_labels[None, :]).astype(jnp.float32) + 0.5 / CLUSTER_COUNT
    height = POINTS_DEV * N_COL
    blocks_x = embedding.reshape(total // height, height, FEATURES)
    blocks_s = squared_norms.reshape(total // height, height)
    log_member = jnp.zeros((total, CLUSTER_COUNT), jnp.float32)
    for sweep in range(SWEEPS):

        def single_block(pair):
            rows, row_sq = pair
            inner = jnp.dot(rows, embedding.T, precision=lax.Precision.HIGHEST)
            distance = jnp.sqrt(row_sq[:, None] + squared_norms[None, :] - 2.0 * inner + 1.0)
            return jnp.dot(distance, member, precision=lax.Precision.HIGHEST)
        attraction = lax.map(single_block, (blocks_x, blocks_s)).reshape(total, CLUSTER_COUNT)
        counts = lax.optimization_barrier(jnp.sum(member, axis=0))
        cohesion = lax.optimization_barrier(jnp.sum(member * attraction, axis=0))
        pair_energy = attraction / counts[None, :] - cohesion[None, :] / (2.0 * counts[None, :] ** 2)
        member_logits = -pair_energy / ANNEAL_TEMP_VALUE
        highest = lax.optimization_barrier(jnp.max(member_logits, axis=1, keepdims=True))
        log_member = member_logits - highest - jnp.log(lax.optimization_barrier(jnp.sum(jnp.exp(member_logits - highest), axis=1, keepdims=True)))
        member = jnp.exp(log_member)
    return log_member
```

```python
import itertools

import jax
import jax.numpy as jnp
from jax import lax
from jax.sharding import Mesh
from jax.sharding import PartitionSpec as P

CLUSTER_COUNT = 128
ANNEAL_TEMP_VALUE = 0.02
SIDE = 8

EVERY = ("y_lo", "z", "y_hi", "x", "core")
SIZES = (2, 4, 2, 4, 2)


def place(y_lo, z, y_hi, x, core):
    return (((y_lo * 4 + z) * 2 + y_hi) * 4 + x) * 2 + core


def column_groups():
    groups = []
    for pair, x, core in itertools.product(range(2), range(4), range(2)):
        groups.append([place(lo, z, lo ^ pair, x, core) for lo in range(2) for z in range(4)])
    return groups


COLUMN_GROUPS = column_groups()


def exchange_rows(blocks):
    return lax.all_to_all(blocks, ("y_lo", "x"), 0, 0, tiled=True)


def exchange_columns(blocks):
    return lax.all_to_all(blocks, EVERY, 0, 0, axis_index_groups=COLUMN_GROUPS, tiled=True)


def copies(x, count):
    return jnp.broadcast_to(x, (count, *x.shape))


def other_core(x):
    return lax.ppermute(x, "core", [(0, 1), (1, 0)])


def first_member(seeds):
    labels = jnp.arange(CLUSTER_COUNT, dtype=jnp.float32)
    return 0.5 * (seeds[:, None] == labels[None, :]).astype(jnp.float32) + 0.5 / CLUSTER_COUNT


def log_softmax_energy(attraction, counts, cohesion):
    energy = attraction / counts - cohesion / (2.0 * counts**2)
    logits = -energy / ANNEAL_TEMP_VALUE
    highest = jnp.max(logits, axis=1, keepdims=True)
    return logits - highest - jnp.log(jnp.sum(jnp.exp(logits - highest), axis=1, keepdims=True))


def points_of(blocks, points):
    return blocks[:, :points].reshape(-1, blocks.shape[-1])


def shards(embedding, seed_cluster):
    points, width = embedding.shape
    side = jnp.concatenate([seed_cluster.astype(jnp.float32), jnp.sum(embedding * embedding, axis=1)])
    block = jnp.concatenate([embedding, jnp.broadcast_to(side, (SIDE, width))], axis=0)
    spread = copies(block, 8)
    rows = exchange_rows(spread)
    columns = [exchange_columns(spread)]
    columns.append(other_core(columns[0]))

    row_points, row_side = points_of(rows, points), rows[:, points]
    row_seeds, row_sq = row_side[:, :points].reshape(-1), row_side[:, points:].reshape(-1)
    distances, weighted = [], 0.0
    for part in columns:
        part_side = part[:, points]
        seeds, sq = part_side[:, :points].reshape(-1), part_side[:, points:].reshape(-1)
        inner = jnp.dot(row_points, points_of(part, points).T, precision=lax.Precision.HIGH)
        distance = jnp.sqrt(row_sq[:, None] + sq[None, :] - 2.0 * inner + 1.0)
        distances.append(distance)
        weighted = weighted + jnp.dot(distance, first_member(seeds), precision=lax.Precision.HIGH)

    own = first_member(seed_cluster.astype(jnp.float32))
    small = jnp.stack([jnp.sum(first_member(row_seeds) * weighted, axis=0), jnp.sum(own, axis=0)])

    def summed(weighted, small):
        tail = copies(jnp.pad(small, ((0, SIDE - len(small)), (0, 0))), 8)
        blocks = jnp.concatenate([weighted.reshape(8, points, -1), tail], axis=1)
        return jnp.sum(exchange_rows(blocks), axis=0)

    first = summed(weighted, small)
    firsts = [exchange_columns(copies(first, 8))]
    firsts.append(other_core(firsts[0]))
    totals = sum(jnp.sum(part[:, points : points + 2], axis=0) for part in firsts)
    cohesion, counts = totals[:1], totals[1:]

    weighted, sizes = 0.0, 0.0
    for part, distance in zip(firsts, distances):
        member = jnp.exp(log_softmax_energy(points_of(part, points), counts, cohesion))
        sizes = sizes + jnp.sum(member, axis=0, keepdims=True)
        weighted = weighted + jnp.dot(distance, member, precision=lax.Precision.HIGH)
    own = jnp.exp(log_softmax_energy(first[:points], counts, cohesion))

    second = summed(weighted, sizes)
    attraction, counts = second[:points], second[points : points + 1]
    parts = lax.all_to_all(copies(jnp.sum(own * attraction, axis=0, keepdims=True), 128), EVERY, 0, 0, tiled=True)
    return log_softmax_energy(attraction, counts, jnp.sum(parts, axis=0))


def solution(mesh):
    finer = Mesh(mesh.devices.reshape(SIZES), EVERY)
    return jax.shard_map(
        shards, mesh=finer, in_specs=(P(EVERY, None), P(EVERY)), out_specs=P(EVERY, None), check_vma=False
    )
```

```python
import itertools

import jax
import jax.numpy as jnp
from jax import lax
from jax.sharding import Mesh
from jax.sharding import PartitionSpec as P

CLUSTER_COUNT = 128
ANNEAL_TEMP_VALUE = 0.02
SIDE = 8

EVERY = ("y_lo", "z", "y_hi", "x", "core")
SIZES = (2, 4, 2, 4, 2)


def place(y_lo, z, y_hi, x, core):
    return (((y_lo * 4 + z) * 2 + y_hi) * 4 + x) * 2 + core


def column_groups():
    groups = []
    for pair, x, core in itertools.product(range(2), range(4), range(2)):
        groups.append([place(lo, z, lo ^ pair, x, core) for lo in range(2) for z in range(4)])
    return groups


COLUMN_GROUPS = column_groups()


def exchange_rows(blocks):
    return lax.all_to_all(blocks, ("y_lo", "x"), 0, 0, tiled=True)


def exchange_columns(blocks):
    return lax.all_to_all(blocks, EVERY, 0, 0, axis_index_groups=COLUMN_GROUPS, tiled=True)


def row_peers(x):
    found = []
    for flip, step in itertools.product(range(2), range(4)):
        pairs = []
        for lo, z, hi, at, core in itertools.product(*map(range, SIZES)):
            pairs.append((place(lo ^ flip, z, hi, (at + step) % 4, core), place(lo, z, hi, at, core)))
        found.append(lax.ppermute(x, EVERY, pairs) if flip or step else x)
    return jnp.stack(found)


def by_member(blocks):
    _, *rest = blocks.shape
    blocks = blocks.reshape(2, 4, *rest)
    blocks = lax.dynamic_slice_in_dim(jnp.concatenate([blocks] * 2, 1), (4 - lax.axis_index("x")) % 4, 4, 1)
    blocks = lax.dynamic_slice_in_dim(jnp.concatenate([blocks] * 2, 0), lax.axis_index("y_lo"), 2, 0)
    return blocks.reshape(8, *rest)


def halves(x):
    high = lax.reduce_precision(x, 8, 7)
    return high.astype(jnp.bfloat16), (x - high).astype(jnp.bfloat16)


def product(a, b):
    return jnp.dot(a, b, preferred_element_type=jnp.float32)


def copies(x, count):
    return jnp.broadcast_to(x, (count, *x.shape))


def other_core(x):
    return lax.ppermute(x, "core", [(0, 1), (1, 0)])


def first_member(seeds):
    labels = jnp.arange(CLUSTER_COUNT, dtype=jnp.float32)
    return 0.5 * (seeds[:, None] == labels[None, :]).astype(jnp.float32) + 0.5 / CLUSTER_COUNT


def log_softmax_energy(attraction, counts, cohesion):
    energy = attraction / counts - cohesion / (2.0 * counts**2)
    logits = -energy / ANNEAL_TEMP_VALUE
    highest = jnp.max(logits, axis=1, keepdims=True)
    return logits - highest - jnp.log(jnp.sum(jnp.exp(logits - highest), axis=1, keepdims=True))


def points_of(blocks, points):
    return blocks[:, :points].reshape(-1, blocks.shape[-1])


def shards(embedding, seed_cluster):
    points, width = embedding.shape
    side = jnp.concatenate([seed_cluster.astype(jnp.float32), jnp.sum(embedding * embedding, axis=1)])
    block = jnp.concatenate([embedding, jnp.broadcast_to(side, (SIDE, width))], axis=0)
    spread = copies(block, 8)
    rows = row_peers(block)
    columns = [exchange_columns(spread)]
    columns.append(other_core(columns[0]))

    row_points, row_side = points_of(rows, points), rows[:, points]
    row_seeds, row_sq = row_side[:, :points].reshape(-1), row_side[:, points:].reshape(-1)
    distances, weighted = [], 0.0
    for part in columns:
        part_side = part[:, points]
        seeds, sq = part_side[:, :points].reshape(-1), part_side[:, points:].reshape(-1)
        inner = jnp.dot(row_points, points_of(part, points).T, precision=lax.Precision.HIGH)
        distance = jnp.sqrt(row_sq[:, None] + sq[None, :] - 2.0 * inner + 1.0)
        high, low = halves(distance)
        distances.append((high, low))
        member = first_member(seeds).astype(jnp.bfloat16)
        weighted = weighted + product(high, member) + product(low, member)

    own = first_member(seed_cluster.astype(jnp.float32))
    small = jnp.stack([jnp.sum(first_member(row_seeds) * weighted, axis=0), jnp.sum(own, axis=0)])

    def summed(weighted, small):
        tail = copies(jnp.pad(small, ((0, SIDE - len(small)), (0, 0))), 8)
        blocks = jnp.concatenate([by_member(weighted.reshape(8, points, -1)), tail], axis=1)
        return jnp.sum(exchange_rows(blocks), axis=0)

    first = summed(weighted, small)
    firsts = [exchange_columns(copies(first, 8))]
    firsts.append(other_core(firsts[0]))
    totals = sum(jnp.sum(part[:, points : points + 2], axis=0) for part in firsts)
    cohesion, counts = totals[:1], totals[1:]

    weighted, sizes = 0.0, 0.0
    for part, distance in zip(firsts, distances):
        member = jnp.exp(log_softmax_energy(points_of(part, points), counts, cohesion))
        sizes = sizes + jnp.sum(member, axis=0, keepdims=True)
        (high, low), (member_high, member_low) = distance, halves(member)
        weighted = weighted + product(high, member_high) + product(high, member_low) + product(low, member_high)
    own = jnp.exp(log_softmax_energy(first[:points], counts, cohesion))

    second = summed(weighted, sizes)
    attraction, counts = second[:points], second[points : points + 1]
    parts = lax.all_to_all(copies(jnp.sum(own * attraction, axis=0, keepdims=True), 128), EVERY, 0, 0, tiled=True)
    return log_softmax_energy(attraction, counts, jnp.sum(parts, axis=0))


def solution(mesh):
    finer = Mesh(mesh.devices.reshape(SIZES), EVERY)
    return jax.shard_map(
        shards, mesh=finer, in_specs=(P(EVERY, None), P(EVERY)), out_specs=P(EVERY, None), check_vma=False
    )
```

```python
import itertools

import jax
import jax.numpy as jnp
from jax import lax
from jax.sharding import Mesh
from jax.sharding import PartitionSpec as P

CLUSTER_COUNT = 128
ANNEAL_TEMP_VALUE = 0.02
SIDE = 8

EVERY = ("y_lo", "z", "y_hi", "x", "core")
SIZES = (2, 4, 2, 4, 2)


def place(y_lo, z, y_hi, x, core):
    return (((y_lo * 4 + z) * 2 + y_hi) * 4 + x) * 2 + core


def column_groups():
    groups = []
    for pair, x, core in itertools.product(range(2), range(4), range(2)):
        groups.append([place(lo, z, lo ^ pair, x, core) for lo in range(2) for z in range(4)])
    return groups


COLUMN_GROUPS = column_groups()


def exchange_rows(blocks):
    return lax.all_to_all(blocks, ("y_lo", "x"), 0, 0, tiled=True)


def exchange_columns(blocks):
    return lax.all_to_all(blocks, EVERY, 0, 0, axis_index_groups=COLUMN_GROUPS, tiled=True)


def moved(x, flip, step):
    pairs = []
    for lo, z, hi, at, core in itertools.product(*map(range, SIZES)):
        pairs.append((place(lo ^ flip, z, hi, (at + step) % 4, core), place(lo, z, hi, at, core)))
    return lax.ppermute(x, EVERY, pairs)


def row_peers(x):
    pair = jnp.stack([x, moved(x, 1, 0)])
    ring = [pair] + [moved(pair, 0, step) for step in range(1, 4)]
    return jnp.stack(ring, axis=1).reshape(8, *x.shape)


def by_member(blocks):
    _, *rest = blocks.shape
    blocks = blocks.reshape(2, 4, *rest)
    blocks = lax.dynamic_slice_in_dim(jnp.concatenate([blocks] * 2, 1), (4 - lax.axis_index("x")) % 4, 4, 1)
    blocks = lax.dynamic_slice_in_dim(jnp.concatenate([blocks] * 2, 0), lax.axis_index("y_lo"), 2, 0)
    return blocks.reshape(8, *rest)


def halves(x):
    high = lax.reduce_precision(x, 8, 7)
    return high.astype(jnp.bfloat16), (x - high).astype(jnp.bfloat16)


def product(a, b):
    return jnp.dot(a, b, preferred_element_type=jnp.float32)


def copies(x, count):
    return jnp.broadcast_to(x, (count, *x.shape))


def other_core(x):
    return lax.ppermute(x, "core", [(0, 1), (1, 0)])


def first_member(seeds):
    labels = jnp.arange(CLUSTER_COUNT, dtype=jnp.float32)
    return 0.5 * (seeds[:, None] == labels[None, :]).astype(jnp.float32) + 0.5 / CLUSTER_COUNT


def log_softmax_energy(attraction, counts, cohesion):
    energy = attraction / counts - cohesion / (2.0 * counts**2)
    logits = -energy / ANNEAL_TEMP_VALUE
    highest = jnp.max(logits, axis=1, keepdims=True)
    return logits - highest - jnp.log(jnp.sum(jnp.exp(logits - highest), axis=1, keepdims=True))


def points_of(blocks, points):
    return blocks[:, :points].reshape(-1, blocks.shape[-1])


def shards(embedding, seed_cluster):
    points, width = embedding.shape
    side = jnp.concatenate([seed_cluster.astype(jnp.float32), jnp.sum(embedding * embedding, axis=1)])
    block = jnp.concatenate([embedding, jnp.broadcast_to(side, (SIDE, width))], axis=0)
    spread = copies(block, 8)
    rows = row_peers(block)
    rows, *columns = lax.optimization_barrier((rows, exchange_columns(spread)))
    columns.append(other_core(columns[0]))

    row_points, row_side = points_of(rows, points), rows[:, points]
    row_seeds, row_sq = row_side[:, :points].reshape(-1), row_side[:, points:].reshape(-1)
    distances, weighted = [], 0.0
    for part in columns:
        part_side = part[:, points]
        seeds, sq = part_side[:, :points].reshape(-1), part_side[:, points:].reshape(-1)
        inner = jnp.dot(row_points, points_of(part, points).T, precision=lax.Precision.HIGH)
        distance = jnp.sqrt(row_sq[:, None] + sq[None, :] - 2.0 * inner + 1.0)
        high, low = halves(distance)
        distances.append((high, low))
        member = first_member(seeds).astype(jnp.bfloat16)
        weighted = weighted + product(high, member) + product(low, member)

    own = first_member(seed_cluster.astype(jnp.float32))
    small = jnp.stack([jnp.sum(first_member(row_seeds) * weighted, axis=0), jnp.sum(own, axis=0)])

    def summed(weighted, small):
        tail = copies(jnp.pad(small, ((0, SIDE - len(small)), (0, 0))), 8)
        blocks = jnp.concatenate([by_member(weighted.reshape(8, points, -1)), tail], axis=1)
        return jnp.sum(exchange_rows(blocks), axis=0)

    first = summed(weighted, small)
    firsts = [exchange_columns(copies(first, 8))]
    firsts.append(other_core(firsts[0]))
    totals = sum(jnp.sum(part[:, points : points + 2], axis=0) for part in firsts)
    cohesion, counts = totals[:1], totals[1:]

    weighted, sizes = 0.0, 0.0
    for part, distance in zip(firsts, distances):
        member = jnp.exp(log_softmax_energy(points_of(part, points), counts, cohesion))
        sizes = sizes + jnp.sum(member, axis=0, keepdims=True)
        (high, low), (member_high, member_low) = distance, halves(member)
        weighted = weighted + product(high, member_high) + product(high, member_low) + product(low, member_high)
    own = jnp.exp(log_softmax_energy(first[:points], counts, cohesion))

    second = summed(weighted, sizes)
    attraction, counts = second[:points], second[points : points + 1]
    parts = lax.all_to_all(copies(jnp.sum(own * attraction, axis=0, keepdims=True), 128), EVERY, 0, 0, tiled=True)
    return log_softmax_energy(attraction, counts, jnp.sum(parts, axis=0))


def solution(mesh):
    finer = Mesh(mesh.devices.reshape(SIZES), EVERY)
    return jax.shard_map(
        shards, mesh=finer, in_specs=(P(EVERY, None), P(EVERY)), out_specs=P(EVERY, None), check_vma=False
    )
```

```python
import itertools

import jax
import jax.numpy as jnp
from jax import lax
from jax.experimental import pallas as pl
from jax.experimental.pallas import tpu as pltpu
from jax.sharding import Mesh
from jax.sharding import PartitionSpec as P

CLUSTER_COUNT = 128
ANNEAL_TEMP_VALUE = 0.02
SIDE = 8

EVERY = ("y_lo", "z", "y_hi", "x", "core")
SIZES = (2, 4, 2, 4, 2)


def place(y_lo, z, y_hi, x, core):
    return (((y_lo * 4 + z) * 2 + y_hi) * 4 + x) * 2 + core


def column_groups():
    groups = []
    for pair, x, core in itertools.product(range(2), range(4), range(2)):
        groups.append([place(lo, z, lo ^ pair, x, core) for lo in range(2) for z in range(4)])
    return groups


COLUMN_GROUPS = column_groups()


def exchange_rows(blocks):
    return lax.all_to_all(blocks, ("y_lo", "x"), 0, 0, tiled=True)


def exchange_columns(blocks):
    return lax.all_to_all(blocks, EVERY, 0, 0, axis_index_groups=COLUMN_GROUPS, tiled=True)


def moved(x, flip, step):
    pairs = []
    for lo, z, hi, at, core in itertools.product(*map(range, SIZES)):
        pairs.append((place(lo ^ flip, z, hi, (at + step) % 4, core), place(lo, z, hi, at, core)))
    return lax.ppermute(x, EVERY, pairs)


def row_peers(x):
    pair = jnp.stack([x, moved(x, 1, 0)])
    ring = [pair] + [moved(pair, 0, step) for step in range(1, 4)]
    return jnp.stack(ring, axis=1).reshape(8, *x.shape)


def member_order():
    y_lo, x = lax.axis_index("y_lo"), lax.axis_index("x")
    offset = jnp.arange(8, dtype=jnp.int32)
    return (y_lo ^ (offset // 4)) * 4 + (x + offset % 4) % 4


def halves(x):
    high = x.astype(jnp.bfloat16)
    return high, (x - high.astype(jnp.float32)).astype(jnp.bfloat16)


def product(a, b):
    return jnp.dot(a, b, preferred_element_type=jnp.float32)


def seed_member(seeds):
    labels = lax.broadcasted_iota(jnp.int32, (CLUSTER_COUNT, seeds.shape[1]), 0).astype(jnp.float32)
    return 0.5 * (labels == seeds).astype(jnp.float32).T + 0.5 / CLUSTER_COUNT


def store_by_member(order, total, tail, out):
    points = out.shape[1] - SIDE
    for offset in range(8):
        member = order[offset]
        out[member, pl.ds(0, points)] = total[pl.ds(offset * points, points)]
        out[member, pl.ds(points, SIDE)] = tail


def tail_rows(*lines):
    at = lax.broadcasted_iota(jnp.int32, (SIDE, CLUSTER_COUNT), 0)
    tail = jnp.zeros((SIDE, CLUSTER_COUNT), jnp.float32)
    for index, line in enumerate(lines):
        tail = jnp.where(at == index, line, tail)
    return tail


STEPS = 8
TILE = 256
CHUNK = 256


def pair_kernel(order, rows, own, other, high_out, low_out, out, left, squares, total):
    step = pl.program_id(0)
    points, width = rows.shape[1] - SIDE, rows.shape[2]

    @pl.when(step == 0)
    def _():
        for offset in range(8):
            x = rows[offset, pl.ds(0, points)]
            at = pl.ds(offset * points, points)
            squares[at] = jnp.broadcast_to(jnp.sum(x * x, axis=1, keepdims=True) + 1.0, (points, 128))
            high, low = halves(-2.0 * x)
            left[at, pl.ds(0, width)] = high
            left[at, pl.ds(width, width)] = high
            left[at, pl.ds(2 * width, width)] = low
        total[...] = jnp.zeros_like(total)

    columns = jnp.where(step < STEPS // 2, own[...], other[...])
    high, low = halves(columns[:, :points].reshape(TILE, width))
    right = jnp.concatenate([high, low, high], axis=1)
    side = [columns[block, points : points + 1] for block in range(2)]
    sq = jnp.concatenate([line[:, points:] for line in side], axis=1)
    member = jnp.concatenate([seed_member(line[:, :points]) for line in side], axis=0).astype(jnp.bfloat16)
    for chunk in range(total.shape[0] // CHUNK):
        at = pl.ds(chunk * CHUNK, CHUNK)
        inner = lax.dot_general(left[at], right, (((1,), (1,)), ((), ())), preferred_element_type=jnp.float32)
        squared = inner + jnp.concatenate([squares[at]] * 2, axis=1) + sq
        high, low = halves(squared * lax.rsqrt(squared))
        high_out[0, at] = high
        low_out[0, at] = low
        total[at] += product(high, member) + product(low, member)

    @pl.when(step == STEPS - 1)
    def _():
        cohesion = jnp.zeros((1, CLUSTER_COUNT), jnp.float32)
        for offset in range(8):
            member = seed_member(rows[offset, pl.ds(points, 1)][:, :points])
            if offset == 0:
                counts = jnp.sum(member, axis=0, keepdims=True)
            cohesion += jnp.sum(member * total[pl.ds(offset * points, points)], axis=0, keepdims=True)
        store_by_member(order, total, tail_rows(cohesion, counts), out)


def member_kernel(order, own, other, high_in, low_in, out, sums, total):
    step = pl.program_id(0)
    points = own.shape[1] - SIDE

    @pl.when(step == 0)
    def _():
        sums[...] = jnp.zeros_like(sums)
        for block in range(8):
            sums[...] += own[block, pl.ds(points, SIDE)] + other[block, pl.ds(points, SIDE)]
        sums[pl.ds(2, 1)] = jnp.zeros((1, CLUSTER_COUNT), jnp.float32)
        total[...] = jnp.zeros_like(total)

    first = (step % (STEPS // 2)) * 2
    attraction = jnp.where(step < STEPS // 2, own[pl.ds(first, 2)], other[pl.ds(first, 2)])
    attraction = attraction[:, :points].reshape(TILE, CLUSTER_COUNT)
    member = jnp.exp(log_softmax_energy(attraction, sums[pl.ds(1, 1)], sums[pl.ds(0, 1)]))
    sums[pl.ds(2, 1)] += jnp.sum(member, axis=0, keepdims=True)
    high, low = halves(member)
    both = jnp.concatenate([high, low], axis=1)
    for chunk in range(total.shape[0] // CHUNK):
        at = pl.ds(chunk * CHUNK, CHUNK)
        wide = product(high_in[0, at], both)
        total[at] += wide[:, :CLUSTER_COUNT] + wide[:, CLUSTER_COUNT:] + product(low_in[0, at], high)

    @pl.when(step == STEPS - 1)
    def _():
        store_by_member(order, total, tail_rows(sums[pl.ds(2, 1)]), out)


PARAMS = pltpu.CompilerParams(dimension_semantics=("arbitrary",), vmem_limit_bytes=40 << 20)


def pairs(order, rows, own, other):
    blocks, lines, width = rows.shape
    tall = blocks * (lines - SIDE)
    half = STEPS // 2
    tile = lambda where: pl.BlockSpec((2, lines, width), where)
    piece = pl.BlockSpec((1, tall, TILE), lambda step, order: (step, 0, 0))
    kept = jax.ShapeDtypeStruct((STEPS, tall, TILE), jnp.bfloat16)
    return pl.pallas_call(
        pair_kernel,
        out_shape=(kept, kept, jax.ShapeDtypeStruct((blocks, lines, CLUSTER_COUNT), jnp.float32)),
        grid_spec=pltpu.PrefetchScalarGridSpec(
            num_scalar_prefetch=1,
            grid=(STEPS,),
            in_specs=[
                pl.BlockSpec((blocks, lines, width), lambda step, order: (0, 0, 0)),
                tile(lambda step, order: (jnp.minimum(step, half - 1), 0, 0)),
                tile(lambda step, order: (jnp.maximum(step - half, 0), 0, 0)),
            ],
            out_specs=[piece, piece, pl.BlockSpec((blocks, lines, CLUSTER_COUNT), lambda step, order: (0, 0, 0))],
            scratch_shapes=[
                pltpu.VMEM((tall, 3 * width), jnp.bfloat16),
                pltpu.VMEM((tall, 128), jnp.float32),
                pltpu.VMEM((tall, CLUSTER_COUNT), jnp.float32),
            ],
        ),
        compiler_params=PARAMS,
        name="pairs",
    )(order, rows, own, other)


def members(order, own, other, high, low):
    blocks, lines, clusters = own.shape
    tall = blocks * (lines - SIDE)
    whole = pl.BlockSpec((blocks, lines, clusters), lambda step, order: (0, 0, 0))
    piece = pl.BlockSpec((1, tall, TILE), lambda step, order: (step, 0, 0))
    return pl.pallas_call(
        member_kernel,
        out_shape=jax.ShapeDtypeStruct(own.shape, jnp.float32),
        grid_spec=pltpu.PrefetchScalarGridSpec(
            num_scalar_prefetch=1,
            grid=(STEPS,),
            in_specs=[whole, whole, piece, piece],
            out_specs=whole,
            scratch_shapes=[pltpu.VMEM((SIDE, clusters), jnp.float32), pltpu.VMEM((tall, clusters), jnp.float32)],
        ),
        compiler_params=PARAMS,
        name="members",
    )(order, own, other, high, low)


def copies(x, count):
    return jnp.broadcast_to(x, (count, *x.shape))


def other_core(x):
    return lax.ppermute(x, "core", [(0, 1), (1, 0)])


def log_softmax_energy(attraction, counts, cohesion):
    energy = attraction / counts - cohesion / (2.0 * counts**2)
    logits = -energy / ANNEAL_TEMP_VALUE
    highest = jnp.max(logits, axis=1, keepdims=True)
    return logits - highest - jnp.log(jnp.sum(jnp.exp(logits - highest), axis=1, keepdims=True))


def shards(embedding, seed_cluster):
    points, width = embedding.shape
    side = jnp.concatenate([seed_cluster.astype(jnp.float32), jnp.sum(embedding * embedding, axis=1)])
    block = jnp.concatenate([embedding, jnp.broadcast_to(side, (SIDE, width))], axis=0)
    rows = row_peers(block)
    rows, columns = lax.optimization_barrier((rows, exchange_columns(copies(block, 8))))
    order = member_order()
    high, low, weighted = pairs(order, rows, columns, other_core(columns))

    first = jnp.sum(exchange_rows(weighted), axis=0)
    firsts = exchange_columns(copies(first, 8))
    others = other_core(firsts)
    weighted = members(order, firsts, others, high, low)
    cohesion, counts = jnp.sum(firsts[:, points : points + 2] + others[:, points : points + 2], axis=0)
    own = jnp.exp(log_softmax_energy(first[:points], counts, cohesion))

    second = jnp.sum(exchange_rows(weighted), axis=0)
    attraction, counts = second[:points], second[points : points + 1]
    parts = lax.all_to_all(copies(jnp.sum(own * attraction, axis=0, keepdims=True), 128), EVERY, 0, 0, tiled=True)
    return log_softmax_energy(attraction, counts, jnp.sum(parts, axis=0))


def solution(mesh):
    finer = Mesh(mesh.devices.reshape(SIZES), EVERY)
    return jax.shard_map(
        shards, mesh=finer, in_specs=(P(EVERY, None), P(EVERY)), out_specs=P(EVERY, None), check_vma=False
    )
```

```python
import itertools

import jax
import jax.numpy as jnp
from jax import lax
from jax.experimental import pallas as pl
from jax.experimental.pallas import tpu as pltpu
from jax.sharding import Mesh
from jax.sharding import PartitionSpec as P

CLUSTER_COUNT = 128
ANNEAL_TEMP_VALUE = 0.02
SIDE = 8

EVERY = ("y_lo", "z", "y_hi", "x", "core")
SIZES = (2, 4, 2, 4, 2)


def place(y_lo, z, y_hi, x, core):
    return (((y_lo * 4 + z) * 2 + y_hi) * 4 + x) * 2 + core


def column_groups():
    groups = []
    for pair, x, core in itertools.product(range(2), range(4), range(2)):
        groups.append([place(lo, z, lo ^ pair, x, core) for lo in range(2) for z in range(4)])
    return groups


COLUMN_GROUPS = column_groups()


def exchange_rows(blocks):
    return lax.all_to_all(blocks, ("y_lo", "x"), 0, 0, tiled=True)


def exchange_columns(blocks):
    return lax.all_to_all(blocks, EVERY, 0, 0, axis_index_groups=COLUMN_GROUPS, tiled=True)


def moved(x, flip, step):
    pairs = []
    for lo, z, hi, at, core in itertools.product(*map(range, SIZES)):
        pairs.append((place(lo ^ flip, z, hi, (at + step) % 4, core), place(lo, z, hi, at, core)))
    return lax.ppermute(x, EVERY, pairs)


def row_peers(x):
    pair = jnp.stack([x, moved(x, 1, 0)])
    return [pair] + [moved(pair, 0, step) for step in range(1, 4)]


def member_order():
    y_lo, x = lax.axis_index("y_lo"), lax.axis_index("x")
    offset = jnp.arange(8, dtype=jnp.int32)
    return (y_lo ^ (offset % 2)) * 4 + (x + offset // 2) % 4


def halves(x):
    high = x.astype(jnp.bfloat16)
    return high, (x - high.astype(jnp.float32)).astype(jnp.bfloat16)


def product(a, b):
    return jnp.dot(a, b, preferred_element_type=jnp.float32)


def seed_member(seeds):
    labels = lax.broadcasted_iota(jnp.int32, (CLUSTER_COUNT, seeds.shape[1]), 0).astype(jnp.float32)
    return 0.5 * (labels == seeds).astype(jnp.float32).T + 0.5 / CLUSTER_COUNT


def tail_rows(*lines):
    at = lax.broadcasted_iota(jnp.int32, (SIDE, CLUSTER_COUNT), 0)
    tail = jnp.zeros((SIDE, CLUSTER_COUNT), jnp.float32)
    for index, line in enumerate(lines):
        tail = jnp.where(at == index, line, tail)
    return tail


def column_kernel(own, other, right, squares, member):
    points, width = own.shape[1] - SIDE, own.shape[2]
    for source, start in ((own, 0), (other, 8)):
        for block in range(8):
            at = pl.ds((start + block) * points, points)
            high, low = halves(source[block, pl.ds(0, points)])
            right[at, pl.ds(0, width)] = high
            right[at, pl.ds(width, width)] = low
            right[at, pl.ds(2 * width, width)] = high
            line = source[block, pl.ds(points, 1)]
            squares[:, at] = jnp.broadcast_to(line[:, points:], (SIDE, points))
            member[at] = seed_member(line[:, :points]).astype(jnp.bfloat16)


def pair_kernel(rows, right, squares, member, high_out, low_out, out):
    blocks, lines, width = rows.shape
    points = lines - SIDE
    x = rows[:, pl.ds(0, points)].reshape(blocks * points, width)
    square = jnp.sum(x * x, axis=1, keepdims=True) + 1.0
    high, low = halves(-2.0 * x)
    left = jnp.concatenate([high, high, low], axis=1)
    inner = lax.dot_general(left, right[...], (((1,), (1,)), ((), ())), preferred_element_type=jnp.float32)
    squared = inner + square + squares[pl.ds(0, 1)]
    high, low = halves(squared * lax.rsqrt(squared))
    high_out[...] = high
    low_out[...] = low
    total = product(high, member[...]) + product(low, member[...])
    cohesion = jnp.zeros((1, CLUSTER_COUNT), jnp.float32)
    counts = []
    for block in range(blocks):
        own = seed_member(rows[block, pl.ds(points, 1)][:, :points])
        part = total[block * points : (block + 1) * points]
        out[block, pl.ds(0, points)] = part
        cohesion += jnp.sum(own * part, axis=0, keepdims=True)
        counts.append(jnp.sum(own, axis=0, keepdims=True))
    out[0, pl.ds(points, SIDE)] = tail_rows(cohesion, counts[0])


def place_kernel(order, first, second, third, fourth, out):
    parts = (first, second, third, fourth)
    points = first.shape[1] - SIDE
    cohesion = sum(part[0, pl.ds(points, 1)] for part in parts)
    tail = tail_rows(cohesion, first[0, pl.ds(points + 1, 1)])
    for offset in range(8):
        member = order[offset]
        out[member, pl.ds(0, points)] = parts[offset // 2][offset % 2, pl.ds(0, points)]
        out[member, pl.ds(points, SIDE)] = tail


def member_kernel(order, own, other, *rest):
    *kept, out, both = rest
    points = own.shape[1] - SIDE
    sums = jnp.zeros((SIDE, CLUSTER_COUNT), jnp.float32)
    for block in range(8):
        sums += own[block, pl.ds(points, SIDE)] + other[block, pl.ds(points, SIDE)]
    cohesion, counts = sums[0:1], sums[1:2]
    sizes = jnp.zeros((1, CLUSTER_COUNT), jnp.float32)
    for source, start in ((own, 0), (other, 8)):
        for block in range(8):
            member = jnp.exp(log_softmax_energy(source[block, pl.ds(0, points)], counts, cohesion))
            sizes += jnp.sum(member, axis=0, keepdims=True)
            at = pl.ds((start + block) * points, points)
            both[at, pl.ds(0, CLUSTER_COUNT)], both[at, pl.ds(CLUSTER_COUNT, CLUSTER_COUNT)] = halves(member)
    tail = tail_rows(sizes)
    for step in range(4):
        wide = product(kept[2 * step][...], both[...])
        total = product(kept[2 * step + 1][...], both[:, pl.ds(0, CLUSTER_COUNT)])
        total += wide[:, :CLUSTER_COUNT] + wide[:, CLUSTER_COUNT:]
        for block in range(2):
            place_at = order[2 * step + block]
            out[place_at, pl.ds(0, points)] = total[block * points : (block + 1) * points]
            out[place_at, pl.ds(points, SIDE)] = tail


def sum_kernel(blocks, out, *spread):
    total = blocks[0]
    for block in range(1, 8):
        total += blocks[block]
    out[...] = total
    for copy in spread:
        copy[...] = jnp.broadcast_to(total, copy.shape)


def on_chip(kernel, name, shapes, inputs, with_order=False, scratch=()):
    vmem = pl.BlockSpec(memory_space=pltpu.VMEM)
    specs = [vmem] * len(inputs)
    if with_order:
        specs[0] = pl.BlockSpec(memory_space=pltpu.SMEM)
    shapes = [jax.ShapeDtypeStruct(*shape) for shape in shapes]
    return pl.pallas_call(
        kernel,
        out_shape=shapes,
        in_specs=specs,
        out_specs=[vmem] * len(shapes),
        scratch_shapes=scratch,
        compiler_params=pltpu.CompilerParams(vmem_limit_bytes=12 << 20),
        name=name,
    )(*inputs)


def copies(x, count):
    return jnp.broadcast_to(x, (count, *x.shape))


def other_core(x):
    return lax.ppermute(x, "core", [(0, 1), (1, 0)])


def log_softmax_energy(attraction, counts, cohesion):
    energy = attraction / counts - cohesion / (2.0 * counts**2)
    logits = -energy / ANNEAL_TEMP_VALUE
    highest = jnp.max(logits, axis=1, keepdims=True)
    return logits - highest - jnp.log(jnp.sum(jnp.exp(logits - highest), axis=1, keepdims=True))


def shards(embedding, seed_cluster):
    points, width = embedding.shape
    side = jnp.concatenate([seed_cluster.astype(jnp.float32), jnp.sum(embedding * embedding, axis=1)])
    block = jnp.concatenate([embedding, jnp.broadcast_to(side, (SIDE, width))], axis=0)
    columns = exchange_columns(copies(block, 8))
    rows = row_peers(block)
    columns, _ = lax.optimization_barrier((columns, rows[1]))
    order = member_order()
    tall = 16 * points
    prepared = on_chip(
        column_kernel,
        "columns",
        [((tall, 3 * width), jnp.bfloat16), ((SIDE, tall), jnp.float32), ((tall, CLUSTER_COUNT), jnp.bfloat16)],
        [columns, other_core(columns)],
    )
    kept, weighted = [], []
    for two in rows:
        piece = ((2 * points, tall), jnp.bfloat16)
        out = ((2, points + SIDE, CLUSTER_COUNT), jnp.float32)
        high, low, part = on_chip(pair_kernel, "pairs", [piece, piece, out], [two, *prepared])
        kept += [high, low]
        weighted.append(part)
    exchange = [((8, points + SIDE, CLUSTER_COUNT), jnp.float32)]
    (weighted,) = on_chip(place_kernel, "place", exchange, [order, *weighted], with_order=True)

    line = ((points + SIDE, CLUSTER_COUNT), jnp.float32)
    first, spread = on_chip(sum_kernel, "sum_spread", [line, *exchange], [exchange_rows(weighted)])
    firsts = exchange_columns(spread)
    others = other_core(firsts)
    (weighted,) = on_chip(
        member_kernel,
        "members",
        exchange,
        [order, firsts, others, *kept],
        with_order=True,
        scratch=[pltpu.VMEM((tall, 2 * CLUSTER_COUNT), jnp.bfloat16)],
    )
    cohesion, counts = jnp.sum(firsts[:, points : points + 2] + others[:, points : points + 2], axis=0)
    own = jnp.exp(log_softmax_energy(first[:points], counts, cohesion))

    (second,) = on_chip(sum_kernel, "sum", [line], [exchange_rows(weighted)])
    attraction, counts = second[:points], second[points : points + 1]
    parts = lax.all_to_all(copies(jnp.sum(own * attraction, axis=0, keepdims=True), 128), EVERY, 0, 0, tiled=True)
    return log_softmax_energy(attraction, counts, jnp.sum(parts, axis=0))


def solution(mesh):
    finer = Mesh(mesh.devices.reshape(SIZES), EVERY)
    return jax.shard_map(
        shards, mesh=finer, in_specs=(P(EVERY, None), P(EVERY)), out_specs=P(EVERY, None), check_vma=False
    )
```

```python
import itertools

import jax
import jax.numpy as jnp
from jax import lax
from jax.experimental import pallas as pl
from jax.experimental.pallas import tpu as pltpu
from jax.sharding import Mesh
from jax.sharding import PartitionSpec as P

CLUSTER_COUNT = 128
ANNEAL_TEMP_VALUE = 0.02
SIDE = 8

EVERY = ("y_lo", "z", "y_hi", "x", "core")
SIZES = (2, 4, 2, 4, 2)


def place(y_lo, z, y_hi, x, core):
    return (((y_lo * 4 + z) * 2 + y_hi) * 4 + x) * 2 + core


def column_groups():
    groups = []
    for pair, x, core in itertools.product(range(2), range(4), range(2)):
        groups.append([place(lo, z, lo ^ pair, x, core) for lo in range(2) for z in range(4)])
    return groups


COLUMN_GROUPS = column_groups()


def exchange_rows(blocks):
    return lax.all_to_all(blocks, ("y_lo", "x"), 0, 0, tiled=True)


def exchange_columns(blocks):
    return lax.all_to_all(blocks, EVERY, 0, 0, axis_index_groups=COLUMN_GROUPS, tiled=True)


def moved(x, flip, step):
    pairs = []
    for lo, z, hi, at, core in itertools.product(*map(range, SIZES)):
        pairs.append((place(lo ^ flip, z, hi, (at + step) % 4, core), place(lo, z, hi, at, core)))
    return lax.ppermute(x, EVERY, pairs)


def row_peers(x):
    return [moved(x, flip, step) if flip or step else x for flip in range(2) for step in (0, 1, 3, 2)]


def member_order():
    y_lo, x = lax.axis_index("y_lo"), lax.axis_index("x")
    offset = jnp.arange(8, dtype=jnp.int32)
    step = offset % 4
    step = jnp.where(step < 2, step, 5 - step)
    return (y_lo ^ (offset // 4)) * 4 + (x + step) % 4


def halves(x):
    high = x.astype(jnp.bfloat16)
    return high, (x - high.astype(jnp.float32)).astype(jnp.bfloat16)


def product(a, b):
    return jnp.dot(a, b, preferred_element_type=jnp.float32)


def seed_member(seeds):
    labels = lax.broadcasted_iota(jnp.int32, (CLUSTER_COUNT, seeds.shape[1]), 0).astype(jnp.float32)
    return 0.5 * (labels == seeds).astype(jnp.float32).T + 0.5 / CLUSTER_COUNT


def tail_rows(*lines):
    at = lax.broadcasted_iota(jnp.int32, (SIDE, CLUSTER_COUNT), 0)
    tail = jnp.zeros((SIDE, CLUSTER_COUNT), jnp.float32)
    for index, line in enumerate(lines):
        tail = jnp.where(at == index, line, tail)
    return tail


def column_kernel(own, other, right, squares, member):
    points, width = own.shape[1] - SIDE, own.shape[2]
    for source, start in ((own, 0), (other, 8)):
        for block in range(8):
            at = pl.ds((start + block) * points, points)
            high, low = halves(source[block, pl.ds(0, points)])
            right[at, pl.ds(0, width)] = high
            right[at, pl.ds(width, width)] = low
            right[at, pl.ds(2 * width, width)] = high
            line = source[block, pl.ds(points, 1)]
            squares[:, at] = jnp.broadcast_to(line[:, points:], (SIDE, points))
            member[at] = seed_member(line[:, :points]).astype(jnp.bfloat16)


def pair_kernel(first, second, right, squares, member, high_out, low_out, out):
    rows = (first, second)
    points, width = first.shape[0] - SIDE, first.shape[1]
    x = jnp.concatenate([block[pl.ds(0, points)] for block in rows], axis=0)
    square = jnp.sum(x * x, axis=1, keepdims=True) + 1.0
    high, low = halves(-2.0 * x)
    left = jnp.concatenate([high, high, low], axis=1)
    inner = lax.dot_general(left, right[...], (((1,), (1,)), ((), ())), preferred_element_type=jnp.float32)
    squared = inner + square + squares[pl.ds(0, 1)]
    high, low = halves(squared * lax.rsqrt(squared))
    high_out[...] = high
    low_out[...] = low
    total = product(high, member[...]) + product(low, member[...])
    cohesion = jnp.zeros((1, CLUSTER_COUNT), jnp.float32)
    counts = []
    for block in range(2):
        own = seed_member(rows[block][pl.ds(points, 1)][:, :points])
        part = total[block * points : (block + 1) * points]
        out[block, pl.ds(0, points)] = part
        cohesion += jnp.sum(own * part, axis=0, keepdims=True)
        counts.append(jnp.sum(own, axis=0, keepdims=True))
    out[0, pl.ds(points, SIDE)] = tail_rows(cohesion, counts[0])


def place_kernel(order, first, second, third, fourth, out):
    parts = (first, second, third, fourth)
    points = first.shape[1] - SIDE
    cohesion = sum(part[0, pl.ds(points, 1)] for part in parts)
    tail = tail_rows(cohesion, first[0, pl.ds(points + 1, 1)])
    for offset in range(8):
        member = order[offset]
        out[member, pl.ds(0, points)] = parts[offset // 2][offset % 2, pl.ds(0, points)]
        out[member, pl.ds(points, SIDE)] = tail


def member_kernel(order, own, other, *rest):
    *kept, out, both = rest
    points = own.shape[1] - SIDE
    sums = jnp.zeros((SIDE, CLUSTER_COUNT), jnp.float32)
    for block in range(8):
        sums += own[block, pl.ds(points, SIDE)] + other[block, pl.ds(points, SIDE)]
    cohesion, counts = sums[0:1], sums[1:2]
    sizes = jnp.zeros((1, CLUSTER_COUNT), jnp.float32)
    for source, start in ((own, 0), (other, 8)):
        for block in range(8):
            member = jnp.exp(log_softmax_energy(source[block, pl.ds(0, points)], counts, cohesion))
            sizes += jnp.sum(member, axis=0, keepdims=True)
            at = pl.ds((start + block) * points, points)
            both[at, pl.ds(0, CLUSTER_COUNT)], both[at, pl.ds(CLUSTER_COUNT, CLUSTER_COUNT)] = halves(member)
    tail = tail_rows(sizes)
    for step in range(4):
        wide = product(kept[2 * step][...], both[...])
        total = product(kept[2 * step + 1][...], both[:, pl.ds(0, CLUSTER_COUNT)])
        total += wide[:, :CLUSTER_COUNT] + wide[:, CLUSTER_COUNT:]
        for block in range(2):
            place_at = order[2 * step + block]
            out[place_at, pl.ds(0, points)] = total[block * points : (block + 1) * points]
            out[place_at, pl.ds(points, SIDE)] = tail


def sum_kernel(blocks, out, *spread):
    total = blocks[0]
    for block in range(1, 8):
        total += blocks[block]
    out[...] = total
    for copy in spread:
        copy[...] = jnp.broadcast_to(total, copy.shape)


def on_chip(kernel, name, shapes, inputs, with_order=False, scratch=()):
    vmem = pl.BlockSpec(memory_space=pltpu.VMEM)
    specs = [vmem] * len(inputs)
    if with_order:
        specs[0] = pl.BlockSpec(memory_space=pltpu.SMEM)
    shapes = [jax.ShapeDtypeStruct(*shape) for shape in shapes]
    return pl.pallas_call(
        kernel,
        out_shape=shapes,
        in_specs=specs,
        out_specs=[vmem] * len(shapes),
        scratch_shapes=scratch,
        compiler_params=pltpu.CompilerParams(vmem_limit_bytes=12 << 20),
        name=name,
    )(*inputs)


def copies(x, count):
    return jnp.broadcast_to(x, (count, *x.shape))


def other_core(x):
    return lax.ppermute(x, "core", [(0, 1), (1, 0)])


def log_softmax_energy(attraction, counts, cohesion):
    energy = attraction / counts - cohesion / (2.0 * counts**2)
    logits = -energy / ANNEAL_TEMP_VALUE
    highest = jnp.max(logits, axis=1, keepdims=True)
    return logits - highest - jnp.log(jnp.sum(jnp.exp(logits - highest), axis=1, keepdims=True))


def shards(embedding, seed_cluster):
    points, width = embedding.shape
    side = jnp.concatenate([seed_cluster.astype(jnp.float32), jnp.sum(embedding * embedding, axis=1)])
    block = jnp.concatenate([embedding, jnp.broadcast_to(side, (SIDE, width))], axis=0)
    columns = exchange_columns(copies(block, 8))
    rows = row_peers(block)
    columns, *_ = lax.optimization_barrier((columns, *rows[1:5]))
    order = member_order()
    tall = 16 * points
    prepared = on_chip(
        column_kernel,
        "columns",
        [((tall, 3 * width), jnp.bfloat16), ((SIDE, tall), jnp.float32), ((tall, CLUSTER_COUNT), jnp.bfloat16)],
        [columns, other_core(columns)],
    )
    kept, weighted = [], []
    for at in range(0, 8, 2):
        piece = ((2 * points, tall), jnp.bfloat16)
        out = ((2, points + SIDE, CLUSTER_COUNT), jnp.float32)
        high, low, part = on_chip(pair_kernel, "pairs", [piece, piece, out], [*rows[at : at + 2], *prepared])
        kept += [high, low]
        weighted.append(part)
    exchange = [((8, points + SIDE, CLUSTER_COUNT), jnp.float32)]
    (weighted,) = on_chip(place_kernel, "place", exchange, [order, *weighted], with_order=True)

    line = ((points + SIDE, CLUSTER_COUNT), jnp.float32)
    first, spread = on_chip(sum_kernel, "sum_spread", [line, *exchange], [exchange_rows(weighted)])
    firsts = exchange_columns(spread)
    others = other_core(firsts)
    (weighted,) = on_chip(
        member_kernel,
        "members",
        exchange,
        [order, firsts, others, *kept],
        with_order=True,
        scratch=[pltpu.VMEM((tall, 2 * CLUSTER_COUNT), jnp.bfloat16)],
    )
    cohesion, counts = jnp.sum(firsts[:, points : points + 2] + others[:, points : points + 2], axis=0)
    own = jnp.exp(log_softmax_energy(first[:points], counts, cohesion))

    (second,) = on_chip(sum_kernel, "sum", [line], [exchange_rows(weighted)])
    attraction, counts = second[:points], second[points : points + 1]
    parts = lax.all_to_all(copies(jnp.sum(own * attraction, axis=0, keepdims=True), 128), EVERY, 0, 0, tiled=True)
    return log_softmax_energy(attraction, counts, jnp.sum(parts, axis=0))


def solution(mesh):
    finer = Mesh(mesh.devices.reshape(SIZES), EVERY)
    return jax.shard_map(
        shards, mesh=finer, in_specs=(P(EVERY, None), P(EVERY)), out_specs=P(EVERY, None), check_vma=False
    )
```

```python
import functools
import itertools

import jax
import jax.numpy as jnp
from jax import lax
from jax.experimental import pallas as pl
from jax.experimental.pallas import tpu as pltpu
from jax.sharding import Mesh
from jax.sharding import PartitionSpec as P

CLUSTER_COUNT = 128
ANNEAL_TEMP_VALUE = 0.02
SIDE = 8

EVERY = ("y_lo", "z", "y_hi", "x", "core")
SIZES = (2, 4, 2, 4, 2)


def place(y_lo, z, y_hi, x, core):
    return (((y_lo * 4 + z) * 2 + y_hi) * 4 + x) * 2 + core


def column_groups():
    groups = []
    for pair, x, core in itertools.product(range(2), range(4), range(2)):
        groups.append([place(lo, z, lo ^ pair, x, core) for lo in range(2) for z in range(4)])
    return groups


COLUMN_GROUPS = column_groups()


def exchange_rows(blocks):
    return lax.all_to_all(blocks, ("y_lo", "x"), 0, 0, tiled=True)


def exchange_columns(blocks):
    return lax.all_to_all(blocks, EVERY, 0, 0, axis_index_groups=COLUMN_GROUPS, tiled=True)


def moved(x, flip, step):
    pairs = []
    for lo, z, hi, at, core in itertools.product(*map(range, SIZES)):
        pairs.append((place(lo ^ flip, z, hi, (at + step) % 4, core), place(lo, z, hi, at, core)))
    return lax.ppermute(x, EVERY, pairs)


def row_peers(x):
    return [moved(x, flip, step) if flip or step else x for flip in range(2) for step in (0, 1, 3, 2)]


def member_order():
    y_lo, x = lax.axis_index("y_lo"), lax.axis_index("x")
    offset = jnp.arange(8, dtype=jnp.int32)
    step = offset % 4
    step = jnp.where(step < 2, step, 5 - step)
    return (y_lo ^ (offset // 4)) * 4 + (x + step) % 4


def halves(x):
    high = x.astype(jnp.bfloat16)
    return high, (x - high.astype(jnp.float32)).astype(jnp.bfloat16)


def product(a, b):
    return jnp.dot(a, b, preferred_element_type=jnp.float32)


def seed_member(seeds):
    labels = lax.broadcasted_iota(jnp.int32, (CLUSTER_COUNT, seeds.shape[1]), 0).astype(jnp.float32)
    return 0.5 * (labels == seeds).astype(jnp.float32).T + 0.5 / CLUSTER_COUNT


def tail_rows(*lines):
    at = lax.broadcasted_iota(jnp.int32, (SIDE, CLUSTER_COUNT), 0)
    tail = jnp.zeros((SIDE, CLUSTER_COUNT), jnp.float32)
    for index, line in enumerate(lines):
        tail = jnp.where(at == index, line, tail)
    return tail


def column_kernel(own, other, right, squares, member):
    points, width = own.shape[1] - SIDE, own.shape[2]
    for source, start in ((own, 0), (other, 8)):
        for block in range(8):
            at = pl.ds((start + block) * points, points)
            high, low = halves(source[block, pl.ds(0, points)])
            right[at, pl.ds(0, width)] = high
            right[at, pl.ds(width, width)] = low
            right[at, pl.ds(2 * width, width)] = high
            line = source[block, pl.ds(points, 1)]
            squares[:, at] = jnp.broadcast_to(line[:, points:], (SIDE, points))
            member[at] = seed_member(line[:, :points]).astype(jnp.bfloat16)


def prepare_kernel(embedding, seeds, block, spread):
    points, width = embedding.shape
    x = embedding[...]
    side = jnp.concatenate([seeds[...].astype(jnp.float32), jnp.sum((x * x).T, axis=0, keepdims=True)], axis=1)
    side = jnp.broadcast_to(side, (SIDE, width))
    block[pl.ds(0, points)] = x
    block[pl.ds(points, SIDE)] = side
    for copy in range(spread.shape[0]):
        spread[copy, pl.ds(0, points)] = x
        spread[copy, pl.ds(points, SIDE)] = side


def pair_kernel(piece, order, first, second, right, squares, member, *rest):
    *_, high_out, low_out, out = rest
    points, width = first.shape[0] - SIDE, first.shape[1]
    at = pl.ds(piece * 2 * points, 2 * points)
    x = jnp.concatenate([first[pl.ds(0, points)], second[pl.ds(0, points)]], axis=0)
    square = jnp.sum(x * x, axis=1, keepdims=True) + 1.0
    high, low = halves(-2.0 * x)
    left = jnp.concatenate([high, high, low], axis=1)
    inner = lax.dot_general(left, right[...], (((1,), (1,)), ((), ())), preferred_element_type=jnp.float32)
    squared = inner + square + squares[pl.ds(0, 1)]
    high, low = halves(squared * lax.rsqrt(squared))
    high_out[at] = high
    low_out[at] = low
    total = product(high, member[...]) + product(low, member[...])
    if piece:
        tail = rest[2][order[0], pl.ds(points, SIDE)]
        cohesion, counts = tail[0:1], tail[1:2]
    else:
        cohesion = jnp.zeros((1, CLUSTER_COUNT), jnp.float32)
        counts = jnp.sum(seed_member(first[pl.ds(points, 1)][:, :points]), axis=0, keepdims=True)
    for index, block in enumerate((first, second)):
        own = seed_member(block[pl.ds(points, 1)][:, :points])
        part = total[index * points : (index + 1) * points]
        out[order[2 * piece + index], pl.ds(0, points)] = part
        cohesion += jnp.sum(own * part, axis=0, keepdims=True)
    tail = tail_rows(cohesion, counts)
    for target in range(8 if piece == 3 else 1):
        out[order[target], pl.ds(points, SIDE)] = tail


def member_kernel(order, own, other, high, low, first, out, own_member, both):
    points = own.shape[1] - SIDE
    sums = jnp.zeros((SIDE, CLUSTER_COUNT), jnp.float32)
    for block in range(8):
        sums += own[block, pl.ds(points, SIDE)] + other[block, pl.ds(points, SIDE)]
    cohesion, counts = sums[0:1], sums[1:2]
    own_member[...] = jnp.exp(log_softmax_energy(first[pl.ds(0, points)], counts, cohesion))
    sizes = jnp.zeros((1, CLUSTER_COUNT), jnp.float32)
    for source, start in ((own, 0), (other, 8)):
        for block in range(8):
            member = jnp.exp(log_softmax_energy(source[block, pl.ds(0, points)], counts, cohesion))
            sizes += jnp.sum(member, axis=0, keepdims=True)
            at = pl.ds((start + block) * points, points)
            both[at, pl.ds(0, CLUSTER_COUNT)], both[at, pl.ds(CLUSTER_COUNT, CLUSTER_COUNT)] = halves(member)
    tail = tail_rows(sizes)
    wide = product(high[...], both[...])
    total = product(low[...], both[:, pl.ds(0, CLUSTER_COUNT)])
    total += wide[:, :CLUSTER_COUNT] + wide[:, CLUSTER_COUNT:]
    for block in range(8):
        out[order[block], pl.ds(0, points)] = total[block * points : (block + 1) * points]
        out[order[block], pl.ds(points, SIDE)] = tail


def summed(blocks):
    total = blocks[0]
    for block in range(1, 8):
        total += blocks[block]
    return total


def sum_kernel(blocks, out, spread):
    out[...] = summed(blocks)
    spread[...] = jnp.broadcast_to(out[...], spread.shape)


def own_kernel(blocks, own, out, part):
    points = own.shape[0]
    out[...] = summed(blocks)
    part[...] = jnp.sum(own[...] * out[pl.ds(0, points)], axis=0, keepdims=True)


def final_kernel(second, cohesion, out):
    points = out.shape[0]
    out[...] = log_softmax_energy(second[pl.ds(0, points)], second[pl.ds(points, 1)], cohesion[...])


def on_chip(kernel, name, shapes, inputs, order_at=None, scratch=(), aliases={}):
    vmem = pl.BlockSpec(memory_space=pltpu.VMEM)
    specs = [vmem] * len(inputs)
    if order_at is not None:
        specs[order_at] = pl.BlockSpec(memory_space=pltpu.SMEM)
    shapes = [jax.ShapeDtypeStruct(*shape) for shape in shapes]
    return pl.pallas_call(
        kernel,
        out_shape=shapes,
        in_specs=specs,
        out_specs=[vmem] * len(shapes),
        scratch_shapes=scratch,
        input_output_aliases=aliases,
        compiler_params=pltpu.CompilerParams(vmem_limit_bytes=12 << 20),
        name=name,
    )(*inputs)


def copies(x, count):
    return jnp.broadcast_to(x, (count, *x.shape))


def other_core(x):
    return lax.ppermute(x, "core", [(0, 1), (1, 0)])


def log_softmax_energy(attraction, counts, cohesion):
    energy = attraction / counts - cohesion / (2.0 * counts**2)
    logits = -energy / ANNEAL_TEMP_VALUE
    highest = jnp.max(logits, axis=1, keepdims=True)
    return logits - highest - jnp.log(jnp.sum(jnp.exp(logits - highest), axis=1, keepdims=True))


def shards(embedding, seed_cluster):
    points, width = embedding.shape
    lines, tall = points + SIDE, 16 * points
    block, spread = on_chip(
        prepare_kernel,
        "prepare",
        [((lines, width), jnp.float32), ((8, lines, width), jnp.float32)],
        [embedding, seed_cluster.reshape(1, points)],
    )
    columns = exchange_columns(spread)
    rows = row_peers(block)
    columns, *_ = lax.optimization_barrier((columns, *rows[1:7]))
    order = member_order()
    prepared = on_chip(
        column_kernel,
        "columns",
        [((tall, 3 * width), jnp.bfloat16), ((SIDE, tall), jnp.float32), ((tall, CLUSTER_COUNT), jnp.bfloat16)],
        [columns, other_core(columns)],
    )
    kept = ((8 * points, tall), jnp.bfloat16)
    exchange = ((8, lines, CLUSTER_COUNT), jnp.float32)
    state = []
    for piece in range(4):
        state = on_chip(
            functools.partial(pair_kernel, piece),
            f"pairs_{piece}",
            [kept, kept, exchange],
            [order, *rows[2 * piece : 2 * piece + 2], *prepared, *state],
            order_at=0,
            aliases={6: 0, 7: 1, 8: 2} if state else {},
        )
    high, low, weighted = state

    line = ((lines, CLUSTER_COUNT), jnp.float32)
    first, spread = on_chip(sum_kernel, "sum_spread", [line, exchange], [exchange_rows(weighted)])
    firsts = exchange_columns(spread)
    weighted, own = on_chip(
        member_kernel,
        "members",
        [exchange, ((points, CLUSTER_COUNT), jnp.float32)],
        [order, firsts, other_core(firsts), high, low, first],
        order_at=0,
        scratch=[pltpu.VMEM((tall, 2 * CLUSTER_COUNT), jnp.bfloat16)],
    )

    part = ((1, CLUSTER_COUNT), jnp.float32)
    second, part = on_chip(own_kernel, "own_sums", [line, part], [exchange_rows(weighted), own])
    parts = lax.all_to_all(copies(part, 128), EVERY, 0, 0, tiled=True)
    (out,) = on_chip(
        final_kernel,
        "final",
        [((points, CLUSTER_COUNT), jnp.float32)],
        [second, jnp.sum(parts, axis=0)],
    )
    return out


def solution(mesh):
    finer = Mesh(mesh.devices.reshape(SIZES), EVERY)
    return jax.shard_map(
        shards, mesh=finer, in_specs=(P(EVERY, None), P(EVERY)), out_specs=P(EVERY, None), check_vma=False
    )
```

```python
import functools
import itertools

import jax
import jax.numpy as jnp
from jax import lax
from jax.experimental import pallas as pl
from jax.experimental.pallas import tpu as pltpu
from jax.sharding import Mesh
from jax.sharding import PartitionSpec as P

CLUSTER_COUNT = 128
ANNEAL_TEMP_VALUE = 0.02
SIDE = 8

EVERY = ("y_lo", "z", "y_hi", "x", "core")
SIZES = (2, 4, 2, 4, 2)


def place(y_lo, z, y_hi, x, core):
    return (((y_lo * 4 + z) * 2 + y_hi) * 4 + x) * 2 + core


NEAR = ((0, 1), (2, 3))
FAR = ((0, 3), (1, 2))


def cubes(pairs):
    groups = []
    for along_y, along_z, along_x, core in itertools.product(pairs, pairs, pairs, range(2)):
        groups.append([place(y % 2, z, y // 2, x, core) for y in along_y for z in along_z for x in along_x])
    return groups


ROW_GROUPS, COLUMN_GROUPS = cubes(NEAR), cubes(FAR)
ROW_ORDER = (0, 1, 2, 4, 3, 5, 6, 7)


def exchange_rows(blocks):
    return lax.all_to_all(blocks, EVERY, 0, 0, axis_index_groups=ROW_GROUPS, tiled=True)


def exchange_columns(blocks):
    return lax.all_to_all(blocks, EVERY, 0, 0, axis_index_groups=COLUMN_GROUPS, tiled=True)


def moved(x, flips):
    along_y, along_z, along_x = flips // 4, flips // 2 % 2, flips % 2
    pairs = []
    for lo, z, hi, at, core in itertools.product(*map(range, SIZES)):
        pairs.append((place(lo ^ along_y, z ^ along_z, hi, at ^ along_x, core), place(lo, z, hi, at, core)))
    return lax.ppermute(x, EVERY, pairs)


def row_peers(x):
    return [moved(x, flips) if flips else x for flips in ROW_ORDER]


def member_at(offset):
    member = 0
    for name, bit in (("y_lo", 4), ("z", 2), ("x", 1)):
        own = lax.axis_index(name) % 2
        member += bit * ((1 - own) if ROW_ORDER[offset] & bit else own)
    return member


def halves(x):
    high = x.astype(jnp.bfloat16)
    return high, (x - high.astype(jnp.float32)).astype(jnp.bfloat16)


def product(a, b):
    return jnp.dot(a, b, preferred_element_type=jnp.float32)


def seed_member(seeds):
    labels = lax.broadcasted_iota(jnp.int32, (CLUSTER_COUNT, seeds.shape[1]), 0).astype(jnp.float32)
    return 0.5 * (labels == seeds).astype(jnp.float32).T + 0.5 / CLUSTER_COUNT


def tail_rows(*lines):
    at = lax.broadcasted_iota(jnp.int32, (SIDE, CLUSTER_COUNT), 0)
    tail = jnp.zeros((SIDE, CLUSTER_COUNT), jnp.float32)
    for index, line in enumerate(lines):
        tail = jnp.where(at == index, line, tail)
    return tail


def column_kernel(own, other, right, squares, member):
    points, width = own.shape[1] - SIDE, own.shape[2]
    for source, start in ((own, 0), (other, 8)):
        for block in range(8):
            at = pl.ds((start + block) * points, points)
            high, low = halves(source[block, pl.ds(0, points)])
            right[at, pl.ds(0, width)] = high
            right[at, pl.ds(width, width)] = low
            right[at, pl.ds(2 * width, width)] = high
            line = source[block, pl.ds(points, 1)]
            squares[:, at] = jnp.broadcast_to(line[:, points:], (SIDE, points))
            member[at] = seed_member(line[:, :points]).astype(jnp.bfloat16)


def prepare_kernel(embedding, seeds, block, spread, labels, arrived, sent, tails):
    points, width = embedding.shape
    body, end = pl.ds(0, points), pl.ds(points, SIDE)
    loads = [
        pltpu.make_async_copy(embedding, block.at[body], arrived.at[0]),
        pltpu.make_async_copy(seeds, labels, arrived.at[1]),
    ]
    bodies = [pltpu.make_async_copy(embedding, spread.at[copy, body], sent.at[copy]) for copy in range(8)]
    for load in loads:
        load.start()
    for copy in bodies:
        copy.start()
    for load in loads:
        load.wait()
    x = block[body]
    side = jnp.concatenate([labels[...].astype(jnp.float32), jnp.sum((x * x).T, axis=0, keepdims=True)], axis=1)
    block[end] = jnp.broadcast_to(side, (SIDE, width))
    ends = [pltpu.make_async_copy(block.at[end], spread.at[copy, end], tails.at[copy]) for copy in range(8)]
    for copy in ends:
        copy.start()
    for copy in bodies + ends:
        copy.wait()


def pair_kernel(piece, first, second, right, squares, member, *rest):
    *_, high_out, low_out, out = rest
    points, width = first.shape[0] - SIDE, first.shape[1]
    at = pl.ds(piece * 2 * points, 2 * points)
    x = jnp.concatenate([first[pl.ds(0, points)], second[pl.ds(0, points)]], axis=0)
    square = jnp.sum(x * x, axis=1, keepdims=True) + 1.0
    high, low = halves(-2.0 * x)
    left = jnp.concatenate([high, high, low], axis=1)
    inner = lax.dot_general(left, right[...], (((1,), (1,)), ((), ())), preferred_element_type=jnp.float32)
    squared = inner + square + squares[pl.ds(0, 1)]
    high, low = halves(squared * lax.rsqrt(squared))
    high_out[at] = high
    low_out[at] = low
    total = product(high, member[...]) + product(low, member[...])
    if piece:
        tail = rest[2][member_at(0), pl.ds(points, SIDE)]
        cohesion, counts = tail[0:1], tail[1:2]
    else:
        cohesion = jnp.zeros((1, CLUSTER_COUNT), jnp.float32)
        counts = jnp.sum(seed_member(first[pl.ds(points, 1)][:, :points]), axis=0, keepdims=True)
    for index, block in enumerate((first, second)):
        own = seed_member(block[pl.ds(points, 1)][:, :points])
        part = total[index * points : (index + 1) * points]
        out[member_at(2 * piece + index), pl.ds(0, points)] = part
        cohesion += jnp.sum(own * part, axis=0, keepdims=True)
    tail = tail_rows(cohesion, counts)
    for target in range(8 if piece == 3 else 1):
        out[member_at(target), pl.ds(points, SIDE)] = tail


def member_kernel(own, other, high, low, first, out, own_member, both):
    points = own.shape[1] - SIDE
    sums = jnp.zeros((SIDE, CLUSTER_COUNT), jnp.float32)
    for block in range(8):
        sums += own[block, pl.ds(points, SIDE)] + other[block, pl.ds(points, SIDE)]
    cohesion, counts = sums[0:1], sums[1:2]
    own_member[...] = jnp.exp(log_softmax_energy(first[pl.ds(0, points)], counts, cohesion))
    sizes = jnp.zeros((1, CLUSTER_COUNT), jnp.float32)
    for source, start in ((own, 0), (other, 8)):
        for block in range(8):
            member = jnp.exp(log_softmax_energy(source[block, pl.ds(0, points)], counts, cohesion))
            sizes += jnp.sum(member, axis=0, keepdims=True)
            at = pl.ds((start + block) * points, points)
            both[at, pl.ds(0, CLUSTER_COUNT)], both[at, pl.ds(CLUSTER_COUNT, CLUSTER_COUNT)] = halves(member)
    tail = tail_rows(sizes)
    wide = product(high[...], both[...])
    total = product(low[...], both[:, pl.ds(0, CLUSTER_COUNT)])
    total += wide[:, :CLUSTER_COUNT] + wide[:, CLUSTER_COUNT:]
    for block in range(8):
        out[member_at(block), pl.ds(0, points)] = total[block * points : (block + 1) * points]
        out[member_at(block), pl.ds(points, SIDE)] = tail


def summed(blocks):
    total = blocks[0]
    for block in range(1, 8):
        total += blocks[block]
    return total


def sum_kernel(blocks, out, spread):
    out[...] = summed(blocks)
    spread[...] = jnp.broadcast_to(out[...], spread.shape)


def own_kernel(blocks, own, out, part):
    points = own.shape[0]
    out[...] = summed(blocks)
    part[...] = jnp.sum(own[...] * out[pl.ds(0, points)], axis=0, keepdims=True)


def final_kernel(second, cohesion, out):
    points = out.shape[0]
    out[...] = log_softmax_energy(second[pl.ds(0, points)], second[pl.ds(points, 1)], cohesion[...])


def on_chip(kernel, name, shapes, inputs, scratch=(), aliases={}):
    vmem = pl.BlockSpec(memory_space=pltpu.VMEM)
    specs = [vmem] * len(inputs)
    shapes = [jax.ShapeDtypeStruct(*shape) for shape in shapes]
    return pl.pallas_call(
        kernel,
        out_shape=shapes,
        in_specs=specs,
        out_specs=[vmem] * len(shapes),
        scratch_shapes=scratch,
        input_output_aliases=aliases,
        compiler_params=pltpu.CompilerParams(vmem_limit_bytes=12 << 20),
        name=name,
    )(*inputs)


def copies(x, count):
    return jnp.broadcast_to(x, (count, *x.shape))


def other_core(x):
    return lax.ppermute(x, "core", [(0, 1), (1, 0)])


def log_softmax_energy(attraction, counts, cohesion):
    energy = attraction / counts - cohesion / (2.0 * counts**2)
    logits = -energy / ANNEAL_TEMP_VALUE
    highest = jnp.max(logits, axis=1, keepdims=True)
    return logits - highest - jnp.log(jnp.sum(jnp.exp(logits - highest), axis=1, keepdims=True))


def shards(embedding, seed_cluster):
    points, width = embedding.shape
    lines, tall = points + SIDE, 16 * points
    anywhere = pl.BlockSpec(memory_space=pl.ANY)
    block, spread = pl.pallas_call(
        prepare_kernel,
        out_shape=[jax.ShapeDtypeStruct((lines, width), jnp.float32), jax.ShapeDtypeStruct((8, lines, width), jnp.float32)],
        in_specs=[anywhere, anywhere],
        out_specs=[pl.BlockSpec(memory_space=pltpu.VMEM), anywhere],
        scratch_shapes=[
            pltpu.VMEM((1, points), jnp.int32),
            pltpu.SemaphoreType.DMA((2,)),
            pltpu.SemaphoreType.DMA((8,)),
            pltpu.SemaphoreType.DMA((8,)),
        ],
        name="prepare",
    )(embedding, seed_cluster.reshape(1, points))
    columns = exchange_columns(spread)
    rows = row_peers(block)
    columns, *_ = lax.optimization_barrier((columns, *rows[1:7]))
    prepared = on_chip(
        column_kernel,
        "columns",
        [((tall, 3 * width), jnp.bfloat16), ((SIDE, tall), jnp.float32), ((tall, CLUSTER_COUNT), jnp.bfloat16)],
        [columns, other_core(columns)],
    )
    kept = ((8 * points, tall), jnp.bfloat16)
    exchange = ((8, lines, CLUSTER_COUNT), jnp.float32)
    state = []
    for piece in range(4):
        state = on_chip(
            functools.partial(pair_kernel, piece),
            f"pairs_{piece}",
            [kept, kept, exchange],
            [*rows[2 * piece : 2 * piece + 2], *prepared, *state],
            aliases={5: 0, 6: 1, 7: 2} if state else {},
        )
    high, low, weighted = state

    line = ((lines, CLUSTER_COUNT), jnp.float32)
    first, spread = on_chip(sum_kernel, "sum_spread", [line, exchange], [exchange_rows(weighted)])
    firsts = exchange_columns(spread)
    weighted, own = on_chip(
        member_kernel,
        "members",
        [exchange, ((points, CLUSTER_COUNT), jnp.float32)],
        [firsts, other_core(firsts), high, low, first],
        scratch=[pltpu.VMEM((tall, 2 * CLUSTER_COUNT), jnp.bfloat16)],
    )

    part = ((1, CLUSTER_COUNT), jnp.float32)
    second, part = on_chip(own_kernel, "own_sums", [line, part], [exchange_rows(weighted), own])
    parts = lax.all_to_all(copies(part, 128), EVERY, 0, 0, tiled=True)
    (out,) = on_chip(
        final_kernel,
        "final",
        [((points, CLUSTER_COUNT), jnp.float32)],
        [second, jnp.sum(parts, axis=0)],
    )
    return out


def solution(mesh):
    finer = Mesh(mesh.devices.reshape(SIZES), EVERY)
    return jax.shard_map(
        shards, mesh=finer, in_specs=(P(EVERY, None), P(EVERY)), out_specs=P(EVERY, None), check_vma=False
    )
```

```python
import functools
import itertools

import jax
import jax.numpy as jnp
from jax import lax
from jax.experimental import pallas as pl
from jax.experimental.pallas import tpu as pltpu
from jax.sharding import Mesh
from jax.sharding import PartitionSpec as P

CLUSTER_COUNT = 128
ANNEAL_TEMP_VALUE = 0.02
SIDE = 8

EVERY = ("y_lo", "z", "y_hi", "x", "core")
SIZES = (2, 4, 2, 4, 2)


def place(y_lo, z, y_hi, x, core):
    return (((y_lo * 4 + z) * 2 + y_hi) * 4 + x) * 2 + core


NEAR = ((0, 1), (2, 3))
FAR = ((0, 3), (1, 2))


def cubes(pairs):
    groups = []
    for along_y, along_z, along_x, core in itertools.product(pairs, pairs, pairs, range(2)):
        groups.append([place(y % 2, z, y // 2, x, core) for y in along_y for z in along_z for x in along_x])
    return groups


ROW_GROUPS, COLUMN_GROUPS = cubes(NEAR), cubes(FAR)
ROW_ORDER = (0, 1, 2, 4, 3, 5, 6, 7)


def exchange_rows(blocks):
    return lax.all_to_all(blocks, EVERY, 0, 0, axis_index_groups=ROW_GROUPS, tiled=True)


def exchange_columns(blocks):
    return lax.all_to_all(blocks, EVERY, 0, 0, axis_index_groups=COLUMN_GROUPS, tiled=True)


def moved(x, flips):
    along_y, along_z, along_x = flips // 4, flips // 2 % 2, flips % 2
    pairs = []
    for lo, z, hi, at, core in itertools.product(*map(range, SIZES)):
        pairs.append((place(lo ^ along_y, z ^ along_z, hi, at ^ along_x, core), place(lo, z, hi, at, core)))
    return lax.ppermute(x, EVERY, pairs)


def row_peers(x):
    return [moved(x, flips) if flips else x for flips in ROW_ORDER]


def member_at(offset):
    member = 0
    for name, bit in (("y_lo", 4), ("z", 2), ("x", 1)):
        own = lax.axis_index(name) % 2
        member += bit * ((1 - own) if ROW_ORDER[offset] & bit else own)
    return member


def halves(x):
    high = x.astype(jnp.bfloat16)
    return high, (x - high.astype(jnp.float32)).astype(jnp.bfloat16)


def product(a, b):
    return jnp.dot(a, b, preferred_element_type=jnp.float32)


def seed_member(seeds):
    labels = lax.broadcasted_iota(jnp.int32, (CLUSTER_COUNT, seeds.shape[1]), 0).astype(jnp.float32)
    return 0.5 * (labels == seeds).astype(jnp.float32).T + 0.5 / CLUSTER_COUNT


def tail_rows(*lines):
    at = lax.broadcasted_iota(jnp.int32, (SIDE, CLUSTER_COUNT), 0)
    tail = jnp.zeros((SIDE, CLUSTER_COUNT), jnp.float32)
    for index, line in enumerate(lines):
        tail = jnp.where(at == index, line, tail)
    return tail


def column_kernel(own, other, right, squares, member):
    points, width = own.shape[1] - SIDE, own.shape[2]
    for source, start in ((own, 0), (other, 8)):
        for block in range(8):
            at = pl.ds((start + block) * points, points)
            high, low = halves(source[block, pl.ds(0, points)])
            right[at, pl.ds(0, width)] = high
            right[at, pl.ds(width, width)] = low
            right[at, pl.ds(2 * width, width)] = high
            line = source[block, pl.ds(points, 1)]
            squares[:, at] = jnp.broadcast_to(line[:, points:], (SIDE, points))
            member[at] = seed_member(line[:, :points]).astype(jnp.bfloat16)


def prepare_kernel(embedding, seeds, block, spread, labels, arrived, sent):
    points, width = embedding.shape
    body, end = pl.ds(0, points), pl.ds(points, SIDE)
    loads = [
        pltpu.make_async_copy(embedding, block.at[body], arrived.at[0]),
        pltpu.make_async_copy(seeds, labels, arrived.at[1]),
    ]
    for load in loads:
        load.start()
    for load in loads:
        load.wait()
    x = block[body]
    side = jnp.concatenate([labels[...].astype(jnp.float32), jnp.sum((x * x).T, axis=0, keepdims=True)], axis=1)
    block[end] = jnp.broadcast_to(side, (SIDE, width))
    sends = [pltpu.make_async_copy(block, spread.at[copy], sent.at[copy]) for copy in range(8)]
    for copy in sends:
        copy.start()
    for copy in sends:
        copy.wait()


def pair_kernel(piece, first, second, right, squares, member, *rest):
    *_, high_out, low_out, out = rest
    points, width = first.shape[0] - SIDE, first.shape[1]
    at = pl.ds(piece * 2 * points, 2 * points)
    x = jnp.concatenate([first[pl.ds(0, points)], second[pl.ds(0, points)]], axis=0)
    square = jnp.sum(x * x, axis=1, keepdims=True) + 1.0
    high, low = halves(-2.0 * x)
    left = jnp.concatenate([high, high, low], axis=1)
    inner = lax.dot_general(left, right[...], (((1,), (1,)), ((), ())), preferred_element_type=jnp.float32)
    squared = inner + square + squares[pl.ds(0, 1)]
    high, low = halves(squared * lax.rsqrt(squared))
    high_out[at] = high
    low_out[at] = low
    total = product(high, member[...]) + product(low, member[...])
    if piece:
        tail = rest[2][member_at(0), pl.ds(points, SIDE)]
        cohesion, counts = tail[0:1], tail[1:2]
    else:
        cohesion = jnp.zeros((1, CLUSTER_COUNT), jnp.float32)
        counts = jnp.sum(seed_member(first[pl.ds(points, 1)][:, :points]), axis=0, keepdims=True)
    for index, block in enumerate((first, second)):
        own = seed_member(block[pl.ds(points, 1)][:, :points])
        part = total[index * points : (index + 1) * points]
        out[member_at(2 * piece + index), pl.ds(0, points)] = part
        cohesion += jnp.sum(own * part, axis=0, keepdims=True)
    tail = tail_rows(cohesion, counts)
    for target in range(8 if piece == 3 else 1):
        out[member_at(target), pl.ds(points, SIDE)] = tail


def member_kernel(own, other, high, low, first, out, own_member, both):
    points = own.shape[1] - SIDE
    sums = jnp.zeros((SIDE, CLUSTER_COUNT), jnp.float32)
    for block in range(8):
        sums += own[block, pl.ds(points, SIDE)] + other[block, pl.ds(points, SIDE)]
    cohesion, counts = sums[0:1], sums[1:2]
    own_member[...] = jnp.exp(log_softmax_energy(first[pl.ds(0, points)], counts, cohesion))
    sizes = jnp.zeros((1, CLUSTER_COUNT), jnp.float32)
    for source, start in ((own, 0), (other, 8)):
        for block in range(8):
            member = jnp.exp(log_softmax_energy(source[block, pl.ds(0, points)], counts, cohesion))
            sizes += jnp.sum(member, axis=0, keepdims=True)
            at = pl.ds((start + block) * points, points)
            both[at, pl.ds(0, CLUSTER_COUNT)], both[at, pl.ds(CLUSTER_COUNT, CLUSTER_COUNT)] = halves(member)
    tail = tail_rows(sizes)
    wide = product(high[...], both[...])
    total = product(low[...], both[:, pl.ds(0, CLUSTER_COUNT)])
    total += wide[:, :CLUSTER_COUNT] + wide[:, CLUSTER_COUNT:]
    for block in range(8):
        out[member_at(block), pl.ds(0, points)] = total[block * points : (block + 1) * points]
        out[member_at(block), pl.ds(points, SIDE)] = tail


def summed(blocks):
    total = blocks[0]
    for block in range(1, 8):
        total += blocks[block]
    return total


def sum_kernel(blocks, out, spread):
    out[...] = summed(blocks)
    spread[...] = jnp.broadcast_to(out[...], spread.shape)


def own_kernel(blocks, own, out, part):
    points = own.shape[0]
    out[...] = summed(blocks)
    part[...] = jnp.sum(own[...] * out[pl.ds(0, points)], axis=0, keepdims=True)


def final_kernel(second, cohesion, out):
    points = out.shape[0]
    out[...] = log_softmax_energy(second[pl.ds(0, points)], second[pl.ds(points, 1)], cohesion[...])


def on_chip(kernel, name, shapes, inputs, scratch=(), aliases={}):
    vmem = pl.BlockSpec(memory_space=pltpu.VMEM)
    specs = [vmem] * len(inputs)
    shapes = [jax.ShapeDtypeStruct(*shape) for shape in shapes]
    return pl.pallas_call(
        kernel,
        out_shape=shapes,
        in_specs=specs,
        out_specs=[vmem] * len(shapes),
        scratch_shapes=scratch,
        input_output_aliases=aliases,
        compiler_params=pltpu.CompilerParams(vmem_limit_bytes=12 << 20),
        name=name,
    )(*inputs)


def copies(x, count):
    return jnp.broadcast_to(x, (count, *x.shape))


def other_core(x):
    return lax.ppermute(x, "core", [(0, 1), (1, 0)])


def log_softmax_energy(attraction, counts, cohesion):
    energy = attraction / counts - cohesion / (2.0 * counts**2)
    logits = -energy / ANNEAL_TEMP_VALUE
    highest = jnp.max(logits, axis=1, keepdims=True)
    return logits - highest - jnp.log(jnp.sum(jnp.exp(logits - highest), axis=1, keepdims=True))


def shards(embedding, seed_cluster):
    points, width = embedding.shape
    lines, tall = points + SIDE, 16 * points
    anywhere = pl.BlockSpec(memory_space=pl.ANY)
    block, spread = pl.pallas_call(
        prepare_kernel,
        out_shape=[jax.ShapeDtypeStruct((lines, width), jnp.float32), jax.ShapeDtypeStruct((8, lines, width), jnp.float32)],
        in_specs=[anywhere, anywhere],
        out_specs=[pl.BlockSpec(memory_space=pltpu.VMEM), anywhere],
        scratch_shapes=[
            pltpu.VMEM((1, points), jnp.int32),
            pltpu.SemaphoreType.DMA((2,)),
            pltpu.SemaphoreType.DMA((8,)),
        ],
        name="prepare",
    )(embedding, seed_cluster.reshape(1, points))
    columns = exchange_columns(spread)
    rows = row_peers(block)
    columns, *_ = lax.optimization_barrier((columns, *rows[1:7]))
    prepared = on_chip(
        column_kernel,
        "columns",
        [((tall, 3 * width), jnp.bfloat16), ((SIDE, tall), jnp.float32), ((tall, CLUSTER_COUNT), jnp.bfloat16)],
        [columns, other_core(columns)],
    )
    kept = ((8 * points, tall), jnp.bfloat16)
    exchange = ((8, lines, CLUSTER_COUNT), jnp.float32)
    state = []
    for piece in range(4):
        state = on_chip(
            functools.partial(pair_kernel, piece),
            f"pairs_{piece}",
            [kept, kept, exchange],
            [*rows[2 * piece : 2 * piece + 2], *prepared, *state],
            aliases={5: 0, 6: 1, 7: 2} if state else {},
        )
    high, low, weighted = state

    line = ((lines, CLUSTER_COUNT), jnp.float32)
    first, spread = on_chip(sum_kernel, "sum_spread", [line, exchange], [exchange_rows(weighted)])
    firsts = exchange_columns(spread)
    weighted, own = on_chip(
        member_kernel,
        "members",
        [exchange, ((points, CLUSTER_COUNT), jnp.float32)],
        [firsts, other_core(firsts), high, low, first],
        scratch=[pltpu.VMEM((tall, 2 * CLUSTER_COUNT), jnp.bfloat16)],
    )

    part = ((1, CLUSTER_COUNT), jnp.float32)
    second, part = on_chip(own_kernel, "own_sums", [line, part], [exchange_rows(weighted), own])
    parts = lax.all_to_all(copies(part, 128), EVERY, 0, 0, tiled=True)
    (out,) = on_chip(
        final_kernel,
        "final",
        [((points, CLUSTER_COUNT), jnp.float32)],
        [second, jnp.sum(parts, axis=0)],
    )
    return out


def solution(mesh):
    finer = Mesh(mesh.devices.reshape(SIZES), EVERY)
    return jax.shard_map(
        shards, mesh=finer, in_specs=(P(EVERY, None), P(EVERY)), out_specs=P(EVERY, None), check_vma=False
    )
```

```python
import functools
import itertools

import jax
import jax.numpy as jnp
from jax import lax
from jax.experimental import pallas as pl
from jax.experimental.pallas import tpu as pltpu
from jax.sharding import Mesh
from jax.sharding import PartitionSpec as P

CLUSTER_COUNT = 128
ANNEAL_TEMP_VALUE = 0.02
SIDE = 8

EVERY = ("y_lo", "z", "y_hi", "x", "core")
SIZES = (2, 4, 2, 4, 2)


def place(y_lo, z, y_hi, x, core):
    return (((y_lo * 4 + z) * 2 + y_hi) * 4 + x) * 2 + core


NEAR = ((0, 1), (2, 3))
FAR = ((0, 3), (1, 2))


def cubes(pairs):
    groups = []
    for along_y, along_z, along_x, core in itertools.product(pairs, pairs, pairs, range(2)):
        groups.append([place(y % 2, z, y // 2, x, core) for y in along_y for z in along_z for x in along_x])
    return groups


ROW_GROUPS, COLUMN_GROUPS = cubes(NEAR), cubes(FAR)
ROW_ORDER = (0, 1, 2, 4, 3, 5, 6, 7)


def exchange_rows(blocks):
    return lax.all_to_all(blocks, EVERY, 0, 0, axis_index_groups=ROW_GROUPS, tiled=True)


def exchange_columns(blocks):
    return lax.all_to_all(blocks, EVERY, 0, 0, axis_index_groups=COLUMN_GROUPS, tiled=True)


def moved(x, flips):
    along_y, along_z, along_x = flips // 4, flips // 2 % 2, flips % 2
    pairs = []
    for lo, z, hi, at, core in itertools.product(*map(range, SIZES)):
        pairs.append((place(lo ^ along_y, z ^ along_z, hi, at ^ along_x, core), place(lo, z, hi, at, core)))
    return lax.ppermute(x, EVERY, pairs)


def row_peers(x):
    return [moved(x, flips) if flips else x for flips in ROW_ORDER]


def member_at(offset):
    member = 0
    for name, bit in (("y_lo", 4), ("z", 2), ("x", 1)):
        own = lax.axis_index(name) % 2
        member += bit * ((1 - own) if ROW_ORDER[offset] & bit else own)
    return member


def halves(x):
    high = x.astype(jnp.bfloat16)
    return high, (x - high.astype(jnp.float32)).astype(jnp.bfloat16)


def product(a, b):
    return jnp.dot(a, b, preferred_element_type=jnp.float32)


def seed_member(seeds):
    labels = lax.broadcasted_iota(jnp.int32, (CLUSTER_COUNT, seeds.shape[1]), 0).astype(jnp.float32)
    return 0.5 * (labels == seeds).astype(jnp.float32).T + 0.5 / CLUSTER_COUNT


def tail_rows(*lines):
    at = lax.broadcasted_iota(jnp.int32, (SIDE, CLUSTER_COUNT), 0)
    tail = jnp.zeros((SIDE, CLUSTER_COUNT), jnp.float32)
    for index, line in enumerate(lines):
        tail = jnp.where(at == index, line, tail)
    return tail


def prepare_kernel(embedding, seeds, block, spread, labels, arrived):
    points, width = embedding.shape
    body, end = pl.ds(0, points), pl.ds(points, SIDE)
    loads = [
        pltpu.make_async_copy(embedding, block.at[body], arrived.at[0]),
        pltpu.make_async_copy(seeds, labels, arrived.at[1]),
    ]
    for load in loads:
        load.start()
    for load in loads:
        load.wait()
    x = block[body]
    side = jnp.concatenate([labels[...].astype(jnp.float32), jnp.sum((x * x).T, axis=0, keepdims=True)], axis=1)
    side = jnp.broadcast_to(side, (SIDE, width))
    block[end] = side
    for copy in range(spread.shape[0]):
        spread[copy, body] = x
        spread[copy, end] = side


CHUNK = 256


def weigh(columns, left, squares, high_out, low_out, right, line, member, chunks, keep):
    points, width = columns.shape[1] - SIDE, columns.shape[2]
    for block in range(8):
        at = pl.ds(block * points, points)
        high, low = halves(columns[block, pl.ds(0, points)])
        right[at, pl.ds(0, width)] = high
        right[at, pl.ds(width, width)] = low
        right[at, pl.ds(2 * width, width)] = high
        side = columns[block, pl.ds(points, 1)]
        line[:, at] = jnp.broadcast_to(side[:, points:], (SIDE, points))
        member[at] = seed_member(side[:, :points]).astype(jnp.bfloat16)
    for chunk in range(chunks):
        at = pl.ds(chunk * CHUNK, CHUNK)
        inner = lax.dot_general(left[at], right[...], (((1,), (1,)), ((), ())), preferred_element_type=jnp.float32)
        squared = inner + squares[at] + line[pl.ds(0, 1)]
        high, low = halves(squared * lax.rsqrt(squared))
        high_out[at] = high
        low_out[at] = low
        keep(chunk, product(high, member[...]) + product(low, member[...]))


def own_pair_kernel(*refs):
    rows, (columns, left, squares, high_out, low_out, out, right, line, member) = refs[:8], refs[8:]
    points, width = rows[0].shape[0] - SIDE, rows[0].shape[1]
    for offset, block in enumerate(rows):
        x = block[pl.ds(0, points)]
        at = pl.ds(offset * points, points)
        squares[at] = jnp.sum(x * x, axis=1, keepdims=True) + 1.0
        high, low = halves(-2.0 * x)
        left[at, pl.ds(0, width)] = high
        left[at, pl.ds(width, width)] = high
        left[at, pl.ds(2 * width, width)] = low

    def keep(chunk, total):
        out[pl.ds(chunk * CHUNK, CHUNK)] = total

    weigh(columns, left, squares, high_out, low_out, right, line, member, out.shape[0] // CHUNK, keep)


def other_pair_kernel(*refs):
    rows, (columns, left, squares, weighted, high_out, low_out, out, right, line, member) = refs[:8], refs[8:]
    points = rows[0].shape[0] - SIDE
    cohesion = [jnp.zeros((1, CLUSTER_COUNT), jnp.float32)]

    def keep(chunk, total):
        total += weighted[pl.ds(chunk * CHUNK, CHUNK)]
        for index in range(CHUNK // points):
            offset = chunk * (CHUNK // points) + index
            part = total[index * points : (index + 1) * points]
            out[member_at(offset), pl.ds(0, points)] = part
            own = seed_member(rows[offset][pl.ds(points, 1)][:, :points])
            cohesion[0] += jnp.sum(own * part, axis=0, keepdims=True)

    weigh(columns, left, squares, high_out, low_out, right, line, member, weighted.shape[0] // CHUNK, keep)
    counts = jnp.sum(seed_member(rows[0][pl.ds(points, 1)][:, :points]), axis=0, keepdims=True)
    tail = tail_rows(cohesion[0], counts)
    for target in range(8):
        out[target, pl.ds(points, SIDE)] = tail


def member_kernel(own, other, own_high, own_low, other_high, other_low, first, out, own_member, both):
    points = own.shape[1] - SIDE
    sums = jnp.zeros((SIDE, CLUSTER_COUNT), jnp.float32)
    for block in range(8):
        sums += own[block, pl.ds(points, SIDE)] + other[block, pl.ds(points, SIDE)]
    cohesion, counts = sums[0:1], sums[1:2]
    own_member[...] = jnp.exp(log_softmax_energy(first[pl.ds(0, points)], counts, cohesion))
    sizes = jnp.zeros((1, CLUSTER_COUNT), jnp.float32)
    total = 0.0
    for source, high, low in ((own, own_high, own_low), (other, other_high, other_low)):
        for block in range(8):
            member = jnp.exp(log_softmax_energy(source[block, pl.ds(0, points)], counts, cohesion))
            sizes += jnp.sum(member, axis=0, keepdims=True)
            at = pl.ds(block * points, points)
            both[at, pl.ds(0, CLUSTER_COUNT)], both[at, pl.ds(CLUSTER_COUNT, CLUSTER_COUNT)] = halves(member)
        wide = product(high[...], both[...])
        total += product(low[...], both[:, pl.ds(0, CLUSTER_COUNT)])
        total += wide[:, :CLUSTER_COUNT] + wide[:, CLUSTER_COUNT:]
    tail = tail_rows(sizes)
    for block in range(8):
        out[member_at(block), pl.ds(0, points)] = total[block * points : (block + 1) * points]
        out[member_at(block), pl.ds(points, SIDE)] = tail


def summed(blocks):
    total = blocks[0]
    for block in range(1, 8):
        total += blocks[block]
    return total


def sum_kernel(blocks, out, spread):
    out[...] = summed(blocks)
    spread[...] = jnp.broadcast_to(out[...], spread.shape)


def own_kernel(blocks, own, out, part):
    points = own.shape[0]
    out[...] = summed(blocks)
    part[...] = jnp.sum(own[...] * out[pl.ds(0, points)], axis=0, keepdims=True)


def final_kernel(second, cohesion, out):
    points = out.shape[0]
    out[...] = log_softmax_energy(second[pl.ds(0, points)], second[pl.ds(points, 1)], cohesion[...])


PARAMS = pltpu.CompilerParams(vmem_limit_bytes=12 << 20)


def on_chip(kernel, name, shapes, inputs, scratch=()):
    vmem = pl.BlockSpec(memory_space=pltpu.VMEM)
    specs = [vmem] * len(inputs)
    shapes = [jax.ShapeDtypeStruct(*shape) for shape in shapes]
    return pl.pallas_call(
        kernel,
        out_shape=shapes,
        in_specs=specs,
        out_specs=[vmem] * len(shapes),
        scratch_shapes=scratch,
        compiler_params=PARAMS,
        name=name,
    )(*inputs)


def copies(x, count):
    return jnp.broadcast_to(x, (count, *x.shape))


def other_core(x):
    return lax.ppermute(x, "core", [(0, 1), (1, 0)])


def log_softmax_energy(attraction, counts, cohesion):
    energy = attraction / counts - cohesion / (2.0 * counts**2)
    logits = -energy / ANNEAL_TEMP_VALUE
    highest = jnp.max(logits, axis=1, keepdims=True)
    return logits - highest - jnp.log(jnp.sum(jnp.exp(logits - highest), axis=1, keepdims=True))


def shards(embedding, seed_cluster):
    points, width = embedding.shape
    lines, tall = points + SIDE, 8 * points
    anywhere, vmem = pl.BlockSpec(memory_space=pl.ANY), pl.BlockSpec(memory_space=pltpu.VMEM)
    block, spread = pl.pallas_call(
        prepare_kernel,
        out_shape=[jax.ShapeDtypeStruct((lines, width), jnp.float32), jax.ShapeDtypeStruct((8, lines, width), jnp.float32)],
        in_specs=[anywhere, anywhere],
        out_specs=[vmem, vmem],
        scratch_shapes=[pltpu.VMEM((1, points), jnp.int32), pltpu.SemaphoreType.DMA((2,))],
        compiler_params=PARAMS,
        name="prepare",
    )(embedding, seed_cluster.reshape(1, points))
    columns = exchange_columns(spread)
    columns, *rows = lax.optimization_barrier((columns, *row_peers(block)))
    kept = ((tall, tall), jnp.bfloat16)
    exchange = ((8, lines, CLUSTER_COUNT), jnp.float32)
    scratch = [
        pltpu.VMEM((tall, 3 * width), jnp.bfloat16),
        pltpu.VMEM((SIDE, tall), jnp.float32),
        pltpu.VMEM((tall, CLUSTER_COUNT), jnp.bfloat16),
    ]
    left, squares, own_high, own_low, weighted = on_chip(
        own_pair_kernel,
        "own_pairs",
        [((tall, 3 * width), jnp.bfloat16), ((tall, 1), jnp.float32), kept, kept, ((tall, CLUSTER_COUNT), jnp.float32)],
        [*rows, columns],
        scratch=scratch,
    )
    other_high, other_low, weighted = on_chip(
        other_pair_kernel,
        "other_pairs",
        [kept, kept, exchange],
        [*rows, other_core(columns), left, squares, weighted],
        scratch=scratch,
    )

    line = ((lines, CLUSTER_COUNT), jnp.float32)
    first, spread = on_chip(sum_kernel, "sum_spread", [line, exchange], [exchange_rows(weighted)])
    firsts = exchange_columns(spread)
    weighted, own = on_chip(
        member_kernel,
        "members",
        [exchange, ((points, CLUSTER_COUNT), jnp.float32)],
        [firsts, other_core(firsts), own_high, own_low, other_high, other_low, first],
        scratch=[pltpu.VMEM((tall, 2 * CLUSTER_COUNT), jnp.bfloat16)],
    )

    part = ((1, CLUSTER_COUNT), jnp.float32)
    second, part = on_chip(own_kernel, "own_sums", [line, part], [exchange_rows(weighted), own])
    parts = lax.all_to_all(copies(part, 128), EVERY, 0, 0, tiled=True)
    (out,) = on_chip(
        final_kernel,
        "final",
        [((points, CLUSTER_COUNT), jnp.float32)],
        [second, jnp.sum(parts, axis=0)],
    )
    return out


def solution(mesh):
    finer = Mesh(mesh.devices.reshape(SIZES), EVERY)
    return jax.shard_map(
        shards, mesh=finer, in_specs=(P(EVERY, None), P(EVERY)), out_specs=P(EVERY, None), check_vma=False
    )
```

```python
import functools
import itertools

import jax
import jax.numpy as jnp
from jax import lax
from jax.experimental import pallas as pl
from jax.experimental.pallas import tpu as pltpu
from jax.sharding import Mesh
from jax.sharding import PartitionSpec as P

CLUSTER_COUNT = 128
ANNEAL_TEMP_VALUE = 0.02
SIDE = 8

EVERY = ("y_lo", "z", "y_hi", "x", "core")
SIZES = (2, 4, 2, 4, 2)


def place(y_lo, z, y_hi, x, core):
    return (((y_lo * 4 + z) * 2 + y_hi) * 4 + x) * 2 + core


NEAR = ((0, 1), (2, 3))
FAR = ((0, 3), (1, 2))


def cubes(pairs):
    groups = []
    for along_y, along_z, along_x, core in itertools.product(pairs, pairs, pairs, range(2)):
        groups.append([place(y % 2, z, y // 2, x, core) for y in along_y for z in along_z for x in along_x])
    return groups


ROW_GROUPS, COLUMN_GROUPS = cubes(NEAR), cubes(FAR)
ROW_ORDER = (0, 1, 2, 4, 3, 5, 6, 7)


def exchange_rows(blocks):
    return lax.all_to_all(blocks, EVERY, 0, 0, axis_index_groups=ROW_GROUPS, tiled=True)


def exchange_columns(blocks):
    return lax.all_to_all(blocks, EVERY, 0, 0, axis_index_groups=COLUMN_GROUPS, tiled=True)


def moved(x, flips):
    along_y, along_z, along_x = flips // 4, flips // 2 % 2, flips % 2
    pairs = []
    for lo, z, hi, at, core in itertools.product(*map(range, SIZES)):
        pairs.append((place(lo ^ along_y, z ^ along_z, hi, at ^ along_x, core), place(lo, z, hi, at, core)))
    return lax.ppermute(x, EVERY, pairs)


def row_peers(x):
    return [moved(x, flips) if flips else x for flips in ROW_ORDER]


def member_at(offset):
    member = 0
    for name, bit in (("y_lo", 4), ("z", 2), ("x", 1)):
        own = lax.axis_index(name) % 2
        member += bit * ((1 - own) if ROW_ORDER[offset] & bit else own)
    return member


def halves(x):
    high = x.astype(jnp.bfloat16)
    return high, (x - high.astype(jnp.float32)).astype(jnp.bfloat16)


def product(a, b):
    return jnp.dot(a, b, preferred_element_type=jnp.float32)


def seed_member(seeds):
    labels = lax.broadcasted_iota(jnp.int32, (CLUSTER_COUNT, seeds.shape[1]), 0).astype(jnp.float32)
    return 0.5 * (labels == seeds).astype(jnp.float32).T + 0.5 / CLUSTER_COUNT


def tail_rows(*lines):
    at = lax.broadcasted_iota(jnp.int32, (SIDE, CLUSTER_COUNT), 0)
    tail = jnp.zeros((SIDE, CLUSTER_COUNT), jnp.float32)
    for index, line in enumerate(lines):
        tail = jnp.where(at == index, line, tail)
    return tail


def prepare_kernel(embedding, seeds, block, spread, labels, arrived):
    points, width = embedding.shape
    body, end = pl.ds(0, points), pl.ds(points, SIDE)
    loads = [
        pltpu.make_async_copy(embedding, block.at[body], arrived.at[0]),
        pltpu.make_async_copy(seeds, labels, arrived.at[1]),
    ]
    for load in loads:
        load.start()
    for load in loads:
        load.wait()
    x = block[body]
    side = jnp.concatenate([labels[...].astype(jnp.float32), jnp.sum((x * x).T, axis=0, keepdims=True)], axis=1)
    side = jnp.broadcast_to(side, (SIDE, width))
    block[end] = side
    for copy in range(spread.shape[0]):
        spread[copy, body] = x
        spread[copy, end] = side


CHUNK = 256
EARLY = 3


def set_columns(columns, right, line, member):
    points, width = columns.shape[1] - SIDE, columns.shape[2]
    for block in range(8):
        at = pl.ds(block * points, points)
        high, low = halves(columns[block, pl.ds(0, points)])
        right[at, pl.ds(0, width)] = high
        right[at, pl.ds(width, width)] = low
        right[at, pl.ds(2 * width, width)] = high
        side = columns[block, pl.ds(points, 1)]
        line[:, at] = jnp.broadcast_to(side[:, points:], (SIDE, points))
        member[at] = seed_member(side[:, :points]).astype(jnp.bfloat16)


def left_rows(x):
    high, low = halves(-2.0 * x)
    return jnp.concatenate([high, high, low], axis=1), jnp.sum(x * x, axis=1, keepdims=True) + 1.0


def weigh(left, square, right, line, member, high_out, low_out, at):
    inner = lax.dot_general(left, right[...], (((1,), (1,)), ((), ())), preferred_element_type=jnp.float32)
    squared = inner + square + line[pl.ds(0, 1)]
    high, low = halves(squared * lax.rsqrt(squared))
    high_out[at] = high
    low_out[at] = low
    return product(high, member[...]) + product(low, member[...])


def own_pair_kernel(*refs):
    rows, (columns, left, squares, right, line, member, high_out, low_out, out) = refs[:6], refs[6:]
    points = rows[0].shape[0] - SIDE
    set_columns(columns, right, line, member)
    for chunk in range(EARLY):
        at = pl.ds(chunk * CHUNK, CHUNK)
        x = jnp.concatenate([block[pl.ds(0, points)] for block in rows[2 * chunk : 2 * chunk + 2]], axis=0)
        left[at], squares[at] = left_rows(x)
        out[at] = weigh(left[at], squares[at], right, line, member, high_out, low_out, at)


def other_pair_kernel(*refs):
    rows, refs = refs[:8], refs[8:]
    columns, left, squares, own_right, own_line, own_member, _, _, weighted, *refs = refs
    own_high, own_low, high_out, low_out, out, right, line, member = refs
    points = rows[0].shape[0] - SIDE
    cohesion = jnp.zeros((1, CLUSTER_COUNT), jnp.float32)
    set_columns(columns, right, line, member)
    for chunk in range(EARLY + 1):
        at = pl.ds(chunk * CHUNK, CHUNK)
        if chunk < EARLY:
            lefts, square, total = left[at], squares[at], weighted[at]
        else:
            lefts, square = left_rows(jnp.concatenate([block[pl.ds(0, points)] for block in rows[6:]], axis=0))
            total = weigh(lefts, square, own_right, own_line, own_member, own_high, own_low, at)
        total += weigh(lefts, square, right, line, member, high_out, low_out, at)
        for index in range(2):
            offset = 2 * chunk + index
            part = total[index * points : (index + 1) * points]
            out[member_at(offset), pl.ds(0, points)] = part
            own = seed_member(rows[offset][pl.ds(points, 1)][:, :points])
            cohesion += jnp.sum(own * part, axis=0, keepdims=True)
    counts = jnp.sum(seed_member(rows[0][pl.ds(points, 1)][:, :points]), axis=0, keepdims=True)
    tail = tail_rows(cohesion, counts)
    for target in range(8):
        out[target, pl.ds(points, SIDE)] = tail


def tail_kernel(blocks, out):
    points = blocks.shape[1] - SIDE
    out[...] = sum(blocks[block, pl.ds(points, SIDE)] for block in range(8))


def half_product(source, sums, high, low, both):
    points = source.shape[1] - SIDE
    sizes = jnp.zeros((1, CLUSTER_COUNT), jnp.float32)
    for block in range(8):
        member = jnp.exp(log_softmax_energy(source[block, pl.ds(0, points)], sums[1:2], sums[0:1]))
        sizes += jnp.sum(member, axis=0, keepdims=True)
        at = pl.ds(block * points, points)
        both[at, pl.ds(0, CLUSTER_COUNT)], both[at, pl.ds(CLUSTER_COUNT, CLUSTER_COUNT)] = halves(member)
    wide = product(high[...], both[...])
    total = product(low[...], both[:, pl.ds(0, CLUSTER_COUNT)])
    return total + wide[:, :CLUSTER_COUNT] + wide[:, CLUSTER_COUNT:], sizes


def own_member_kernel(blocks, tail, far_tail, high, low, first, out, sums, own_member, both):
    points = own_member.shape[0]
    both_tails = tail[...] + far_tail[...]
    own_member[...] = jnp.exp(log_softmax_energy(first[pl.ds(0, points)], both_tails[1:2], both_tails[0:1]))
    out[...], sizes = half_product(blocks, both_tails, high, low, both)
    sums[...] = tail_rows(both_tails[0:1], both_tails[1:2], sizes)


def other_member_kernel(blocks, sums, high, low, weighted, out, both):
    points = blocks.shape[1] - SIDE
    total, sizes = half_product(blocks, sums[...], high, low, both)
    total += weighted[...]
    tail = tail_rows(sums[pl.ds(2, 1)] + sizes)
    for block in range(8):
        out[member_at(block), pl.ds(0, points)] = total[block * points : (block + 1) * points]
        out[member_at(block), pl.ds(points, SIDE)] = tail


def summed(blocks):
    total = blocks[0]
    for block in range(1, 8):
        total += blocks[block]
    return total


def sum_kernel(blocks, out, spread):
    out[...] = summed(blocks)
    spread[...] = jnp.broadcast_to(out[...], spread.shape)


def own_kernel(blocks, own, out, part):
    points = own.shape[0]
    out[...] = summed(blocks)
    part[...] = jnp.sum(own[...] * out[pl.ds(0, points)], axis=0, keepdims=True)


def final_kernel(second, cohesion, out):
    points = out.shape[0]
    out[...] = log_softmax_energy(second[pl.ds(0, points)], second[pl.ds(points, 1)], cohesion[...])


PARAMS = pltpu.CompilerParams(vmem_limit_bytes=12 << 20)


def on_chip(kernel, name, shapes, inputs, scratch=(), aliases={}):
    vmem = pl.BlockSpec(memory_space=pltpu.VMEM)
    specs = [vmem] * len(inputs)
    shapes = [jax.ShapeDtypeStruct(*shape) for shape in shapes]
    return pl.pallas_call(
        kernel,
        out_shape=shapes,
        in_specs=specs,
        out_specs=[vmem] * len(shapes),
        scratch_shapes=scratch,
        input_output_aliases=aliases,
        compiler_params=PARAMS,
        name=name,
    )(*inputs)


def copies(x, count):
    return jnp.broadcast_to(x, (count, *x.shape))


def other_core(x):
    return lax.ppermute(x, "core", [(0, 1), (1, 0)])


def log_softmax_energy(attraction, counts, cohesion):
    energy = attraction / counts - cohesion / (2.0 * counts**2)
    logits = -energy / ANNEAL_TEMP_VALUE
    highest = jnp.max(logits, axis=1, keepdims=True)
    return logits - highest - jnp.log(jnp.sum(jnp.exp(logits - highest), axis=1, keepdims=True))


def shards(embedding, seed_cluster):
    points, width = embedding.shape
    lines, tall = points + SIDE, 8 * points
    outside, vmem = pl.BlockSpec(memory_space=pltpu.HBM), pl.BlockSpec(memory_space=pltpu.VMEM)
    block, spread = pl.pallas_call(
        prepare_kernel,
        out_shape=[jax.ShapeDtypeStruct((lines, width), jnp.float32), jax.ShapeDtypeStruct((8, lines, width), jnp.float32)],
        in_specs=[outside, outside],
        out_specs=[vmem, vmem],
        scratch_shapes=[pltpu.VMEM((1, points), jnp.int32), pltpu.SemaphoreType.DMA((2,))],
        name="prepare",
    )(embedding, seed_cluster.reshape(1, points))
    columns = exchange_columns(spread)
    rows = row_peers(block)
    columns, *rows[:7] = lax.optimization_barrier((columns, *rows[:7]))
    kept = ((tall, tall), jnp.bfloat16)
    exchange = ((8, lines, CLUSTER_COUNT), jnp.float32)
    early = EARLY * CHUNK
    sides = [((tall, 3 * width), jnp.bfloat16), ((SIDE, tall), jnp.float32), ((tall, CLUSTER_COUNT), jnp.bfloat16)]
    *prepared, own_high, own_low, weighted = on_chip(
        own_pair_kernel,
        "own_pairs",
        [((early, 3 * width), jnp.bfloat16), ((early, 1), jnp.float32), *sides, kept, kept, ((early, CLUSTER_COUNT), jnp.float32)],
        [*rows[:6], columns],
    )
    own_high, own_low, other_high, other_low, weighted = on_chip(
        other_pair_kernel,
        "other_pairs",
        [kept, kept, kept, kept, exchange],
        [*rows, other_core(columns), *prepared, own_high, own_low, weighted],
        scratch=[pltpu.VMEM(*side) for side in sides],
        aliases={14: 0, 15: 1},
    )

    line = ((lines, CLUSTER_COUNT), jnp.float32)
    tail = ((SIDE, CLUSTER_COUNT), jnp.float32)
    first, spread = on_chip(sum_kernel, "sum_spread", [line, exchange], [exchange_rows(weighted)])
    firsts = exchange_columns(spread)
    (sums,) = on_chip(tail_kernel, "tails", [tail], [firsts])
    far_sums = other_core(sums)
    firsts, far_sums = lax.optimization_barrier((firsts, far_sums))
    both = [pltpu.VMEM((tall, 2 * CLUSTER_COUNT), jnp.bfloat16)]
    weighted, sums, own = on_chip(
        own_member_kernel,
        "own_members",
        [((tall, CLUSTER_COUNT), jnp.float32), tail, ((points, CLUSTER_COUNT), jnp.float32)],
        [firsts, sums, far_sums, own_high, own_low, first],
        scratch=both,
    )
    (weighted,) = on_chip(
        other_member_kernel,
        "other_members",
        [exchange],
        [other_core(firsts), sums, other_high, other_low, weighted],
        scratch=both,
    )

    part = ((1, CLUSTER_COUNT), jnp.float32)
    second, part = on_chip(own_kernel, "own_sums", [line, part], [exchange_rows(weighted), own])
    parts = lax.all_to_all(copies(part, 128), EVERY, 0, 0, tiled=True)
    (out,) = on_chip(
        final_kernel,
        "final",
        [((points, CLUSTER_COUNT), jnp.float32)],
        [second, jnp.sum(parts, axis=0)],
    )
    return out


def solution(mesh):
    finer = Mesh(mesh.devices.reshape(SIZES), EVERY)
    return jax.shard_map(
        shards, mesh=finer, in_specs=(P(EVERY, None), P(EVERY)), out_specs=P(EVERY, None), check_vma=False
    )
```

```python
import functools
import itertools

import jax
import jax.numpy as jnp
from jax import lax
from jax.experimental import pallas as pl
from jax.experimental.pallas import tpu as pltpu
from jax.sharding import Mesh
from jax.sharding import PartitionSpec as P

CLUSTER_COUNT = 128
ANNEAL_TEMP_VALUE = 0.02
SIDE = 8

EVERY = ("y_lo", "z", "y_hi", "x", "core")
SIZES = (2, 4, 2, 4, 2)


def place(y_lo, z, y_hi, x, core):
    return (((y_lo * 4 + z) * 2 + y_hi) * 4 + x) * 2 + core


NEAR = ((0, 1), (2, 3))
FAR = ((0, 3), (1, 2))


def cubes(pairs):
    groups = []
    for along_y, along_z, along_x, core in itertools.product(pairs, pairs, pairs, range(2)):
        groups.append([place(y % 2, z, y // 2, x, core) for y in along_y for z in along_z for x in along_x])
    return groups


ROW_GROUPS, COLUMN_GROUPS = cubes(NEAR), cubes(FAR)
ROW_ORDER = (0, 7, 6, 5, 3, 4, 2, 1)


def exchange_rows(blocks):
    return lax.all_to_all(blocks, EVERY, 0, 0, axis_index_groups=ROW_GROUPS, tiled=True)


def exchange_columns(blocks):
    return lax.all_to_all(blocks, EVERY, 0, 0, axis_index_groups=COLUMN_GROUPS, tiled=True)


def moved(x, flips):
    along_y, along_z, along_x = flips // 4, flips // 2 % 2, flips % 2
    pairs = []
    for lo, z, hi, at, core in itertools.product(*map(range, SIZES)):
        pairs.append((place(lo ^ along_y, z ^ along_z, hi, at ^ along_x, core), place(lo, z, hi, at, core)))
    return lax.ppermute(x, EVERY, pairs)


def row_peers(x):
    return [moved(x, flips) if flips else x for flips in ROW_ORDER]


def member_at(offset):
    member = 0
    for name, bit in (("y_lo", 4), ("z", 2), ("x", 1)):
        own = lax.axis_index(name) % 2
        member += bit * ((1 - own) if ROW_ORDER[offset] & bit else own)
    return member


def halves(x):
    high = x.astype(jnp.bfloat16)
    return high, (x - high.astype(jnp.float32)).astype(jnp.bfloat16)


def product(a, b):
    return jnp.dot(a, b, preferred_element_type=jnp.float32)


def seed_member(seeds):
    labels = lax.broadcasted_iota(jnp.int32, (CLUSTER_COUNT, seeds.shape[1]), 0).astype(jnp.float32)
    return 0.5 * (labels == seeds).astype(jnp.float32).T + 0.5 / CLUSTER_COUNT


def tail_rows(*lines):
    at = lax.broadcasted_iota(jnp.int32, (SIDE, CLUSTER_COUNT), 0)
    tail = jnp.zeros((SIDE, CLUSTER_COUNT), jnp.float32)
    for index, line in enumerate(lines):
        tail = jnp.where(at == index, line, tail)
    return tail


def prepare_kernel(embedding, seeds, block, spread, labels, arrived):
    points, width = embedding.shape
    body, end = pl.ds(0, points), pl.ds(points, SIDE)
    loads = [
        pltpu.make_async_copy(embedding, block.at[body], arrived.at[0]),
        pltpu.make_async_copy(seeds, labels, arrived.at[1]),
    ]
    for load in loads:
        load.start()
    for load in loads:
        load.wait()
    x = block[body]
    side = jnp.concatenate([labels[...].astype(jnp.float32), jnp.sum((x * x).T, axis=0, keepdims=True)], axis=1)
    side = jnp.broadcast_to(side, (SIDE, width))
    block[end] = side
    for copy in range(spread.shape[0]):
        spread[copy, body] = x
        spread[copy, end] = side


CHUNK = 256


def weigh(columns, left, squares, high_out, low_out, right, line, member, chunks, keep):
    points, width = columns.shape[1] - SIDE, columns.shape[2]
    for block in range(8):
        at = pl.ds(block * points, points)
        high, low = halves(columns[block, pl.ds(0, points)])
        right[at, pl.ds(0, width)] = high
        right[at, pl.ds(width, width)] = low
        right[at, pl.ds(2 * width, width)] = high
        side = columns[block, pl.ds(points, 1)]
        line[:, at] = jnp.broadcast_to(side[:, points:], (SIDE, points))
        member[at] = seed_member(side[:, :points]).astype(jnp.bfloat16)
    for chunk in range(chunks):
        at = pl.ds(chunk * CHUNK, CHUNK)
        inner = lax.dot_general(left[at], right[...], (((1,), (1,)), ((), ())), preferred_element_type=jnp.float32)
        squared = inner + squares[at] + line[pl.ds(0, 1)]
        high, low = halves(squared * lax.rsqrt(squared))
        high_out[at] = high
        low_out[at] = low
        keep(chunk, product(high, member[...]) + product(low, member[...]))


def own_pair_kernel(*refs):
    rows, (columns, left, squares, high_out, low_out, out, right, line, member) = refs[:8], refs[8:]
    points, width = rows[0].shape[0] - SIDE, rows[0].shape[1]
    for offset, block in enumerate(rows):
        x = block[pl.ds(0, points)]
        at = pl.ds(offset * points, points)
        squares[at] = jnp.sum(x * x, axis=1, keepdims=True) + 1.0
        high, low = halves(-2.0 * x)
        left[at, pl.ds(0, width)] = high
        left[at, pl.ds(width, width)] = high
        left[at, pl.ds(2 * width, width)] = low

    def keep(chunk, total):
        out[pl.ds(chunk * CHUNK, CHUNK)] = total

    weigh(columns, left, squares, high_out, low_out, right, line, member, out.shape[0] // CHUNK, keep)


def other_pair_kernel(*refs):
    rows, (columns, left, squares, weighted, high_out, low_out, out, right, line, member) = refs[:8], refs[8:]
    points = rows[0].shape[0] - SIDE
    cohesion = [jnp.zeros((1, CLUSTER_COUNT), jnp.float32)]

    def keep(chunk, total):
        total += weighted[pl.ds(chunk * CHUNK, CHUNK)]
        for index in range(CHUNK // points):
            offset = chunk * (CHUNK // points) + index
            part = total[index * points : (index + 1) * points]
            out[member_at(offset), pl.ds(0, points)] = part
            own = seed_member(rows[offset][pl.ds(points, 1)][:, :points])
            cohesion[0] += jnp.sum(own * part, axis=0, keepdims=True)

    weigh(columns, left, squares, high_out, low_out, right, line, member, weighted.shape[0] // CHUNK, keep)
    counts = jnp.sum(seed_member(rows[0][pl.ds(points, 1)][:, :points]), axis=0, keepdims=True)
    tail = tail_rows(cohesion[0], counts)
    for target in range(8):
        out[target, pl.ds(points, SIDE)] = tail


def member_kernel(own, other, own_high, own_low, other_high, other_low, first, out, own_member, both):
    points = own.shape[1] - SIDE
    sums = jnp.zeros((SIDE, CLUSTER_COUNT), jnp.float32)
    for block in range(8):
        sums += own[block, pl.ds(points, SIDE)] + other[block, pl.ds(points, SIDE)]
    cohesion, counts = sums[0:1], sums[1:2]
    own_member[...] = jnp.exp(log_softmax_energy(first[pl.ds(0, points)], counts, cohesion))
    sizes = jnp.zeros((1, CLUSTER_COUNT), jnp.float32)
    total = 0.0
    for source, high, low in ((own, own_high, own_low), (other, other_high, other_low)):
        for block in range(8):
            member = jnp.exp(log_softmax_energy(source[block, pl.ds(0, points)], counts, cohesion))
            sizes += jnp.sum(member, axis=0, keepdims=True)
            at = pl.ds(block * points, points)
            both[at, pl.ds(0, CLUSTER_COUNT)], both[at, pl.ds(CLUSTER_COUNT, CLUSTER_COUNT)] = halves(member)
        wide = product(high[...], both[...])
        total += product(low[...], both[:, pl.ds(0, CLUSTER_COUNT)])
        total += wide[:, :CLUSTER_COUNT] + wide[:, CLUSTER_COUNT:]
    tail = tail_rows(sizes)
    for block in range(8):
        out[member_at(block), pl.ds(0, points)] = total[block * points : (block + 1) * points]
        out[member_at(block), pl.ds(points, SIDE)] = tail


def summed(blocks):
    total = blocks[0]
    for block in range(1, 8):
        total += blocks[block]
    return total


def sum_kernel(blocks, out, spread):
    out[...] = summed(blocks)
    spread[...] = jnp.broadcast_to(out[...], spread.shape)


def own_kernel(blocks, own, out, part):
    points = own.shape[0]
    out[...] = summed(blocks)
    part[...] = jnp.sum(own[...] * out[pl.ds(0, points)], axis=0, keepdims=True)


def final_kernel(second, cohesion, out):
    points = out.shape[0]
    out[...] = log_softmax_energy(second[pl.ds(0, points)], second[pl.ds(points, 1)], cohesion[...])


PARAMS = pltpu.CompilerParams(vmem_limit_bytes=12 << 20)


def on_chip(kernel, name, shapes, inputs, scratch=()):
    vmem = pl.BlockSpec(memory_space=pltpu.VMEM)
    specs = [vmem] * len(inputs)
    shapes = [jax.ShapeDtypeStruct(*shape) for shape in shapes]
    return pl.pallas_call(
        kernel,
        out_shape=shapes,
        in_specs=specs,
        out_specs=[vmem] * len(shapes),
        scratch_shapes=scratch,
        compiler_params=PARAMS,
        name=name,
    )(*inputs)


def copies(x, count):
    return jnp.broadcast_to(x, (count, *x.shape))


def other_core(x):
    return lax.ppermute(x, "core", [(0, 1), (1, 0)])


def log_softmax_energy(attraction, counts, cohesion):
    energy = attraction / counts - cohesion / (2.0 * counts**2)
    logits = -energy / ANNEAL_TEMP_VALUE
    highest = jnp.max(logits, axis=1, keepdims=True)
    return logits - highest - jnp.log(jnp.sum(jnp.exp(logits - highest), axis=1, keepdims=True))


def shards(embedding, seed_cluster):
    points, width = embedding.shape
    lines, tall = points + SIDE, 8 * points
    outside, vmem = pl.BlockSpec(memory_space=pltpu.HBM), pl.BlockSpec(memory_space=pltpu.VMEM)
    block, spread = pl.pallas_call(
        prepare_kernel,
        out_shape=[jax.ShapeDtypeStruct((lines, width), jnp.float32), jax.ShapeDtypeStruct((8, lines, width), jnp.float32)],
        in_specs=[outside, outside],
        out_specs=[vmem, vmem],
        scratch_shapes=[pltpu.VMEM((1, points), jnp.int32), pltpu.SemaphoreType.DMA((2,))],
        name="prepare",
    )(embedding, seed_cluster.reshape(1, points))
    columns = exchange_columns(spread)
    columns, *rows = lax.optimization_barrier((columns, *row_peers(block)))
    kept = ((tall, tall), jnp.bfloat16)
    exchange = ((8, lines, CLUSTER_COUNT), jnp.float32)
    scratch = [
        pltpu.VMEM((tall, 3 * width), jnp.bfloat16),
        pltpu.VMEM((SIDE, tall), jnp.float32),
        pltpu.VMEM((tall, CLUSTER_COUNT), jnp.bfloat16),
    ]
    left, squares, own_high, own_low, weighted = on_chip(
        own_pair_kernel,
        "own_pairs",
        [((tall, 3 * width), jnp.bfloat16), ((tall, 1), jnp.float32), kept, kept, ((tall, CLUSTER_COUNT), jnp.float32)],
        [*rows, columns],
        scratch=scratch,
    )
    other_high, other_low, weighted = on_chip(
        other_pair_kernel,
        "other_pairs",
        [kept, kept, exchange],
        [*rows, other_core(columns), left, squares, weighted],
        scratch=scratch,
    )

    line = ((lines, CLUSTER_COUNT), jnp.float32)
    first, spread = on_chip(sum_kernel, "sum_spread", [line, exchange], [exchange_rows(weighted)])
    firsts = exchange_columns(spread)
    weighted, own = on_chip(
        member_kernel,
        "members",
        [exchange, ((points, CLUSTER_COUNT), jnp.float32)],
        [firsts, other_core(firsts), own_high, own_low, other_high, other_low, first],
        scratch=[pltpu.VMEM((tall, 2 * CLUSTER_COUNT), jnp.bfloat16)],
    )

    part = ((1, CLUSTER_COUNT), jnp.float32)
    second, part = on_chip(own_kernel, "own_sums", [line, part], [exchange_rows(weighted), own])
    parts = lax.all_to_all(copies(part, 128), EVERY, 0, 0, tiled=True)
    (out,) = on_chip(
        final_kernel,
        "final",
        [((points, CLUSTER_COUNT), jnp.float32)],
        [second, jnp.sum(parts, axis=0)],
    )
    return out


def solution(mesh):
    finer = Mesh(mesh.devices.reshape(SIZES), EVERY)
    return jax.shard_map(
        shards, mesh=finer, in_specs=(P(EVERY, None), P(EVERY)), out_specs=P(EVERY, None), check_vma=False
    )
```

```python
import functools
import itertools

import jax
import jax.numpy as jnp
from jax import lax
from jax.experimental import pallas as pl
from jax.experimental.pallas import tpu as pltpu
from jax.sharding import Mesh
from jax.sharding import PartitionSpec as P

CLUSTER_COUNT = 128
ANNEAL_TEMP_VALUE = 0.02
SIDE = 8

EVERY = ("y_lo", "z", "y_hi", "x", "core")
SIZES = (2, 4, 2, 4, 2)


def place(y_lo, z, y_hi, x, core):
    return (((y_lo * 4 + z) * 2 + y_hi) * 4 + x) * 2 + core


NEAR = ((0, 1), (2, 3))
FAR = ((0, 3), (1, 2))


def cubes(pairs):
    groups = []
    for along_y, along_z, along_x, core in itertools.product(pairs, pairs, pairs, range(2)):
        groups.append([place(y % 2, z, y // 2, x, core) for y in along_y for z in along_z for x in along_x])
    return groups


ROW_GROUPS, COLUMN_GROUPS = cubes(NEAR), cubes(FAR)
ROW_ORDER = (0, 7, 6, 5, 3, 4, 2, 1)


def exchange_rows(blocks):
    return lax.all_to_all(blocks, EVERY, 0, 0, axis_index_groups=ROW_GROUPS, tiled=True)


def exchange_columns(blocks):
    return lax.all_to_all(blocks, EVERY, 0, 0, axis_index_groups=COLUMN_GROUPS, tiled=True)


def moved(x, flips):
    along_y, along_z, along_x = flips // 4, flips // 2 % 2, flips % 2
    pairs = []
    for lo, z, hi, at, core in itertools.product(*map(range, SIZES)):
        pairs.append((place(lo ^ along_y, z ^ along_z, hi, at ^ along_x, core), place(lo, z, hi, at, core)))
    return lax.ppermute(x, EVERY, pairs)


def row_peers(x):
    return [moved(x, flips) if flips else x for flips in ROW_ORDER]


def member_at(offset):
    member = 0
    for name, bit in (("y_lo", 4), ("z", 2), ("x", 1)):
        own = lax.axis_index(name) % 2
        member += bit * ((1 - own) if ROW_ORDER[offset] & bit else own)
    return member


def halves(x):
    high = x.astype(jnp.bfloat16)
    return high, (x - high.astype(jnp.float32)).astype(jnp.bfloat16)


def product(a, b):
    return jnp.dot(a, b, preferred_element_type=jnp.float32)


def seed_member(seeds):
    labels = lax.broadcasted_iota(jnp.int32, (CLUSTER_COUNT, seeds.shape[1]), 0).astype(jnp.float32)
    return 0.5 * (labels == seeds).astype(jnp.float32).T + 0.5 / CLUSTER_COUNT


def tail_rows(*lines):
    at = lax.broadcasted_iota(jnp.int32, (SIDE, CLUSTER_COUNT), 0)
    tail = jnp.zeros((SIDE, CLUSTER_COUNT), jnp.float32)
    for index, line in enumerate(lines):
        tail = jnp.where(at == index, line, tail)
    return tail


def prepare_kernel(embedding, seeds, block, spread, labels, arrived):
    points, width = embedding.shape
    body, end = pl.ds(0, points), pl.ds(points, SIDE)
    loads = [
        pltpu.make_async_copy(embedding, block.at[body], arrived.at[0]),
        pltpu.make_async_copy(seeds, labels, arrived.at[1]),
    ]
    for load in loads:
        load.start()
    for load in loads:
        load.wait()
    x = block[body]
    side = jnp.concatenate([labels[...].astype(jnp.float32), jnp.sum((x * x).T, axis=0, keepdims=True)], axis=1)
    side = jnp.broadcast_to(side, (SIDE, width))
    block[end] = side
    for copy in range(spread.shape[0]):
        spread[copy, body] = x
        spread[copy, end] = side


CHUNK = 256
EARLY = 3


def set_columns(columns, right, line, member):
    points, width = columns.shape[1] - SIDE, columns.shape[2]
    for block in range(8):
        at = pl.ds(block * points, points)
        high, low = halves(columns[block, pl.ds(0, points)])
        right[at, pl.ds(0, width)] = high
        right[at, pl.ds(width, width)] = low
        right[at, pl.ds(2 * width, width)] = high
        side = columns[block, pl.ds(points, 1)]
        line[:, at] = jnp.broadcast_to(side[:, points:], (SIDE, points))
        member[at] = seed_member(side[:, :points]).astype(jnp.bfloat16)


def left_rows(x):
    high, low = halves(-2.0 * x)
    return jnp.concatenate([high, high, low], axis=1), jnp.sum(x * x, axis=1, keepdims=True) + 1.0


def weigh(left, square, right, line, member, high_out, low_out, at):
    inner = lax.dot_general(left, right[...], (((1,), (1,)), ((), ())), preferred_element_type=jnp.float32)
    squared = inner + square + line[pl.ds(0, 1)]
    high, low = halves(squared * lax.rsqrt(squared))
    high_out[at] = high
    low_out[at] = low
    return product(high, member[...]) + product(low, member[...])


def own_pair_kernel(*refs):
    rows, (columns, left, squares, right, line, member, high_out, low_out, out) = refs[:6], refs[6:]
    points = rows[0].shape[0] - SIDE
    set_columns(columns, right, line, member)
    for chunk in range(EARLY):
        at = pl.ds(chunk * CHUNK, CHUNK)
        x = jnp.concatenate([block[pl.ds(0, points)] for block in rows[2 * chunk : 2 * chunk + 2]], axis=0)
        left[at], squares[at] = left_rows(x)
        out[at] = weigh(left[at], squares[at], right, line, member, high_out, low_out, at)


def other_pair_kernel(*refs):
    rows, refs = refs[:8], refs[8:]
    columns, left, squares, own_right, own_line, own_member, _, _, weighted, *refs = refs
    own_high, own_low, high_out, low_out, out, right, line, member = refs
    points = rows[0].shape[0] - SIDE
    cohesion = jnp.zeros((1, CLUSTER_COUNT), jnp.float32)
    set_columns(columns, right, line, member)
    for chunk in range(EARLY + 1):
        at = pl.ds(chunk * CHUNK, CHUNK)
        if chunk < EARLY:
            lefts, square, total = left[at], squares[at], weighted[at]
        else:
            lefts, square = left_rows(jnp.concatenate([block[pl.ds(0, points)] for block in rows[6:]], axis=0))
            total = weigh(lefts, square, own_right, own_line, own_member, own_high, own_low, at)
        total += weigh(lefts, square, right, line, member, high_out, low_out, at)
        for index in range(2):
            offset = 2 * chunk + index
            part = total[index * points : (index + 1) * points]
            out[member_at(offset), pl.ds(0, points)] = part
            own = seed_member(rows[offset][pl.ds(points, 1)][:, :points])
            cohesion += jnp.sum(own * part, axis=0, keepdims=True)
    counts = jnp.sum(seed_member(rows[0][pl.ds(points, 1)][:, :points]), axis=0, keepdims=True)
    tail = tail_rows(cohesion, counts)
    for target in range(8):
        out[target, pl.ds(points, SIDE)] = tail


def tail_kernel(blocks, out):
    points = blocks.shape[1] - SIDE
    out[...] = sum(blocks[block, pl.ds(points, SIDE)] for block in range(8))


def half_product(source, sums, high, low, both):
    points = source.shape[1] - SIDE
    sizes = jnp.zeros((1, CLUSTER_COUNT), jnp.float32)
    for block in range(8):
        member = jnp.exp(log_softmax_energy(source[block, pl.ds(0, points)], sums[1:2], sums[0:1]))
        sizes += jnp.sum(member, axis=0, keepdims=True)
        at = pl.ds(block * points, points)
        both[at, pl.ds(0, CLUSTER_COUNT)], both[at, pl.ds(CLUSTER_COUNT, CLUSTER_COUNT)] = halves(member)
    wide = product(high[...], both[...])
    total = product(low[...], both[:, pl.ds(0, CLUSTER_COUNT)])
    return total + wide[:, :CLUSTER_COUNT] + wide[:, CLUSTER_COUNT:], sizes


def own_member_kernel(blocks, tail, far_tail, high, low, first, out, sums, own_member, both):
    points = own_member.shape[0]
    both_tails = tail[...] + far_tail[...]
    own_member[...] = jnp.exp(log_softmax_energy(first[pl.ds(0, points)], both_tails[1:2], both_tails[0:1]))
    out[...], sizes = half_product(blocks, both_tails, high, low, both)
    sums[...] = tail_rows(both_tails[0:1], both_tails[1:2], sizes)


def other_member_kernel(blocks, sums, high, low, weighted, out, both):
    points = blocks.shape[1] - SIDE
    total, sizes = half_product(blocks, sums[...], high, low, both)
    total += weighted[...]
    tail = tail_rows(sums[pl.ds(2, 1)] + sizes)
    for block in range(8):
        out[member_at(block), pl.ds(0, points)] = total[block * points : (block + 1) * points]
        out[member_at(block), pl.ds(points, SIDE)] = tail


def summed(blocks):
    total = blocks[0]
    for block in range(1, 8):
        total += blocks[block]
    return total


def sum_kernel(blocks, out, spread):
    out[...] = summed(blocks)
    spread[...] = jnp.broadcast_to(out[...], spread.shape)


def own_kernel(blocks, own, out, part):
    points = own.shape[0]
    out[...] = summed(blocks)
    part[...] = jnp.sum(own[...] * out[pl.ds(0, points)], axis=0, keepdims=True)


def final_kernel(second, cohesion, out):
    points = out.shape[0]
    out[...] = log_softmax_energy(second[pl.ds(0, points)], second[pl.ds(points, 1)], cohesion[...])


PARAMS = pltpu.CompilerParams(vmem_limit_bytes=12 << 20)


def on_chip(kernel, name, shapes, inputs, scratch=(), aliases={}):
    vmem = pl.BlockSpec(memory_space=pltpu.VMEM)
    specs = [vmem] * len(inputs)
    shapes = [jax.ShapeDtypeStruct(*shape) for shape in shapes]
    return pl.pallas_call(
        kernel,
        out_shape=shapes,
        in_specs=specs,
        out_specs=[vmem] * len(shapes),
        scratch_shapes=scratch,
        input_output_aliases=aliases,
        compiler_params=PARAMS,
        name=name,
    )(*inputs)


def copies(x, count):
    return jnp.broadcast_to(x, (count, *x.shape))


def other_core(x):
    return lax.ppermute(x, "core", [(0, 1), (1, 0)])


def log_softmax_energy(attraction, counts, cohesion):
    energy = attraction / counts - cohesion / (2.0 * counts**2)
    logits = -energy / ANNEAL_TEMP_VALUE
    highest = jnp.max(logits, axis=1, keepdims=True)
    return logits - highest - jnp.log(jnp.sum(jnp.exp(logits - highest), axis=1, keepdims=True))


def shards(embedding, seed_cluster):
    points, width = embedding.shape
    lines, tall = points + SIDE, 8 * points
    outside, vmem = pl.BlockSpec(memory_space=pltpu.HBM), pl.BlockSpec(memory_space=pltpu.VMEM)
    block, spread = pl.pallas_call(
        prepare_kernel,
        out_shape=[jax.ShapeDtypeStruct((lines, width), jnp.float32), jax.ShapeDtypeStruct((8, lines, width), jnp.float32)],
        in_specs=[outside, outside],
        out_specs=[vmem, vmem],
        scratch_shapes=[pltpu.VMEM((1, points), jnp.int32), pltpu.SemaphoreType.DMA((2,))],
        name="prepare",
    )(embedding, seed_cluster.reshape(1, points))
    columns = exchange_columns(spread)
    rows = row_peers(block)
    columns, *rows[:7] = lax.optimization_barrier((columns, *rows[:7]))
    kept = ((tall, tall), jnp.bfloat16)
    exchange = ((8, lines, CLUSTER_COUNT), jnp.float32)
    early = EARLY * CHUNK
    sides = [((tall, 3 * width), jnp.bfloat16), ((SIDE, tall), jnp.float32), ((tall, CLUSTER_COUNT), jnp.bfloat16)]
    *prepared, own_high, own_low, weighted = on_chip(
        own_pair_kernel,
        "own_pairs",
        [((early, 3 * width), jnp.bfloat16), ((early, 1), jnp.float32), *sides, kept, kept, ((early, CLUSTER_COUNT), jnp.float32)],
        [*rows[:6], columns],
    )
    own_high, own_low, other_high, other_low, weighted = on_chip(
        other_pair_kernel,
        "other_pairs",
        [kept, kept, kept, kept, exchange],
        [*rows, other_core(columns), *prepared, own_high, own_low, weighted],
        scratch=[pltpu.VMEM(*side) for side in sides],
        aliases={14: 0, 15: 1},
    )

    line = ((lines, CLUSTER_COUNT), jnp.float32)
    tail = ((SIDE, CLUSTER_COUNT), jnp.float32)
    first, spread = on_chip(sum_kernel, "sum_spread", [line, exchange], [exchange_rows(weighted)])
    firsts = exchange_columns(spread)
    (sums,) = on_chip(tail_kernel, "tails", [tail], [firsts])
    far_sums = other_core(sums)
    firsts, far_sums = lax.optimization_barrier((firsts, far_sums))
    both = [pltpu.VMEM((tall, 2 * CLUSTER_COUNT), jnp.bfloat16)]
    weighted, sums, own = on_chip(
        own_member_kernel,
        "own_members",
        [((tall, CLUSTER_COUNT), jnp.float32), tail, ((points, CLUSTER_COUNT), jnp.float32)],
        [firsts, sums, far_sums, own_high, own_low, first],
        scratch=both,
    )
    (weighted,) = on_chip(
        other_member_kernel,
        "other_members",
        [exchange],
        [other_core(firsts), sums, other_high, other_low, weighted],
        scratch=both,
    )

    part = ((1, CLUSTER_COUNT), jnp.float32)
    second, part = on_chip(own_kernel, "own_sums", [line, part], [exchange_rows(weighted), own])
    parts = lax.all_to_all(copies(part, 128), EVERY, 0, 0, tiled=True)
    (out,) = on_chip(
        final_kernel,
        "final",
        [((points, CLUSTER_COUNT), jnp.float32)],
        [second, jnp.sum(parts, axis=0)],
    )
    return out


def solution(mesh):
    finer = Mesh(mesh.devices.reshape(SIZES), EVERY)
    return jax.shard_map(
        shards, mesh=finer, in_specs=(P(EVERY, None), P(EVERY)), out_specs=P(EVERY, None), check_vma=False
    )
```

```python
import functools
import itertools

import jax
import jax.numpy as jnp
from jax import lax
from jax.experimental import pallas as pl
from jax.experimental.pallas import tpu as pltpu
from jax.sharding import Mesh
from jax.sharding import PartitionSpec as P

CLUSTER_COUNT = 128
ANNEAL_TEMP_VALUE = 0.02
SIDE = 8

EVERY = ("y_lo", "z", "y_hi", "x", "core")
SIZES = (2, 4, 2, 4, 2)


def place(y_lo, z, y_hi, x, core):
    return (((y_lo * 4 + z) * 2 + y_hi) * 4 + x) * 2 + core


def column_groups():
    groups = []
    for pair, x, core in itertools.product(range(2), range(4), range(2)):
        groups.append([place(lo, z, lo ^ pair, x, core) for lo in range(2) for z in range(4)])
    return groups


COLUMN_GROUPS = column_groups()
ROW_ORDER = ((0, 0), (1, 2), (1, 3), (1, 1), (0, 2), (1, 0), (0, 3), (0, 1))


def exchange_rows(blocks):
    return lax.all_to_all(blocks, ("y_lo", "x"), 0, 0, tiled=True)


def exchange_columns(blocks):
    return lax.all_to_all(blocks, EVERY, 0, 0, axis_index_groups=COLUMN_GROUPS, tiled=True)


def moved(x, flip, step):
    pairs = []
    for lo, z, hi, at, core in itertools.product(*map(range, SIZES)):
        pairs.append((place(lo ^ flip, z, hi, (at + step) % 4, core), place(lo, z, hi, at, core)))
    return lax.ppermute(x, EVERY, pairs)


def row_peers(x):
    return [moved(x, flip, step) if flip or step else x for flip, step in ROW_ORDER]


def member_at(offset):
    y_lo, x = lax.axis_index("y_lo"), lax.axis_index("x")
    flip, step = ROW_ORDER[offset]
    return ((1 - y_lo) if flip else y_lo) * 4 + (x + step) % 4


def halves(x):
    high = x.astype(jnp.bfloat16)
    return high, (x - high.astype(jnp.float32)).astype(jnp.bfloat16)


def product(a, b):
    return jnp.dot(a, b, preferred_element_type=jnp.float32)


def seed_member(seeds):
    labels = lax.broadcasted_iota(jnp.int32, (CLUSTER_COUNT, seeds.shape[1]), 0).astype(jnp.float32)
    return 0.5 * (labels == seeds).astype(jnp.float32).T + 0.5 / CLUSTER_COUNT


def tail_rows(*lines):
    at = lax.broadcasted_iota(jnp.int32, (SIDE, CLUSTER_COUNT), 0)
    tail = jnp.zeros((SIDE, CLUSTER_COUNT), jnp.float32)
    for index, line in enumerate(lines):
        tail = jnp.where(at == index, line, tail)
    return tail


def prepare_kernel(embedding, seeds, block, spread, labels, arrived):
    points, width = embedding.shape
    body, end = pl.ds(0, points), pl.ds(points, SIDE)
    loads = [
        pltpu.make_async_copy(embedding, block.at[body], arrived.at[0]),
        pltpu.make_async_copy(seeds, labels, arrived.at[1]),
    ]
    for load in loads:
        load.start()
    for load in loads:
        load.wait()
    x = block[body]
    side = jnp.concatenate([labels[...].astype(jnp.float32), jnp.sum((x * x).T, axis=0, keepdims=True)], axis=1)
    side = jnp.broadcast_to(side, (SIDE, width))
    block[end] = side
    for copy in range(spread.shape[0]):
        spread[copy, body] = x
        spread[copy, end] = side


CHUNK = 256


def weigh(columns, left, squares, high_out, low_out, right, line, member, chunks, keep):
    points, width = columns.shape[1] - SIDE, columns.shape[2]
    for block in range(8):
        at = pl.ds(block * points, points)
        high, low = halves(columns[block, pl.ds(0, points)])
        right[at, pl.ds(0, width)] = high
        right[at, pl.ds(width, width)] = low
        right[at, pl.ds(2 * width, width)] = high
        side = columns[block, pl.ds(points, 1)]
        line[:, at] = jnp.broadcast_to(side[:, points:], (SIDE, points))
        member[at] = seed_member(side[:, :points]).astype(jnp.bfloat16)
    for chunk in range(chunks):
        at = pl.ds(chunk * CHUNK, CHUNK)
        inner = lax.dot_general(left[at], right[...], (((1,), (1,)), ((), ())), preferred_element_type=jnp.float32)
        squared = inner + squares[at] + line[pl.ds(0, 1)]
        high, low = halves(squared * lax.rsqrt(squared))
        high_out[at] = high
        low_out[at] = low
        keep(chunk, product(high, member[...]) + product(low, member[...]))


def own_pair_kernel(*refs):
    rows, (columns, left, squares, high_out, low_out, out, right, line, member) = refs[:8], refs[8:]
    points, width = rows[0].shape[0] - SIDE, rows[0].shape[1]
    for offset, block in enumerate(rows):
        x = block[pl.ds(0, points)]
        at = pl.ds(offset * points, points)
        squares[at] = jnp.sum(x * x, axis=1, keepdims=True) + 1.0
        high, low = halves(-2.0 * x)
        left[at, pl.ds(0, width)] = high
        left[at, pl.ds(width, width)] = high
        left[at, pl.ds(2 * width, width)] = low

    def keep(chunk, total):
        out[pl.ds(chunk * CHUNK, CHUNK)] = total

    weigh(columns, left, squares, high_out, low_out, right, line, member, out.shape[0] // CHUNK, keep)


def other_pair_kernel(*refs):
    rows, (columns, left, squares, weighted, high_out, low_out, out, right, line, member) = refs[:8], refs[8:]
    points = rows[0].shape[0] - SIDE
    cohesion = [jnp.zeros((1, CLUSTER_COUNT), jnp.float32)]

    def keep(chunk, total):
        total += weighted[pl.ds(chunk * CHUNK, CHUNK)]
        for index in range(CHUNK // points):
            offset = chunk * (CHUNK // points) + index
            part = total[index * points : (index + 1) * points]
            out[member_at(offset), pl.ds(0, points)] = part
            own = seed_member(rows[offset][pl.ds(points, 1)][:, :points])
            cohesion[0] += jnp.sum(own * part, axis=0, keepdims=True)

    weigh(columns, left, squares, high_out, low_out, right, line, member, weighted.shape[0] // CHUNK, keep)
    counts = jnp.sum(seed_member(rows[0][pl.ds(points, 1)][:, :points]), axis=0, keepdims=True)
    tail = tail_rows(cohesion[0], counts)
    for target in range(8):
        out[target, pl.ds(points, SIDE)] = tail


def member_kernel(own, other, own_high, own_low, other_high, other_low, first, out, own_member, both):
    points = own.shape[1] - SIDE
    sums = jnp.zeros((SIDE, CLUSTER_COUNT), jnp.float32)
    for block in range(8):
        sums += own[block, pl.ds(points, SIDE)] + other[block, pl.ds(points, SIDE)]
    cohesion, counts = sums[0:1], sums[1:2]
    own_member[...] = jnp.exp(log_softmax_energy(first[pl.ds(0, points)], counts, cohesion))
    sizes = jnp.zeros((1, CLUSTER_COUNT), jnp.float32)
    total = 0.0
    for source, high, low in ((own, own_high, own_low), (other, other_high, other_low)):
        for block in range(8):
            member = jnp.exp(log_softmax_energy(source[block, pl.ds(0, points)], counts, cohesion))
            sizes += jnp.sum(member, axis=0, keepdims=True)
            at = pl.ds(block * points, points)
            both[at, pl.ds(0, CLUSTER_COUNT)], both[at, pl.ds(CLUSTER_COUNT, CLUSTER_COUNT)] = halves(member)
        wide = product(high[...], both[...])
        total += product(low[...], both[:, pl.ds(0, CLUSTER_COUNT)])
        total += wide[:, :CLUSTER_COUNT] + wide[:, CLUSTER_COUNT:]
    tail = tail_rows(sizes)
    for block in range(8):
        out[member_at(block), pl.ds(0, points)] = total[block * points : (block + 1) * points]
        out[member_at(block), pl.ds(points, SIDE)] = tail


def summed(blocks):
    total = blocks[0]
    for block in range(1, 8):
        total += blocks[block]
    return total


def sum_kernel(blocks, out, spread):
    out[...] = summed(blocks)
    spread[...] = jnp.broadcast_to(out[...], spread.shape)


def own_kernel(blocks, own, out, part):
    points = own.shape[0]
    out[...] = summed(blocks)
    part[...] = jnp.sum(own[...] * out[pl.ds(0, points)], axis=0, keepdims=True)


def final_kernel(second, cohesion, out):
    points = out.shape[0]
    out[...] = log_softmax_energy(second[pl.ds(0, points)], second[pl.ds(points, 1)], cohesion[...])


PARAMS = pltpu.CompilerParams(vmem_limit_bytes=12 << 20)


def on_chip(kernel, name, shapes, inputs, scratch=()):
    vmem = pl.BlockSpec(memory_space=pltpu.VMEM)
    specs = [vmem] * len(inputs)
    shapes = [jax.ShapeDtypeStruct(*shape) for shape in shapes]
    return pl.pallas_call(
        kernel,
        out_shape=shapes,
        in_specs=specs,
        out_specs=[vmem] * len(shapes),
        scratch_shapes=scratch,
        compiler_params=PARAMS,
        name=name,
    )(*inputs)


def copies(x, count):
    return jnp.broadcast_to(x, (count, *x.shape))


def other_core(x):
    return lax.ppermute(x, "core", [(0, 1), (1, 0)])


def log_softmax_energy(attraction, counts, cohesion):
    energy = attraction / counts - cohesion / (2.0 * counts**2)
    logits = -energy / ANNEAL_TEMP_VALUE
    highest = jnp.max(logits, axis=1, keepdims=True)
    return logits - highest - jnp.log(jnp.sum(jnp.exp(logits - highest), axis=1, keepdims=True))


def shards(embedding, seed_cluster):
    points, width = embedding.shape
    lines, tall = points + SIDE, 8 * points
    outside, vmem = pl.BlockSpec(memory_space=pltpu.HBM), pl.BlockSpec(memory_space=pltpu.VMEM)
    block, spread = pl.pallas_call(
        prepare_kernel,
        out_shape=[jax.ShapeDtypeStruct((lines, width), jnp.float32), jax.ShapeDtypeStruct((8, lines, width), jnp.float32)],
        in_specs=[outside, outside],
        out_specs=[vmem, vmem],
        scratch_shapes=[pltpu.VMEM((1, points), jnp.int32), pltpu.SemaphoreType.DMA((2,))],
        name="prepare",
    )(embedding, seed_cluster.reshape(1, points))
    columns = exchange_columns(spread)
    columns, *rows = lax.optimization_barrier((columns, *row_peers(block)))
    kept = ((tall, tall), jnp.bfloat16)
    exchange = ((8, lines, CLUSTER_COUNT), jnp.float32)
    scratch = [
        pltpu.VMEM((tall, 3 * width), jnp.bfloat16),
        pltpu.VMEM((SIDE, tall), jnp.float32),
        pltpu.VMEM((tall, CLUSTER_COUNT), jnp.bfloat16),
    ]
    left, squares, own_high, own_low, weighted = on_chip(
        own_pair_kernel,
        "own_pairs",
        [((tall, 3 * width), jnp.bfloat16), ((tall, 1), jnp.float32), kept, kept, ((tall, CLUSTER_COUNT), jnp.float32)],
        [*rows, columns],
        scratch=scratch,
    )
    other_high, other_low, weighted = on_chip(
        other_pair_kernel,
        "other_pairs",
        [kept, kept, exchange],
        [*rows, other_core(columns), left, squares, weighted],
        scratch=scratch,
    )

    line = ((lines, CLUSTER_COUNT), jnp.float32)
    first, spread = on_chip(sum_kernel, "sum_spread", [line, exchange], [exchange_rows(weighted)])
    firsts = exchange_columns(spread)
    weighted, own = on_chip(
        member_kernel,
        "members",
        [exchange, ((points, CLUSTER_COUNT), jnp.float32)],
        [firsts, other_core(firsts), own_high, own_low, other_high, other_low, first],
        scratch=[pltpu.VMEM((tall, 2 * CLUSTER_COUNT), jnp.bfloat16)],
    )

    part = ((1, CLUSTER_COUNT), jnp.float32)
    second, part = on_chip(own_kernel, "own_sums", [line, part], [exchange_rows(weighted), own])
    parts = lax.all_to_all(copies(part, 128), EVERY, 0, 0, tiled=True)
    (out,) = on_chip(
        final_kernel,
        "final",
        [((points, CLUSTER_COUNT), jnp.float32)],
        [second, jnp.sum(parts, axis=0)],
    )
    return out


def solution(mesh):
    finer = Mesh(mesh.devices.reshape(SIZES), EVERY)
    return jax.shard_map(
        shards, mesh=finer, in_specs=(P(EVERY, None), P(EVERY)), out_specs=P(EVERY, None), check_vma=False
    )
```

```python
import functools
import itertools

import jax
import jax.numpy as jnp
from jax import lax
from jax.experimental import pallas as pl
from jax.experimental.pallas import tpu as pltpu
from jax.sharding import Mesh
from jax.sharding import PartitionSpec as P

CLUSTER_COUNT = 128
ANNEAL_TEMP_VALUE = 0.02
SIDE = 8

EVERY = ("y_lo", "z", "y_hi", "x", "core")
SIZES = (2, 4, 2, 4, 2)


def place(y_lo, z, y_hi, x, core):
    return (((y_lo * 4 + z) * 2 + y_hi) * 4 + x) * 2 + core


def column_groups():
    groups = []
    for pair, x, core in itertools.product(range(2), range(4), range(2)):
        groups.append([place(lo, z, lo ^ pair, x, core) for lo in range(2) for z in range(4)])
    return groups


COLUMN_GROUPS = column_groups()
ROW_ORDER = ((0, 0), (1, 2), (1, 3), (1, 1), (0, 2), (1, 0), (0, 3), (0, 1))


def exchange_rows(blocks):
    return lax.all_to_all(blocks, ("y_lo", "x"), 0, 0, tiled=True)


def exchange_columns(blocks):
    return lax.all_to_all(blocks, EVERY, 0, 0, axis_index_groups=COLUMN_GROUPS, tiled=True)


def moved(x, flip, step):
    pairs = []
    for lo, z, hi, at, core in itertools.product(*map(range, SIZES)):
        pairs.append((place(lo ^ flip, z, hi, (at + step) % 4, core), place(lo, z, hi, at, core)))
    return lax.ppermute(x, EVERY, pairs)


def row_peers(x):
    return [moved(x, flip, step) if flip or step else x for flip, step in ROW_ORDER]


def member_at(offset):
    y_lo, x = lax.axis_index("y_lo"), lax.axis_index("x")
    flip, step = ROW_ORDER[offset]
    return ((1 - y_lo) if flip else y_lo) * 4 + (x + step) % 4


def halves(x):
    high = x.astype(jnp.bfloat16)
    return high, (x - high.astype(jnp.float32)).astype(jnp.bfloat16)


def product(a, b):
    return jnp.dot(a, b, preferred_element_type=jnp.float32)


def seed_member(seeds):
    labels = lax.broadcasted_iota(jnp.int32, (CLUSTER_COUNT, seeds.shape[1]), 0).astype(jnp.float32)
    return 0.5 * (labels == seeds).astype(jnp.float32).T + 0.5 / CLUSTER_COUNT


def tail_rows(*lines):
    at = lax.broadcasted_iota(jnp.int32, (SIDE, CLUSTER_COUNT), 0)
    tail = jnp.zeros((SIDE, CLUSTER_COUNT), jnp.float32)
    for index, line in enumerate(lines):
        tail = jnp.where(at == index, line, tail)
    return tail


def prepare_kernel(embedding, seeds, block, spread, labels, arrived):
    points, width = embedding.shape
    body, end = pl.ds(0, points), pl.ds(points, SIDE)
    loads = [
        pltpu.make_async_copy(embedding, block.at[body], arrived.at[0]),
        pltpu.make_async_copy(seeds, labels, arrived.at[1]),
    ]
    for load in loads:
        load.start()
    for load in loads:
        load.wait()
    x = block[body]
    side = jnp.concatenate([labels[...].astype(jnp.float32), jnp.sum((x * x).T, axis=0, keepdims=True)], axis=1)
    side = jnp.broadcast_to(side, (SIDE, width))
    block[end] = side
    for copy in range(spread.shape[0]):
        spread[copy, body] = x
        spread[copy, end] = side


CHUNK = 256


def weigh(columns, left, squares, high_out, low_out, right, line, member):
    points, width = columns.shape[1] - SIDE, columns.shape[2]
    for block in range(8):
        at = pl.ds(block * points, points)
        high, low = halves(columns[block, pl.ds(0, points)])
        right[at, pl.ds(0, width)] = high
        right[at, pl.ds(width, width)] = low
        right[at, pl.ds(2 * width, width)] = high
        side = columns[block, pl.ds(points, 1)]
        line[:, at] = jnp.broadcast_to(side[:, points:], (SIDE, points))
        member[at] = seed_member(side[:, :points]).astype(jnp.bfloat16)
    for chunk in range(left.shape[0] // CHUNK):
        at = pl.ds(chunk * CHUNK, CHUNK)
        inner = lax.dot_general(left[at], right[...], (((1,), (1,)), ((), ())), preferred_element_type=jnp.float32)
        squared = inner + squares[at] + line[pl.ds(0, 1)]
        high, low = halves(squared * lax.rsqrt(squared))
        high_out[at] = high
        low_out[at] = low
    return product(high_out[...], member[...]) + product(low_out[...], member[...])


def own_pair_kernel(*refs):
    rows, (columns, left, squares, high_out, low_out, out, right, line, member) = refs[:8], refs[8:]
    points, width = rows[0].shape[0] - SIDE, rows[0].shape[1]
    for offset, block in enumerate(rows):
        x = block[pl.ds(0, points)]
        at = pl.ds(offset * points, points)
        squares[at] = jnp.sum(x * x, axis=1, keepdims=True) + 1.0
        high, low = halves(-2.0 * x)
        left[at, pl.ds(0, width)] = high
        left[at, pl.ds(width, width)] = high
        left[at, pl.ds(2 * width, width)] = low
    out[...] = weigh(columns, left, squares, high_out, low_out, right, line, member)


def other_pair_kernel(*refs):
    rows, (columns, left, squares, weighted, high_out, low_out, out, right, line, member) = refs[:8], refs[8:]
    points = rows[0].shape[0] - SIDE
    total = weighted[...] + weigh(columns, left, squares, high_out, low_out, right, line, member)
    cohesion = jnp.zeros((1, CLUSTER_COUNT), jnp.float32)
    for offset in range(8):
        part = total[offset * points : (offset + 1) * points]
        out[member_at(offset), pl.ds(0, points)] = part
        own = seed_member(rows[offset][pl.ds(points, 1)][:, :points])
        cohesion += jnp.sum(own * part, axis=0, keepdims=True)
    counts = jnp.sum(seed_member(rows[0][pl.ds(points, 1)][:, :points]), axis=0, keepdims=True)
    tail = tail_rows(cohesion, counts)
    for target in range(8):
        out[target, pl.ds(points, SIDE)] = tail


def member_kernel(own, other, own_high, own_low, other_high, other_low, first, out, own_member, both):
    points = own.shape[1] - SIDE
    sums = jnp.zeros((SIDE, CLUSTER_COUNT), jnp.float32)
    for block in range(8):
        sums += own[block, pl.ds(points, SIDE)] + other[block, pl.ds(points, SIDE)]
    cohesion, counts = sums[0:1], sums[1:2]
    own_member[...] = jnp.exp(log_softmax_energy(first[pl.ds(0, points)], counts, cohesion))
    sizes = jnp.zeros((1, CLUSTER_COUNT), jnp.float32)
    total = 0.0
    for source, high, low in ((own, own_high, own_low), (other, other_high, other_low)):
        for block in range(8):
            member = jnp.exp(log_softmax_energy(source[block, pl.ds(0, points)], counts, cohesion))
            sizes += jnp.sum(member, axis=0, keepdims=True)
            at = pl.ds(block * points, points)
            both[at, pl.ds(0, CLUSTER_COUNT)], both[at, pl.ds(CLUSTER_COUNT, CLUSTER_COUNT)] = halves(member)
        wide = product(high[...], both[...])
        total += product(low[...], both[:, pl.ds(0, CLUSTER_COUNT)])
        total += wide[:, :CLUSTER_COUNT] + wide[:, CLUSTER_COUNT:]
    tail = tail_rows(sizes)
    for block in range(8):
        out[member_at(block), pl.ds(0, points)] = total[block * points : (block + 1) * points]
        out[member_at(block), pl.ds(points, SIDE)] = tail


def summed(blocks):
    total = blocks[0]
    for block in range(1, 8):
        total += blocks[block]
    return total


def sum_kernel(blocks, out, spread):
    out[...] = summed(blocks)
    spread[...] = jnp.broadcast_to(out[...], spread.shape)


def own_kernel(blocks, own, out, part):
    points = own.shape[0]
    out[...] = summed(blocks)
    part[...] = jnp.sum(own[...] * out[pl.ds(0, points)], axis=0, keepdims=True)


def final_kernel(second, cohesion, out):
    points = out.shape[0]
    out[...] = log_softmax_energy(second[pl.ds(0, points)], second[pl.ds(points, 1)], cohesion[...])


PARAMS = pltpu.CompilerParams(vmem_limit_bytes=12 << 20)


def on_chip(kernel, name, shapes, inputs, scratch=()):
    vmem = pl.BlockSpec(memory_space=pltpu.VMEM)
    specs = [vmem] * len(inputs)
    shapes = [jax.ShapeDtypeStruct(*shape) for shape in shapes]
    return pl.pallas_call(
        kernel,
        out_shape=shapes,
        in_specs=specs,
        out_specs=[vmem] * len(shapes),
        scratch_shapes=scratch,
        compiler_params=PARAMS,
        name=name,
    )(*inputs)


def copies(x, count):
    return jnp.broadcast_to(x, (count, *x.shape))


def other_core(x):
    return lax.ppermute(x, "core", [(0, 1), (1, 0)])


def log_softmax_energy(attraction, counts, cohesion):
    energy = attraction / counts - cohesion / (2.0 * counts**2)
    logits = -energy / ANNEAL_TEMP_VALUE
    highest = jnp.max(logits, axis=1, keepdims=True)
    return logits - highest - jnp.log(jnp.sum(jnp.exp(logits - highest), axis=1, keepdims=True))


def shards(embedding, seed_cluster):
    points, width = embedding.shape
    lines, tall = points + SIDE, 8 * points
    outside, vmem = pl.BlockSpec(memory_space=pltpu.HBM), pl.BlockSpec(memory_space=pltpu.VMEM)
    block, spread = pl.pallas_call(
        prepare_kernel,
        out_shape=[jax.ShapeDtypeStruct((lines, width), jnp.float32), jax.ShapeDtypeStruct((8, lines, width), jnp.float32)],
        in_specs=[outside, outside],
        out_specs=[vmem, vmem],
        scratch_shapes=[pltpu.VMEM((1, points), jnp.int32), pltpu.SemaphoreType.DMA((2,))],
        name="prepare",
    )(embedding, seed_cluster.reshape(1, points))
    columns = exchange_columns(spread)
    columns, *rows = lax.optimization_barrier((columns, *row_peers(block)))
    kept = ((tall, tall), jnp.bfloat16)
    exchange = ((8, lines, CLUSTER_COUNT), jnp.float32)
    scratch = [
        pltpu.VMEM((tall, 3 * width), jnp.bfloat16),
        pltpu.VMEM((SIDE, tall), jnp.float32),
        pltpu.VMEM((tall, CLUSTER_COUNT), jnp.bfloat16),
    ]
    left, squares, own_high, own_low, weighted = on_chip(
        own_pair_kernel,
        "own_pairs",
        [((tall, 3 * width), jnp.bfloat16), ((tall, 1), jnp.float32), kept, kept, ((tall, CLUSTER_COUNT), jnp.float32)],
        [*rows, columns],
        scratch=scratch,
    )
    other_high, other_low, weighted = on_chip(
        other_pair_kernel,
        "other_pairs",
        [kept, kept, exchange],
        [*rows, other_core(columns), left, squares, weighted],
        scratch=scratch,
    )

    line = ((lines, CLUSTER_COUNT), jnp.float32)
    first, spread = on_chip(sum_kernel, "sum_spread", [line, exchange], [exchange_rows(weighted)])
    firsts = exchange_columns(spread)
    weighted, own = on_chip(
        member_kernel,
        "members",
        [exchange, ((points, CLUSTER_COUNT), jnp.float32)],
        [firsts, other_core(firsts), own_high, own_low, other_high, other_low, first],
        scratch=[pltpu.VMEM((tall, 2 * CLUSTER_COUNT), jnp.bfloat16)],
    )

    part = ((1, CLUSTER_COUNT), jnp.float32)
    second, part = on_chip(own_kernel, "own_sums", [line, part], [exchange_rows(weighted), own])
    parts = lax.all_to_all(copies(part, 128), EVERY, 0, 0, tiled=True)
    (out,) = on_chip(
        final_kernel,
        "final",
        [((points, CLUSTER_COUNT), jnp.float32)],
        [second, jnp.sum(parts, axis=0)],
    )
    return out


def solution(mesh):
    finer = Mesh(mesh.devices.reshape(SIZES), EVERY)
    return jax.shard_map(
        shards, mesh=finer, in_specs=(P(EVERY, None), P(EVERY)), out_specs=P(EVERY, None), check_vma=False
    )
```

```python
import functools
import itertools

import jax
import jax.numpy as jnp
from jax import lax
from jax.experimental import pallas as pl
from jax.experimental.pallas import tpu as pltpu
from jax.sharding import Mesh
from jax.sharding import PartitionSpec as P

CLUSTER_COUNT = 128
ANNEAL_TEMP_VALUE = 0.02
SIDE = 8

EVERY = ("y_lo", "z", "y_hi", "x", "core")
SIZES = (2, 4, 2, 4, 2)


def place(y_lo, z, y_hi, x, core):
    return (((y_lo * 4 + z) * 2 + y_hi) * 4 + x) * 2 + core


def column_groups():
    groups = []
    for pair, x, core in itertools.product(range(2), range(4), range(2)):
        groups.append([place(lo, z, lo ^ pair, x, core) for lo in range(2) for z in range(4)])
    return groups


COLUMN_GROUPS = column_groups()
ROW_ORDER = ((0, 0), (1, 0), (0, 2), (1, 3), (1, 1), (1, 2), (0, 3), (0, 1))


def exchange_rows(blocks):
    return lax.all_to_all(blocks, ("y_lo", "x"), 0, 0, tiled=True)


def exchange_columns(blocks):
    return lax.all_to_all(blocks, EVERY, 0, 0, axis_index_groups=COLUMN_GROUPS, tiled=True)


def moved(x, flip, step):
    pairs = []
    for lo, z, hi, at, core in itertools.product(*map(range, SIZES)):
        pairs.append((place(lo ^ flip, z, hi, (at + step) % 4, core), place(lo, z, hi, at, core)))
    return lax.ppermute(x, EVERY, pairs)


def row_peers(x):
    return [moved(x, flip, step) if flip or step else x for flip, step in ROW_ORDER]


def member_at(offset):
    y_lo, x = lax.axis_index("y_lo"), lax.axis_index("x")
    flip, step = ROW_ORDER[offset]
    return ((1 - y_lo) if flip else y_lo) * 4 + (x + step) % 4


def halves(x):
    high = x.astype(jnp.bfloat16)
    return high, (x - high.astype(jnp.float32)).astype(jnp.bfloat16)


def product(a, b):
    return jnp.dot(a, b, preferred_element_type=jnp.float32)


def seed_member(seeds):
    labels = lax.broadcasted_iota(jnp.int32, (CLUSTER_COUNT, seeds.shape[1]), 0).astype(jnp.float32)
    return 0.5 * (labels == seeds).astype(jnp.float32).T + 0.5 / CLUSTER_COUNT


def tail_rows(*lines):
    at = lax.broadcasted_iota(jnp.int32, (SIDE, CLUSTER_COUNT), 0)
    tail = jnp.zeros((SIDE, CLUSTER_COUNT), jnp.float32)
    for index, line in enumerate(lines):
        tail = jnp.where(at == index, line, tail)
    return tail


def prepare_kernel(embedding, seeds, block, spread, labels, arrived):
    points, width = embedding.shape
    body, end = pl.ds(0, points), pl.ds(points, SIDE)
    loads = [
        pltpu.make_async_copy(embedding, block.at[body], arrived.at[0]),
        pltpu.make_async_copy(seeds, labels, arrived.at[1]),
    ]
    for load in loads:
        load.start()
    for load in loads:
        load.wait()
    x = block[body]
    side = jnp.concatenate([labels[...].astype(jnp.float32), jnp.sum((x * x).T, axis=0, keepdims=True)], axis=1)
    side = jnp.broadcast_to(side, (SIDE, width))
    block[end] = side
    for copy in range(spread.shape[0]):
        spread[copy, body] = x
        spread[copy, end] = side


CHUNK = 256


def weigh(columns, left, squares, high_out, low_out, right, line, member):
    points, width = columns.shape[1] - SIDE, columns.shape[2]
    for block in range(8):
        at = pl.ds(block * points, points)
        high, low = halves(columns[block, pl.ds(0, points)])
        right[at, pl.ds(0, width)] = high
        right[at, pl.ds(width, width)] = low
        right[at, pl.ds(2 * width, width)] = high
        side = columns[block, pl.ds(points, 1)]
        line[:, at] = jnp.broadcast_to(side[:, points:], (SIDE, points))
        member[at] = seed_member(side[:, :points]).astype(jnp.bfloat16)
    for chunk in range(left.shape[0] // CHUNK):
        at = pl.ds(chunk * CHUNK, CHUNK)
        inner = lax.dot_general(left[at], right[...], (((1,), (1,)), ((), ())), preferred_element_type=jnp.float32)
        squared = inner + squares[at] + line[pl.ds(0, 1)]
        high, low = halves(squared * lax.rsqrt(squared))
        high_out[at] = high
        low_out[at] = low
    return product(high_out[...], member[...]) + product(low_out[...], member[...])


def own_pair_kernel(*refs):
    rows, (columns, left, squares, high_out, low_out, out, right, line, member) = refs[:8], refs[8:]
    points, width = rows[0].shape[0] - SIDE, rows[0].shape[1]
    for offset, block in enumerate(rows):
        x = block[pl.ds(0, points)]
        at = pl.ds(offset * points, points)
        squares[at] = jnp.sum(x * x, axis=1, keepdims=True) + 1.0
        high, low = halves(-2.0 * x)
        left[at, pl.ds(0, width)] = high
        left[at, pl.ds(width, width)] = high
        left[at, pl.ds(2 * width, width)] = low
    out[...] = weigh(columns, left, squares, high_out, low_out, right, line, member)


def other_pair_kernel(*refs):
    rows, (columns, left, squares, weighted, high_out, low_out, out, right, line, member) = refs[:8], refs[8:]
    points = rows[0].shape[0] - SIDE
    total = weighted[...] + weigh(columns, left, squares, high_out, low_out, right, line, member)
    cohesion = jnp.zeros((1, CLUSTER_COUNT), jnp.float32)
    for offset in range(8):
        part = total[offset * points : (offset + 1) * points]
        out[member_at(offset), pl.ds(0, points)] = part
        own = seed_member(rows[offset][pl.ds(points, 1)][:, :points])
        cohesion += jnp.sum(own * part, axis=0, keepdims=True)
    counts = jnp.sum(seed_member(rows[0][pl.ds(points, 1)][:, :points]), axis=0, keepdims=True)
    tail = tail_rows(cohesion, counts)
    for target in range(8):
        out[target, pl.ds(points, SIDE)] = tail


def member_kernel(own, other, own_high, own_low, other_high, other_low, first, out, own_member, both):
    points = own.shape[1] - SIDE
    sums = jnp.zeros((SIDE, CLUSTER_COUNT), jnp.float32)
    for block in range(8):
        sums += own[block, pl.ds(points, SIDE)] + other[block, pl.ds(points, SIDE)]
    cohesion, counts = sums[0:1], sums[1:2]
    own_member[...] = jnp.exp(log_softmax_energy(first[pl.ds(0, points)], counts, cohesion))
    sizes = jnp.zeros((1, CLUSTER_COUNT), jnp.float32)
    total = 0.0
    for source, high, low in ((own, own_high, own_low), (other, other_high, other_low)):
        for block in range(8):
            member = jnp.exp(log_softmax_energy(source[block, pl.ds(0, points)], counts, cohesion))
            sizes += jnp.sum(member, axis=0, keepdims=True)
            at = pl.ds(block * points, points)
            both[at, pl.ds(0, CLUSTER_COUNT)], both[at, pl.ds(CLUSTER_COUNT, CLUSTER_COUNT)] = halves(member)
        wide = product(high[...], both[...])
        total += product(low[...], both[:, pl.ds(0, CLUSTER_COUNT)])
        total += wide[:, :CLUSTER_COUNT] + wide[:, CLUSTER_COUNT:]
    tail = tail_rows(sizes)
    for block in range(8):
        out[member_at(block), pl.ds(0, points)] = total[block * points : (block + 1) * points]
        out[member_at(block), pl.ds(points, SIDE)] = tail


def summed(blocks):
    total = blocks[0]
    for block in range(1, 8):
        total += blocks[block]
    return total


def sum_kernel(blocks, out, spread):
    out[...] = summed(blocks)
    spread[...] = jnp.broadcast_to(out[...], spread.shape)


def own_kernel(blocks, own, out, part):
    points = own.shape[0]
    out[...] = summed(blocks)
    part[...] = jnp.sum(own[...] * out[pl.ds(0, points)], axis=0, keepdims=True)


def final_kernel(second, cohesion, out):
    points = out.shape[0]
    out[...] = log_softmax_energy(second[pl.ds(0, points)], second[pl.ds(points, 1)], cohesion[...])


PARAMS = pltpu.CompilerParams(vmem_limit_bytes=12 << 20)


def on_chip(kernel, name, shapes, inputs, scratch=()):
    vmem = pl.BlockSpec(memory_space=pltpu.VMEM)
    specs = [vmem] * len(inputs)
    shapes = [jax.ShapeDtypeStruct(*shape) for shape in shapes]
    return pl.pallas_call(
        kernel,
        out_shape=shapes,
        in_specs=specs,
        out_specs=[vmem] * len(shapes),
        scratch_shapes=scratch,
        compiler_params=PARAMS,
        name=name,
    )(*inputs)


def copies(x, count):
    return jnp.broadcast_to(x, (count, *x.shape))


def other_core(x):
    return lax.ppermute(x, "core", [(0, 1), (1, 0)])


def log_softmax_energy(attraction, counts, cohesion):
    energy = attraction / counts - cohesion / (2.0 * counts**2)
    logits = -energy / ANNEAL_TEMP_VALUE
    highest = jnp.max(logits, axis=1, keepdims=True)
    return logits - highest - jnp.log(jnp.sum(jnp.exp(logits - highest), axis=1, keepdims=True))


def shards(embedding, seed_cluster):
    points, width = embedding.shape
    lines, tall = points + SIDE, 8 * points
    outside, vmem = pl.BlockSpec(memory_space=pltpu.HBM), pl.BlockSpec(memory_space=pltpu.VMEM)
    block, spread = pl.pallas_call(
        prepare_kernel,
        out_shape=[jax.ShapeDtypeStruct((lines, width), jnp.float32), jax.ShapeDtypeStruct((8, lines, width), jnp.float32)],
        in_specs=[outside, outside],
        out_specs=[vmem, vmem],
        scratch_shapes=[pltpu.VMEM((1, points), jnp.int32), pltpu.SemaphoreType.DMA((2,))],
        name="prepare",
    )(embedding, seed_cluster.reshape(1, points))
    columns = exchange_columns(spread)
    columns, *rows = lax.optimization_barrier((columns, *row_peers(block)))
    kept = ((tall, tall), jnp.bfloat16)
    exchange = ((8, lines, CLUSTER_COUNT), jnp.float32)
    scratch = [
        pltpu.VMEM((tall, 3 * width), jnp.bfloat16),
        pltpu.VMEM((SIDE, tall), jnp.float32),
        pltpu.VMEM((tall, CLUSTER_COUNT), jnp.bfloat16),
    ]
    left, squares, own_high, own_low, weighted = on_chip(
        own_pair_kernel,
        "own_pairs",
        [((tall, 3 * width), jnp.bfloat16), ((tall, 1), jnp.float32), kept, kept, ((tall, CLUSTER_COUNT), jnp.float32)],
        [*rows, columns],
        scratch=scratch,
    )
    other_high, other_low, weighted = on_chip(
        other_pair_kernel,
        "other_pairs",
        [kept, kept, exchange],
        [*rows, other_core(columns), left, squares, weighted],
        scratch=scratch,
    )

    line = ((lines, CLUSTER_COUNT), jnp.float32)
    first, spread = on_chip(sum_kernel, "sum_spread", [line, exchange], [exchange_rows(weighted)])
    firsts = exchange_columns(spread)
    weighted, own = on_chip(
        member_kernel,
        "members",
        [exchange, ((points, CLUSTER_COUNT), jnp.float32)],
        [firsts, other_core(firsts), own_high, own_low, other_high, other_low, first],
        scratch=[pltpu.VMEM((tall, 2 * CLUSTER_COUNT), jnp.bfloat16)],
    )

    part = ((1, CLUSTER_COUNT), jnp.float32)
    second, part = on_chip(own_kernel, "own_sums", [line, part], [exchange_rows(weighted), own])
    parts = lax.all_to_all(copies(part, 128), EVERY, 0, 0, tiled=True)
    (out,) = on_chip(
        final_kernel,
        "final",
        [((points, CLUSTER_COUNT), jnp.float32)],
        [second, jnp.sum(parts, axis=0)],
    )
    return out


def solution(mesh):
    finer = Mesh(mesh.devices.reshape(SIZES), EVERY)
    return jax.shard_map(
        shards, mesh=finer, in_specs=(P(EVERY, None), P(EVERY)), out_specs=P(EVERY, None), check_vma=False
    )
```

```python
import functools
import itertools

import jax
import jax.numpy as jnp
from jax import lax
from jax.experimental import pallas as pl
from jax.experimental.pallas import tpu as pltpu
from jax.sharding import Mesh
from jax.sharding import PartitionSpec as P

CLUSTER_COUNT = 128
ANNEAL_TEMP_VALUE = 0.02
SIDE = 8

EVERY = ("y_lo", "z", "y_hi", "x", "core")
SIZES = (2, 4, 2, 4, 2)


def place(y_lo, z, y_hi, x, core):
    return (((y_lo * 4 + z) * 2 + y_hi) * 4 + x) * 2 + core


def column_groups():
    groups = []
    for pair, x, core in itertools.product(range(2), range(4), range(2)):
        groups.append([place(lo, z, lo ^ pair, x, core) for lo in range(2) for z in range(4)])
    return groups


COLUMN_GROUPS = column_groups()
ROW_ORDER = ((0, 0), (1, 2), (1, 3), (1, 1), (0, 2), (0, 3), (0, 1), (1, 0))


def exchange_rows(blocks):
    return lax.all_to_all(blocks, ("y_lo", "x"), 0, 0, tiled=True)


def exchange_columns(blocks):
    return lax.all_to_all(blocks, EVERY, 0, 0, axis_index_groups=COLUMN_GROUPS, tiled=True)


def moved(x, flip, step):
    pairs = []
    for lo, z, hi, at, core in itertools.product(*map(range, SIZES)):
        pairs.append((place(lo ^ flip, z, hi, (at + step) % 4, core), place(lo, z, hi, at, core)))
    return lax.ppermute(x, EVERY, pairs)


def row_peers(x):
    return [moved(x, flip, step) if flip or step else x for flip, step in ROW_ORDER]


def member_at(offset):
    y_lo, x = lax.axis_index("y_lo"), lax.axis_index("x")
    flip, step = ROW_ORDER[offset]
    return ((1 - y_lo) if flip else y_lo) * 4 + (x + step) % 4


def halves(x):
    high = x.astype(jnp.bfloat16)
    return high, (x - high.astype(jnp.float32)).astype(jnp.bfloat16)


def product(a, b):
    return jnp.dot(a, b, preferred_element_type=jnp.float32)


def seed_member(seeds):
    labels = lax.broadcasted_iota(jnp.int32, (CLUSTER_COUNT, seeds.shape[1]), 0).astype(jnp.float32)
    return 0.5 * (labels == seeds).astype(jnp.float32).T + 0.5 / CLUSTER_COUNT


def tail_rows(*lines):
    at = lax.broadcasted_iota(jnp.int32, (SIDE, CLUSTER_COUNT), 0)
    tail = jnp.zeros((SIDE, CLUSTER_COUNT), jnp.float32)
    for index, line in enumerate(lines):
        tail = jnp.where(at == index, line, tail)
    return tail


def prepare_kernel(embedding, seeds, block, spread, labels, arrived):
    points, width = embedding.shape
    body, end = pl.ds(0, points), pl.ds(points, SIDE)
    loads = [
        pltpu.make_async_copy(embedding, block.at[body], arrived.at[0]),
        pltpu.make_async_copy(seeds, labels, arrived.at[1]),
    ]
    for load in loads:
        load.start()
    for load in loads:
        load.wait()
    x = block[body]
    side = jnp.concatenate([labels[...].astype(jnp.float32), jnp.sum((x * x).T, axis=0, keepdims=True)], axis=1)
    side = jnp.broadcast_to(side, (SIDE, width))
    block[end] = side
    for copy in range(spread.shape[0]):
        spread[copy, body] = x
        spread[copy, end] = side


CHUNK = 256


def set_columns(columns, right, line, member):
    points, width = columns.shape[1] - SIDE, columns.shape[2]
    for block in range(8):
        at = pl.ds(block * points, points)
        high, low = halves(columns[block, pl.ds(0, points)])
        right[at, pl.ds(0, width)] = high
        right[at, pl.ds(width, width)] = low
        right[at, pl.ds(2 * width, width)] = high
        side = columns[block, pl.ds(points, 1)]
        line[:, at] = jnp.broadcast_to(side[:, points:], (SIDE, points))
        member[at] = seed_member(side[:, :points]).astype(jnp.bfloat16)


def left_rows(x):
    high, low = halves(-2.0 * x)
    return jnp.concatenate([high, high, low], axis=1), jnp.sum(x * x, axis=1, keepdims=True) + 1.0


def distances(left, square, right, line, high_out, low_out, at):
    inner = lax.dot_general(left, right[...], (((1,), (1,)), ((), ())), preferred_element_type=jnp.float32)
    squared = inner + square + line[pl.ds(0, 1)]
    high_out[at], low_out[at] = halves(squared * lax.rsqrt(squared))


def weights(high, low, member, at):
    return product(high[at], member[...]) + product(low[at], member[...])


EARLY = 768


def own_pair_kernel(*refs):
    rows, (columns, left, squares, right, line, member, high, low, out) = refs[:6], refs[6:]
    points = rows[0].shape[0] - SIDE
    set_columns(columns, right, line, member)
    for offset, block in enumerate(rows):
        at = pl.ds(offset * points, points)
        left[at], squares[at] = left_rows(block[pl.ds(0, points)])
    for start in range(0, EARLY, CHUNK):
        at = pl.ds(start, CHUNK)
        distances(left[at], squares[at], right, line, high, low, at)
    out[...] = weights(high, low, member, pl.ds(0, EARLY))


def other_pair_kernel(columns, left, squares, weighted, right, line, member, high, low, out):
    set_columns(columns, right, line, member)
    for start in range(0, EARLY, CHUNK):
        at = pl.ds(start, CHUNK)
        distances(left[at], squares[at], right, line, high, low, at)
    out[...] = weighted[...] + weights(high, low, member, pl.ds(0, EARLY))


def late_pair_kernel(*refs):
    rows, sides, weighted, refs = refs[:8], (refs[8:11], refs[11:14]), refs[14], refs[19:]
    (*kept, out) = refs
    points = rows[0].shape[0] - SIDE
    at = pl.ds(EARLY, CHUNK)
    left, square = left_rows(jnp.concatenate([block[pl.ds(0, points)] for block in rows[6:]], axis=0))
    late = 0.0
    for half, (right, line, member) in enumerate(sides):
        high, low = kept[2 * half : 2 * half + 2]
        distances(left, square, right, line, high, low, at)
        late += weights(high, low, member, at)
    cohesion = jnp.zeros((1, CLUSTER_COUNT), jnp.float32)
    for offset in range(8):
        start = offset * points
        part = weighted[pl.ds(start, points)] if start < EARLY else late[start - EARLY : start - EARLY + points]
        out[member_at(offset), pl.ds(0, points)] = part
        own = seed_member(rows[offset][pl.ds(points, 1)][:, :points])
        cohesion += jnp.sum(own * part, axis=0, keepdims=True)
    counts = jnp.sum(seed_member(rows[0][pl.ds(points, 1)][:, :points]), axis=0, keepdims=True)
    tail = tail_rows(cohesion, counts)
    for target in range(8):
        out[target, pl.ds(points, SIDE)] = tail


def member_kernel(own, other, own_high, own_low, other_high, other_low, first, out, own_member, both):
    points = own.shape[1] - SIDE
    sums = jnp.zeros((SIDE, CLUSTER_COUNT), jnp.float32)
    for block in range(8):
        sums += own[block, pl.ds(points, SIDE)] + other[block, pl.ds(points, SIDE)]
    cohesion, counts = sums[0:1], sums[1:2]
    own_member[...] = jnp.exp(log_softmax_energy(first[pl.ds(0, points)], counts, cohesion))
    sizes = jnp.zeros((1, CLUSTER_COUNT), jnp.float32)
    total = 0.0
    for source, high, low in ((own, own_high, own_low), (other, other_high, other_low)):
        for block in range(8):
            member = jnp.exp(log_softmax_energy(source[block, pl.ds(0, points)], counts, cohesion))
            sizes += jnp.sum(member, axis=0, keepdims=True)
            at = pl.ds(block * points, points)
            both[at, pl.ds(0, CLUSTER_COUNT)], both[at, pl.ds(CLUSTER_COUNT, CLUSTER_COUNT)] = halves(member)
        wide = product(high[...], both[...])
        total += product(low[...], both[:, pl.ds(0, CLUSTER_COUNT)])
        total += wide[:, :CLUSTER_COUNT] + wide[:, CLUSTER_COUNT:]
    tail = tail_rows(sizes)
    for block in range(8):
        out[member_at(block), pl.ds(0, points)] = total[block * points : (block + 1) * points]
        out[member_at(block), pl.ds(points, SIDE)] = tail


def summed(blocks):
    total = blocks[0]
    for block in range(1, 8):
        total += blocks[block]
    return total


def sum_kernel(blocks, out, spread):
    out[...] = summed(blocks)
    spread[...] = jnp.broadcast_to(out[...], spread.shape)


def own_kernel(blocks, own, out, part):
    points = own.shape[0]
    out[...] = summed(blocks)
    part[...] = jnp.sum(own[...] * out[pl.ds(0, points)], axis=0, keepdims=True)


def final_kernel(second, cohesion, out):
    points = out.shape[0]
    out[...] = log_softmax_energy(second[pl.ds(0, points)], second[pl.ds(points, 1)], cohesion[...])


PARAMS = pltpu.CompilerParams(vmem_limit_bytes=12 << 20)


def on_chip(kernel, name, shapes, inputs, scratch=(), aliases={}):
    vmem = pl.BlockSpec(memory_space=pltpu.VMEM)
    specs = [vmem] * len(inputs)
    shapes = [jax.ShapeDtypeStruct(*shape) for shape in shapes]
    return pl.pallas_call(
        kernel,
        out_shape=shapes,
        in_specs=specs,
        out_specs=[vmem] * len(shapes),
        scratch_shapes=scratch,
        input_output_aliases=aliases,
        compiler_params=PARAMS,
        name=name,
    )(*inputs)


def copies(x, count):
    return jnp.broadcast_to(x, (count, *x.shape))


def other_core(x):
    return lax.ppermute(x, "core", [(0, 1), (1, 0)])


def log_softmax_energy(attraction, counts, cohesion):
    energy = attraction / counts - cohesion / (2.0 * counts**2)
    logits = -energy / ANNEAL_TEMP_VALUE
    highest = jnp.max(logits, axis=1, keepdims=True)
    return logits - highest - jnp.log(jnp.sum(jnp.exp(logits - highest), axis=1, keepdims=True))


def shards(embedding, seed_cluster):
    points, width = embedding.shape
    lines, tall = points + SIDE, 8 * points
    outside, vmem = pl.BlockSpec(memory_space=pltpu.HBM), pl.BlockSpec(memory_space=pltpu.VMEM)
    block, spread = pl.pallas_call(
        prepare_kernel,
        out_shape=[jax.ShapeDtypeStruct((lines, width), jnp.float32), jax.ShapeDtypeStruct((8, lines, width), jnp.float32)],
        in_specs=[outside, outside],
        out_specs=[vmem, vmem],
        scratch_shapes=[pltpu.VMEM((1, points), jnp.int32), pltpu.SemaphoreType.DMA((2,))],
        name="prepare",
    )(embedding, seed_cluster.reshape(1, points))
    columns = exchange_columns(spread)
    rows = row_peers(block)
    columns, *rows[:7] = lax.optimization_barrier((columns, *rows[:7]))
    kept = ((tall, tall), jnp.bfloat16)
    exchange = ((8, lines, CLUSTER_COUNT), jnp.float32)
    sides = [((tall, 3 * width), jnp.bfloat16), ((SIDE, tall), jnp.float32), ((tall, CLUSTER_COUNT), jnp.bfloat16)]
    lefts = [((EARLY, 3 * width), jnp.bfloat16), ((EARLY, 1), jnp.float32)]
    early = ((EARLY, CLUSTER_COUNT), jnp.float32)
    left, squares, *own_sides, own_high, own_low, weighted = on_chip(
        own_pair_kernel, "own_pairs", [*lefts, *sides, kept, kept, early], [*rows[:6], columns]
    )
    *other_sides, other_high, other_low, weighted = on_chip(
        other_pair_kernel,
        "other_pairs",
        [*sides, kept, kept, early],
        [other_core(columns), left, squares, weighted],
    )
    own_high, own_low, other_high, other_low, weighted = on_chip(
        late_pair_kernel,
        "late_pairs",
        [kept] * 4 + [exchange],
        [*rows, *own_sides, *other_sides, weighted, own_high, own_low, other_high, other_low],
        aliases={15: 0, 16: 1, 17: 2, 18: 3},
    )

    line = ((lines, CLUSTER_COUNT), jnp.float32)
    first, spread = on_chip(sum_kernel, "sum_spread", [line, exchange], [exchange_rows(weighted)])
    firsts = exchange_columns(spread)
    weighted, own = on_chip(
        member_kernel,
        "members",
        [exchange, ((points, CLUSTER_COUNT), jnp.float32)],
        [firsts, other_core(firsts), own_high, own_low, other_high, other_low, first],
        scratch=[pltpu.VMEM((tall, 2 * CLUSTER_COUNT), jnp.bfloat16)],
    )

    part = ((1, CLUSTER_COUNT), jnp.float32)
    second, part = on_chip(own_kernel, "own_sums", [line, part], [exchange_rows(weighted), own])
    parts = lax.all_to_all(copies(part, 128), EVERY, 0, 0, tiled=True)
    (out,) = on_chip(
        final_kernel,
        "final",
        [((points, CLUSTER_COUNT), jnp.float32)],
        [second, jnp.sum(parts, axis=0)],
    )
    return out


def solution(mesh):
    finer = Mesh(mesh.devices.reshape(SIZES), EVERY)
    return jax.shard_map(
        shards, mesh=finer, in_specs=(P(EVERY, None), P(EVERY)), out_specs=P(EVERY, None), check_vma=False
    )
```

```python
import functools
import itertools

import jax
import jax.numpy as jnp
from jax import lax
from jax.experimental import pallas as pl
from jax.experimental.pallas import tpu as pltpu
from jax.sharding import Mesh
from jax.sharding import PartitionSpec as P

CLUSTER_COUNT = 128
ANNEAL_TEMP_VALUE = 0.02
SIDE = 8

EVERY = ("y_lo", "z", "y_hi", "x", "core")
SIZES = (2, 4, 2, 4, 2)


def place(y_lo, z, y_hi, x, core):
    return (((y_lo * 4 + z) * 2 + y_hi) * 4 + x) * 2 + core


def column_groups():
    groups = []
    for pair, x, core in itertools.product(range(2), range(4), range(2)):
        groups.append([place(lo, z, lo ^ pair, x, core) for lo in range(2) for z in range(4)])
    return groups


COLUMN_GROUPS = column_groups()
ROW_ORDER = ((0, 0), (1, 2), (1, 3), (1, 1), (0, 2), (0, 3), (0, 1), (1, 0))


def exchange_rows(blocks):
    return lax.all_to_all(blocks, ("y_lo", "x"), 0, 0, tiled=True)


def exchange_columns(blocks):
    return lax.all_to_all(blocks, EVERY, 0, 0, axis_index_groups=COLUMN_GROUPS, tiled=True)


def moved(x, flip, step):
    pairs = []
    for lo, z, hi, at, core in itertools.product(*map(range, SIZES)):
        pairs.append((place(lo ^ flip, z, hi, (at + step) % 4, core), place(lo, z, hi, at, core)))
    return lax.ppermute(x, EVERY, pairs)


def row_peers(x):
    return [moved(x, flip, step) if flip or step else x for flip, step in ROW_ORDER]


def member_at(offset):
    y_lo, x = lax.axis_index("y_lo"), lax.axis_index("x")
    flip, step = ROW_ORDER[offset]
    return ((1 - y_lo) if flip else y_lo) * 4 + (x + step) % 4


def halves(x):
    high = x.astype(jnp.bfloat16)
    return high, (x - high.astype(jnp.float32)).astype(jnp.bfloat16)


def product(a, b):
    return jnp.dot(a, b, preferred_element_type=jnp.float32)


def seed_member(seeds):
    labels = lax.broadcasted_iota(jnp.int32, (CLUSTER_COUNT, seeds.shape[1]), 0).astype(jnp.float32)
    return 0.5 * (labels == seeds).astype(jnp.float32).T + 0.5 / CLUSTER_COUNT


def tail_rows(*lines):
    at = lax.broadcasted_iota(jnp.int32, (SIDE, CLUSTER_COUNT), 0)
    tail = jnp.zeros((SIDE, CLUSTER_COUNT), jnp.float32)
    for index, line in enumerate(lines):
        tail = jnp.where(at == index, line, tail)
    return tail


def prepare_kernel(embedding, seeds, block, spread, labels, arrived):
    points, width = embedding.shape
    body, end = pl.ds(0, points), pl.ds(points, SIDE)
    loads = [
        pltpu.make_async_copy(embedding, block.at[body], arrived.at[0]),
        pltpu.make_async_copy(seeds, labels, arrived.at[1]),
    ]
    for load in loads:
        load.start()
    for load in loads:
        load.wait()
    x = block[body]
    side = jnp.concatenate([labels[...].astype(jnp.float32), jnp.sum((x * x).T, axis=0, keepdims=True)], axis=1)
    side = jnp.broadcast_to(side, (SIDE, width))
    block[end] = side
    for copy in range(spread.shape[0]):
        spread[copy, body] = x
        spread[copy, end] = side


CHUNK = 256


def set_columns(columns, right, line, member):
    points, width = columns.shape[1] - SIDE, columns.shape[2]
    for block in range(8):
        at = pl.ds(block * points, points)
        high, low = halves(columns[block, pl.ds(0, points)])
        right[at, pl.ds(0, width)] = high
        right[at, pl.ds(width, width)] = low
        right[at, pl.ds(2 * width, width)] = high
        side = columns[block, pl.ds(points, 1)]
        line[:, at] = jnp.broadcast_to(side[:, points:], (SIDE, points))
        member[at] = seed_member(side[:, :points]).astype(jnp.bfloat16)


def left_rows(x):
    high, low = halves(-2.0 * x)
    return jnp.concatenate([high, high, low], axis=1), jnp.sum(x * x, axis=1, keepdims=True) + 1.0


def distances(left, square, right, line, high_out, low_out, at):
    inner = lax.dot_general(left, right[...], (((1,), (1,)), ((), ())), preferred_element_type=jnp.float32)
    squared = inner + square + line[pl.ds(0, 1)]
    high_out[at], low_out[at] = halves(squared * lax.rsqrt(squared))


def weights(high, low, member, at):
    return product(high[at], member[...]) + product(low[at], member[...])


EARLY = 768


def own_pair_kernel(*refs):
    rows, (columns, left, squares, right, line, member, high, low, out) = refs[:6], refs[6:]
    points = rows[0].shape[0] - SIDE
    set_columns(columns, right, line, member)
    for offset, block in enumerate(rows):
        at = pl.ds(offset * points, points)
        left[at], squares[at] = left_rows(block[pl.ds(0, points)])
    for start in range(0, EARLY, CHUNK):
        at = pl.ds(start, CHUNK)
        distances(left[at], squares[at], right, line, high, low, at)
    out[...] = weights(high, low, member, pl.ds(0, EARLY))


def other_pair_kernel(columns, left, squares, weighted, right, line, member, high, low, out):
    set_columns(columns, right, line, member)
    for start in range(0, EARLY, CHUNK):
        at = pl.ds(start, CHUNK)
        distances(left[at], squares[at], right, line, high, low, at)
    out[...] = weighted[...] + weights(high, low, member, pl.ds(0, EARLY))


def late_pair_kernel(*refs):
    rows, sides, weighted, refs = refs[:8], (refs[8:11], refs[11:14]), refs[14], refs[19:]
    (*kept, out) = refs
    points = rows[0].shape[0] - SIDE
    at = pl.ds(EARLY, CHUNK)
    left, square = left_rows(jnp.concatenate([block[pl.ds(0, points)] for block in rows[6:]], axis=0))
    late = 0.0
    for half, (right, line, member) in enumerate(sides):
        high, low = kept[2 * half : 2 * half + 2]
        distances(left, square, right, line, high, low, at)
        late += weights(high, low, member, at)
    cohesion = jnp.zeros((1, CLUSTER_COUNT), jnp.float32)
    for offset in range(8):
        start = offset * points
        part = weighted[pl.ds(start, points)] if start < EARLY else late[start - EARLY : start - EARLY + points]
        out[member_at(offset), pl.ds(0, points)] = part
        own = seed_member(rows[offset][pl.ds(points, 1)][:, :points])
        cohesion += jnp.sum(own * part, axis=0, keepdims=True)
    counts = jnp.sum(seed_member(rows[0][pl.ds(points, 1)][:, :points]), axis=0, keepdims=True)
    tail = tail_rows(cohesion, counts)
    for target in range(8):
        out[target, pl.ds(points, SIDE)] = tail


def member_kernel(own, other, own_high, own_low, other_high, other_low, first, out, own_member, both):
    points = own.shape[1] - SIDE
    sums = jnp.zeros((SIDE, CLUSTER_COUNT), jnp.float32)
    for block in range(8):
        sums += own[block, pl.ds(points, SIDE)] + other[block, pl.ds(points, SIDE)]
    cohesion, counts = sums[0:1], sums[1:2]
    own_member[...] = jnp.exp(log_softmax_energy(first[pl.ds(0, points)], counts, cohesion))
    sizes = jnp.zeros((1, CLUSTER_COUNT), jnp.float32)
    total = 0.0
    for source, high, low in ((own, own_high, own_low), (other, other_high, other_low)):
        for block in range(8):
            member = jnp.exp(log_softmax_energy(source[block, pl.ds(0, points)], counts, cohesion))
            sizes += jnp.sum(member, axis=0, keepdims=True)
            at = pl.ds(block * points, points)
            both[at, pl.ds(0, CLUSTER_COUNT)], both[at, pl.ds(CLUSTER_COUNT, CLUSTER_COUNT)] = halves(member)
        wide = product(high[...], both[...])
        total += product(low[...], both[:, pl.ds(0, CLUSTER_COUNT)])
        total += wide[:, :CLUSTER_COUNT] + wide[:, CLUSTER_COUNT:]
    tail = tail_rows(sizes)
    for block in range(8):
        out[member_at(block), pl.ds(0, points)] = total[block * points : (block + 1) * points]
        out[member_at(block), pl.ds(points, SIDE)] = tail


def summed(blocks):
    total = blocks[0]
    for block in range(1, 8):
        total += blocks[block]
    return total


def sum_kernel(blocks, out, spread):
    out[...] = summed(blocks)
    spread[...] = jnp.broadcast_to(out[...], spread.shape)


def own_kernel(blocks, own, out, part):
    points = own.shape[0]
    out[...] = summed(blocks)
    part[...] = jnp.sum(own[...] * out[pl.ds(0, points)], axis=0, keepdims=True)


def final_kernel(second, cohesion, out):
    points = out.shape[0]
    out[...] = log_softmax_energy(second[pl.ds(0, points)], second[pl.ds(points, 1)], cohesion[...])


PARAMS = pltpu.CompilerParams(vmem_limit_bytes=12 << 20)


def on_chip(kernel, name, shapes, inputs, scratch=(), aliases={}):
    vmem = pl.BlockSpec(memory_space=pltpu.VMEM)
    specs = [vmem] * len(inputs)
    shapes = [jax.ShapeDtypeStruct(*shape) for shape in shapes]
    return pl.pallas_call(
        kernel,
        out_shape=shapes,
        in_specs=specs,
        out_specs=[vmem] * len(shapes),
        scratch_shapes=scratch,
        input_output_aliases=aliases,
        compiler_params=PARAMS,
        name=name,
    )(*inputs)


def copies(x, count):
    return jnp.broadcast_to(x, (count, *x.shape))


def other_core(x):
    return lax.ppermute(x, "core", [(0, 1), (1, 0)])


def log_softmax_energy(attraction, counts, cohesion):
    energy = attraction / counts - cohesion / (2.0 * counts**2)
    logits = -energy / ANNEAL_TEMP_VALUE
    highest = jnp.max(logits, axis=1, keepdims=True)
    return logits - highest - jnp.log(jnp.sum(jnp.exp(logits - highest), axis=1, keepdims=True))


def shards(embedding, seed_cluster):
    points, width = embedding.shape
    lines, tall = points + SIDE, 8 * points
    outside, vmem = pl.BlockSpec(memory_space=pltpu.HBM), pl.BlockSpec(memory_space=pltpu.VMEM)
    block, spread = pl.pallas_call(
        prepare_kernel,
        out_shape=[jax.ShapeDtypeStruct((lines, width), jnp.float32), jax.ShapeDtypeStruct((8, lines, width), jnp.float32)],
        in_specs=[outside, outside],
        out_specs=[vmem, vmem],
        scratch_shapes=[pltpu.VMEM((1, points), jnp.int32), pltpu.SemaphoreType.DMA((2,))],
        name="prepare",
    )(embedding, seed_cluster.reshape(1, points))
    columns = exchange_columns(spread)
    rows = row_peers(block)
    columns, *rows[:6] = lax.optimization_barrier((columns, *rows[:6]))
    kept = ((tall, tall), jnp.bfloat16)
    exchange = ((8, lines, CLUSTER_COUNT), jnp.float32)
    sides = [((tall, 3 * width), jnp.bfloat16), ((SIDE, tall), jnp.float32), ((tall, CLUSTER_COUNT), jnp.bfloat16)]
    lefts = [((EARLY, 3 * width), jnp.bfloat16), ((EARLY, 1), jnp.float32)]
    early = ((EARLY, CLUSTER_COUNT), jnp.float32)
    left, squares, *own_sides, own_high, own_low, weighted = on_chip(
        own_pair_kernel, "own_pairs", [*lefts, *sides, kept, kept, early], [*rows[:6], columns]
    )
    *other_sides, other_high, other_low, weighted = on_chip(
        other_pair_kernel,
        "other_pairs",
        [*sides, kept, kept, early],
        [other_core(columns), left, squares, weighted],
    )
    own_high, own_low, other_high, other_low, weighted = on_chip(
        late_pair_kernel,
        "late_pairs",
        [kept] * 4 + [exchange],
        [*rows, *own_sides, *other_sides, weighted, own_high, own_low, other_high, other_low],
        aliases={15: 0, 16: 1, 17: 2, 18: 3},
    )

    line = ((lines, CLUSTER_COUNT), jnp.float32)
    first, spread = on_chip(sum_kernel, "sum_spread", [line, exchange], [exchange_rows(weighted)])
    firsts = exchange_columns(spread)
    weighted, own = on_chip(
        member_kernel,
        "members",
        [exchange, ((points, CLUSTER_COUNT), jnp.float32)],
        [firsts, other_core(firsts), own_high, own_low, other_high, other_low, first],
        scratch=[pltpu.VMEM((tall, 2 * CLUSTER_COUNT), jnp.bfloat16)],
    )

    part = ((1, CLUSTER_COUNT), jnp.float32)
    second, part = on_chip(own_kernel, "own_sums", [line, part], [exchange_rows(weighted), own])
    parts = lax.all_to_all(copies(part, 128), EVERY, 0, 0, tiled=True)
    (out,) = on_chip(
        final_kernel,
        "final",
        [((points, CLUSTER_COUNT), jnp.float32)],
        [second, jnp.sum(parts, axis=0)],
    )
    return out


def solution(mesh):
    finer = Mesh(mesh.devices.reshape(SIZES), EVERY)
    return jax.shard_map(
        shards, mesh=finer, in_specs=(P(EVERY, None), P(EVERY)), out_specs=P(EVERY, None), check_vma=False
    )
```

```python
import functools
import itertools

import jax
import jax.numpy as jnp
from jax import lax
from jax.experimental import pallas as pl
from jax.experimental.pallas import tpu as pltpu
from jax.sharding import Mesh
from jax.sharding import PartitionSpec as P

CLUSTER_COUNT = 128
ANNEAL_TEMP_VALUE = 0.02
SIDE = 8

EVERY = ("y_lo", "z", "y_hi", "x", "core")
SIZES = (2, 4, 2, 4, 2)


def place(y_lo, z, y_hi, x, core):
    return (((y_lo * 4 + z) * 2 + y_hi) * 4 + x) * 2 + core


def column_groups():
    groups = []
    for pair, x, core in itertools.product(range(2), range(4), range(2)):
        groups.append([place(lo, z, lo ^ pair, x, core) for lo in range(2) for z in range(4)])
    return groups


COLUMN_GROUPS = column_groups()
ROW_ORDER = ((0, 0), (0, 3), (0, 2), (1, 1), (1, 3), (1, 2), (0, 1), (1, 0))


def exchange_rows(blocks):
    return lax.all_to_all(blocks, ("y_lo", "x"), 0, 0, tiled=True)


def exchange_columns(blocks):
    return lax.all_to_all(blocks, EVERY, 0, 0, axis_index_groups=COLUMN_GROUPS, tiled=True)


def moved(x, flip, step):
    pairs = []
    for lo, z, hi, at, core in itertools.product(*map(range, SIZES)):
        pairs.append((place(lo ^ flip, z, hi, (at + step) % 4, core), place(lo, z, hi, at, core)))
    return lax.ppermute(x, EVERY, pairs)


def row_peers(x):
    return [moved(x, flip, step) if flip or step else x for flip, step in ROW_ORDER]


def member_at(offset):
    y_lo, x = lax.axis_index("y_lo"), lax.axis_index("x")
    flip, step = ROW_ORDER[offset]
    return ((1 - y_lo) if flip else y_lo) * 4 + (x + step) % 4


def halves(x):
    high = x.astype(jnp.bfloat16)
    return high, (x - high.astype(jnp.float32)).astype(jnp.bfloat16)


def product(a, b):
    return jnp.dot(a, b, preferred_element_type=jnp.float32)


def seed_member(seeds):
    labels = lax.broadcasted_iota(jnp.int32, (CLUSTER_COUNT, seeds.shape[1]), 0).astype(jnp.float32)
    return 0.5 * (labels == seeds).astype(jnp.float32).T + 0.5 / CLUSTER_COUNT


def tail_rows(*lines):
    at = lax.broadcasted_iota(jnp.int32, (SIDE, CLUSTER_COUNT), 0)
    tail = jnp.zeros((SIDE, CLUSTER_COUNT), jnp.float32)
    for index, line in enumerate(lines):
        tail = jnp.where(at == index, line, tail)
    return tail


def prepare_kernel(embedding, seeds, block, spread, labels, arrived):
    points, width = embedding.shape
    body, end = pl.ds(0, points), pl.ds(points, SIDE)
    loads = [
        pltpu.make_async_copy(embedding, block.at[body], arrived.at[0]),
        pltpu.make_async_copy(seeds, labels, arrived.at[1]),
    ]
    for load in loads:
        load.start()
    for load in loads:
        load.wait()
    x = block[body]
    side = jnp.concatenate([labels[...].astype(jnp.float32), jnp.sum((x * x).T, axis=0, keepdims=True)], axis=1)
    side = jnp.broadcast_to(side, (SIDE, width))
    block[end] = side
    for copy in range(spread.shape[0]):
        spread[copy, body] = x
        spread[copy, end] = side


CHUNK = 256


def set_columns(columns, right, line, member):
    points, width = columns.shape[1] - SIDE, columns.shape[2]
    for block in range(8):
        at = pl.ds(block * points, points)
        high, low = halves(columns[block, pl.ds(0, points)])
        right[at, pl.ds(0, width)] = high
        right[at, pl.ds(width, width)] = low
        right[at, pl.ds(2 * width, width)] = high
        side = columns[block, pl.ds(points, 1)]
        line[:, at] = jnp.broadcast_to(side[:, points:], (SIDE, points))
        member[at] = seed_member(side[:, :points]).astype(jnp.bfloat16)


def left_rows(x):
    high, low = halves(-2.0 * x)
    return jnp.concatenate([high, high, low], axis=1), jnp.sum(x * x, axis=1, keepdims=True) + 1.0


def distances(left, square, right, line, high_out, low_out, at):
    inner = lax.dot_general(left, right[...], (((1,), (1,)), ((), ())), preferred_element_type=jnp.float32)
    squared = inner + square + line[pl.ds(0, 1)]
    high_out[at], low_out[at] = halves(squared * lax.rsqrt(squared))


def weights(high, low, member, at):
    return product(high[at], member[...]) + product(low[at], member[...])


EARLY = 768


def own_pair_kernel(*refs):
    rows, (columns, left, squares, right, line, member, high, low, out) = refs[:6], refs[6:]
    points = rows[0].shape[0] - SIDE
    set_columns(columns, right, line, member)
    for offset, block in enumerate(rows):
        at = pl.ds(offset * points, points)
        left[at], squares[at] = left_rows(block[pl.ds(0, points)])
    for start in range(0, EARLY, CHUNK):
        at = pl.ds(start, CHUNK)
        distances(left[at], squares[at], right, line, high, low, at)
    out[...] = weights(high, low, member, pl.ds(0, EARLY))


def other_pair_kernel(columns, left, squares, weighted, right, line, member, high, low, out):
    set_columns(columns, right, line, member)
    for start in range(0, EARLY, CHUNK):
        at = pl.ds(start, CHUNK)
        distances(left[at], squares[at], right, line, high, low, at)
    out[...] = weighted[...] + weights(high, low, member, pl.ds(0, EARLY))


def late_pair_kernel(*refs):
    rows, sides, weighted, refs = refs[:8], (refs[8:11], refs[11:14]), refs[14], refs[19:]
    (*kept, out) = refs
    points = rows[0].shape[0] - SIDE
    at = pl.ds(EARLY, CHUNK)
    left, square = left_rows(jnp.concatenate([block[pl.ds(0, points)] for block in rows[6:]], axis=0))
    late = 0.0
    for half, (right, line, member) in enumerate(sides):
        high, low = kept[2 * half : 2 * half + 2]
        distances(left, square, right, line, high, low, at)
        late += weights(high, low, member, at)
    cohesion = jnp.zeros((1, CLUSTER_COUNT), jnp.float32)
    for offset in range(8):
        start = offset * points
        part = weighted[pl.ds(start, points)] if start < EARLY else late[start - EARLY : start - EARLY + points]
        out[member_at(offset), pl.ds(0, points)] = part
        own = seed_member(rows[offset][pl.ds(points, 1)][:, :points])
        cohesion += jnp.sum(own * part, axis=0, keepdims=True)
    counts = jnp.sum(seed_member(rows[0][pl.ds(points, 1)][:, :points]), axis=0, keepdims=True)
    tail = tail_rows(cohesion, counts)
    for target in range(8):
        out[target, pl.ds(points, SIDE)] = tail


def member_kernel(own, other, own_high, own_low, other_high, other_low, first, out, own_member, both):
    points = own.shape[1] - SIDE
    sums = jnp.zeros((SIDE, CLUSTER_COUNT), jnp.float32)
    for block in range(8):
        sums += own[block, pl.ds(points, SIDE)] + other[block, pl.ds(points, SIDE)]
    cohesion, counts = sums[0:1], sums[1:2]
    own_member[...] = jnp.exp(log_softmax_energy(first[pl.ds(0, points)], counts, cohesion))
    sizes = jnp.zeros((1, CLUSTER_COUNT), jnp.float32)
    total = 0.0
    for source, high, low in ((own, own_high, own_low), (other, other_high, other_low)):
        for block in range(8):
            member = jnp.exp(log_softmax_energy(source[block, pl.ds(0, points)], counts, cohesion))
            sizes += jnp.sum(member, axis=0, keepdims=True)
            at = pl.ds(block * points, points)
            both[at, pl.ds(0, CLUSTER_COUNT)], both[at, pl.ds(CLUSTER_COUNT, CLUSTER_COUNT)] = halves(member)
        wide = product(high[...], both[...])
        total += product(low[...], both[:, pl.ds(0, CLUSTER_COUNT)])
        total += wide[:, :CLUSTER_COUNT] + wide[:, CLUSTER_COUNT:]
    tail = tail_rows(sizes)
    for block in range(8):
        out[member_at(block), pl.ds(0, points)] = total[block * points : (block + 1) * points]
        out[member_at(block), pl.ds(points, SIDE)] = tail


def summed(blocks):
    total = blocks[0]
    for block in range(1, 8):
        total += blocks[block]
    return total


def sum_kernel(blocks, out, spread):
    out[...] = summed(blocks)
    spread[...] = jnp.broadcast_to(out[...], spread.shape)


def own_kernel(blocks, own, out, part):
    points = own.shape[0]
    out[...] = summed(blocks)
    part[...] = jnp.sum(own[...] * out[pl.ds(0, points)], axis=0, keepdims=True)


def final_kernel(second, cohesion, out):
    points = out.shape[0]
    out[...] = log_softmax_energy(second[pl.ds(0, points)], second[pl.ds(points, 1)], cohesion[...])


PARAMS = pltpu.CompilerParams(vmem_limit_bytes=12 << 20)


def on_chip(kernel, name, shapes, inputs, scratch=(), aliases={}):
    vmem = pl.BlockSpec(memory_space=pltpu.VMEM)
    specs = [vmem] * len(inputs)
    shapes = [jax.ShapeDtypeStruct(*shape) for shape in shapes]
    return pl.pallas_call(
        kernel,
        out_shape=shapes,
        in_specs=specs,
        out_specs=[vmem] * len(shapes),
        scratch_shapes=scratch,
        input_output_aliases=aliases,
        compiler_params=PARAMS,
        name=name,
    )(*inputs)


def copies(x, count):
    return jnp.broadcast_to(x, (count, *x.shape))


def other_core(x):
    return lax.ppermute(x, "core", [(0, 1), (1, 0)])


def log_softmax_energy(attraction, counts, cohesion):
    energy = attraction / counts - cohesion / (2.0 * counts**2)
    logits = -energy / ANNEAL_TEMP_VALUE
    highest = jnp.max(logits, axis=1, keepdims=True)
    return logits - highest - jnp.log(jnp.sum(jnp.exp(logits - highest), axis=1, keepdims=True))


def shards(embedding, seed_cluster):
    points, width = embedding.shape
    lines, tall = points + SIDE, 8 * points
    outside, vmem = pl.BlockSpec(memory_space=pltpu.HBM), pl.BlockSpec(memory_space=pltpu.VMEM)
    block, spread = pl.pallas_call(
        prepare_kernel,
        out_shape=[jax.ShapeDtypeStruct((lines, width), jnp.float32), jax.ShapeDtypeStruct((8, lines, width), jnp.float32)],
        in_specs=[outside, outside],
        out_specs=[vmem, vmem],
        scratch_shapes=[pltpu.VMEM((1, points), jnp.int32), pltpu.SemaphoreType.DMA((2,))],
        name="prepare",
    )(embedding, seed_cluster.reshape(1, points))
    columns = exchange_columns(spread)
    rows = row_peers(block)
    columns, *rows[:6] = lax.optimization_barrier((columns, *rows[:6]))
    kept = ((tall, tall), jnp.bfloat16)
    exchange = ((8, lines, CLUSTER_COUNT), jnp.float32)
    sides = [((tall, 3 * width), jnp.bfloat16), ((SIDE, tall), jnp.float32), ((tall, CLUSTER_COUNT), jnp.bfloat16)]
    lefts = [((EARLY, 3 * width), jnp.bfloat16), ((EARLY, 1), jnp.float32)]
    early = ((EARLY, CLUSTER_COUNT), jnp.float32)
    left, squares, *own_sides, own_high, own_low, weighted = on_chip(
        own_pair_kernel, "own_pairs", [*lefts, *sides, kept, kept, early], [*rows[:6], columns]
    )
    *other_sides, other_high, other_low, weighted = on_chip(
        other_pair_kernel,
        "other_pairs",
        [*sides, kept, kept, early],
        [other_core(columns), left, squares, weighted],
    )
    own_high, own_low, other_high, other_low, weighted = on_chip(
        late_pair_kernel,
        "late_pairs",
        [kept] * 4 + [exchange],
        [*rows, *own_sides, *other_sides, weighted, own_high, own_low, other_high, other_low],
        aliases={15: 0, 16: 1, 17: 2, 18: 3},
    )

    line = ((lines, CLUSTER_COUNT), jnp.float32)
    first, spread = on_chip(sum_kernel, "sum_spread", [line, exchange], [exchange_rows(weighted)])
    firsts = exchange_columns(spread)
    weighted, own = on_chip(
        member_kernel,
        "members",
        [exchange, ((points, CLUSTER_COUNT), jnp.float32)],
        [firsts, other_core(firsts), own_high, own_low, other_high, other_low, first],
        scratch=[pltpu.VMEM((tall, 2 * CLUSTER_COUNT), jnp.bfloat16)],
    )

    part = ((1, CLUSTER_COUNT), jnp.float32)
    second, part = on_chip(own_kernel, "own_sums", [line, part], [exchange_rows(weighted), own])
    parts = lax.all_to_all(copies(part, 128), EVERY, 0, 0, tiled=True)
    (out,) = on_chip(
        final_kernel,
        "final",
        [((points, CLUSTER_COUNT), jnp.float32)],
        [second, jnp.sum(parts, axis=0)],
    )
    return out


def solution(mesh):
    finer = Mesh(mesh.devices.reshape(SIZES), EVERY)
    return jax.shard_map(
        shards, mesh=finer, in_specs=(P(EVERY, None), P(EVERY)), out_specs=P(EVERY, None), check_vma=False
    )
```

```python
import functools
import itertools

import jax
import jax.numpy as jnp
from jax import lax
from jax.experimental import pallas as pl
from jax.experimental.pallas import tpu as pltpu
from jax.sharding import Mesh
from jax.sharding import PartitionSpec as P

CLUSTER_COUNT = 128
ANNEAL_TEMP_VALUE = 0.02
SIDE = 8

EVERY = ("y_lo", "z", "y_hi", "x", "core")
SIZES = (2, 4, 2, 4, 2)


def place(y_lo, z, y_hi, x, core):
    return (((y_lo * 4 + z) * 2 + y_hi) * 4 + x) * 2 + core


def column_groups():
    groups = []
    for pair, x, core in itertools.product(range(2), range(4), range(2)):
        groups.append([place(lo, z, lo ^ pair, x, core) for lo in range(2) for z in range(4)])
    return groups


COLUMN_GROUPS = column_groups()
ROW_ORDER = ((0, 0), (1, 2), (1, 3), (1, 1), (0, 2), (0, 3), (0, 1), (1, 0))


def exchange_rows(blocks):
    return lax.all_to_all(blocks, ("y_lo", "x"), 0, 0, tiled=True)


def exchange_columns(blocks):
    return lax.all_to_all(blocks, EVERY, 0, 0, axis_index_groups=COLUMN_GROUPS, tiled=True)


def moved(x, flip, step):
    pairs = []
    for lo, z, hi, at, core in itertools.product(*map(range, SIZES)):
        pairs.append((place(lo ^ flip, z, hi, (at + step) % 4, core), place(lo, z, hi, at, core)))
    return lax.ppermute(x, EVERY, pairs)


def row_peers(x):
    return [moved(x, flip, step) if flip or step else x for flip, step in ROW_ORDER]


def member_at(offset):
    y_lo, x = lax.axis_index("y_lo"), lax.axis_index("x")
    flip, step = ROW_ORDER[offset]
    return ((1 - y_lo) if flip else y_lo) * 4 + (x + step) % 4


def halves(x):
    high = x.astype(jnp.bfloat16)
    return high, (x - high.astype(jnp.float32)).astype(jnp.bfloat16)


def product(a, b):
    return jnp.dot(a, b, preferred_element_type=jnp.float32)


def seed_member(seeds):
    labels = lax.broadcasted_iota(jnp.int32, (CLUSTER_COUNT, seeds.shape[1]), 0).astype(jnp.float32)
    return 0.5 * (labels == seeds).astype(jnp.float32).T + 0.5 / CLUSTER_COUNT


def tail_rows(*lines):
    at = lax.broadcasted_iota(jnp.int32, (SIDE, CLUSTER_COUNT), 0)
    tail = jnp.zeros((SIDE, CLUSTER_COUNT), jnp.float32)
    for index, line in enumerate(lines):
        tail = jnp.where(at == index, line, tail)
    return tail


def prepare_kernel(embedding, seeds, block, spread, labels, arrived):
    points, width = embedding.shape
    body, end = pl.ds(0, points), pl.ds(points, SIDE)
    loads = [
        pltpu.make_async_copy(embedding, block.at[body], arrived.at[0]),
        pltpu.make_async_copy(seeds, labels, arrived.at[1]),
    ]
    for load in loads:
        load.start()
    for load in loads:
        load.wait()
    x = block[body]
    side = jnp.concatenate([labels[...].astype(jnp.float32), jnp.sum((x * x).T, axis=0, keepdims=True)], axis=1)
    side = jnp.broadcast_to(side, (SIDE, width))
    block[end] = side
    for copy in range(spread.shape[0]):
        spread[copy, body] = x
        spread[copy, end] = side


CHUNK = 256


def set_columns(columns, right, line, member):
    points, width = columns.shape[1] - SIDE, columns.shape[2]
    for block in range(8):
        at = pl.ds(block * points, points)
        high, low = halves(columns[block, pl.ds(0, points)])
        right[at, pl.ds(0, width)] = high
        right[at, pl.ds(width, width)] = low
        right[at, pl.ds(2 * width, width)] = high
        side = columns[block, pl.ds(points, 1)]
        line[:, at] = jnp.broadcast_to(side[:, points:], (SIDE, points))
        member[at] = seed_member(side[:, :points]).astype(jnp.bfloat16)


def left_rows(x):
    high, low = halves(-2.0 * x)
    return jnp.concatenate([high, high, low], axis=1), jnp.sum(x * x, axis=1, keepdims=True) + 1.0


def distances(left, square, right, line, high_out, low_out, at):
    inner = lax.dot_general(left, right[...], (((1,), (1,)), ((), ())), preferred_element_type=jnp.float32)
    squared = inner + square + line[pl.ds(0, 1)]
    high_out[at], low_out[at] = halves(squared * lax.rsqrt(squared))


def weights(high, low, member, at):
    return product(high[at], member[...]) + product(low[at], member[...])


EARLY = 768


def own_pair_kernel(*refs):
    rows, (columns, left, squares, right, line, member, high, low, out) = refs[:6], refs[6:]
    points = rows[0].shape[0] - SIDE
    set_columns(columns, right, line, member)
    for offset, block in enumerate(rows):
        at = pl.ds(offset * points, points)
        left[at], squares[at] = left_rows(block[pl.ds(0, points)])
    for start in range(0, EARLY, CHUNK):
        at = pl.ds(start, CHUNK)
        distances(left[at], squares[at], right, line, high, low, at)
    out[...] = weights(high, low, member, pl.ds(0, EARLY))


def other_pair_kernel(columns, left, squares, weighted, right, line, member, high, low, out):
    set_columns(columns, right, line, member)
    for start in range(0, EARLY, CHUNK):
        at = pl.ds(start, CHUNK)
        distances(left[at], squares[at], right, line, high, low, at)
    out[...] = weighted[...] + weights(high, low, member, pl.ds(0, EARLY))


def late_pair_kernel(*refs):
    rows, sides, weighted, refs = refs[:8], (refs[8:11], refs[11:14]), refs[14], refs[19:]
    (*kept, out) = refs
    points = rows[0].shape[0] - SIDE
    at = pl.ds(EARLY, CHUNK)
    left, square = left_rows(jnp.concatenate([block[pl.ds(0, points)] for block in rows[6:]], axis=0))
    late = 0.0
    for half, (right, line, member) in enumerate(sides):
        high, low = kept[2 * half : 2 * half + 2]
        distances(left, square, right, line, high, low, at)
        late += weights(high, low, member, at)
    cohesion = jnp.zeros((1, CLUSTER_COUNT), jnp.float32)
    for offset in range(8):
        start = offset * points
        part = weighted[pl.ds(start, points)] if start < EARLY else late[start - EARLY : start - EARLY + points]
        out[member_at(offset), pl.ds(0, points)] = part
        own = seed_member(rows[offset][pl.ds(points, 1)][:, :points])
        cohesion += jnp.sum(own * part, axis=0, keepdims=True)
    counts = jnp.sum(seed_member(rows[0][pl.ds(points, 1)][:, :points]), axis=0, keepdims=True)
    tail = tail_rows(cohesion, counts)
    for target in range(8):
        out[target, pl.ds(points, SIDE)] = tail


def tail_kernel(blocks, out):
    points = blocks.shape[1] - SIDE
    out[...] = sum(blocks[block, pl.ds(points, SIDE)] for block in range(8))


def half_product(source, sums, high, low, both):
    points = source.shape[1] - SIDE
    sizes = jnp.zeros((1, CLUSTER_COUNT), jnp.float32)
    for block in range(8):
        member = jnp.exp(log_softmax_energy(source[block, pl.ds(0, points)], sums[1:2], sums[0:1]))
        sizes += jnp.sum(member, axis=0, keepdims=True)
        at = pl.ds(block * points, points)
        both[at, pl.ds(0, CLUSTER_COUNT)], both[at, pl.ds(CLUSTER_COUNT, CLUSTER_COUNT)] = halves(member)
    wide = product(high[...], both[...])
    total = product(low[...], both[:, pl.ds(0, CLUSTER_COUNT)])
    return total + wide[:, :CLUSTER_COUNT] + wide[:, CLUSTER_COUNT:], sizes


def own_member_kernel(blocks, tail, far_tail, high, low, first, out, sums, own_member, both):
    points = own_member.shape[0]
    both_tails = tail[...] + far_tail[...]
    own_member[...] = jnp.exp(log_softmax_energy(first[pl.ds(0, points)], both_tails[1:2], both_tails[0:1]))
    out[...], sizes = half_product(blocks, both_tails, high, low, both)
    sums[...] = tail_rows(both_tails[0:1], both_tails[1:2], sizes)


def other_member_kernel(blocks, sums, high, low, weighted, out, both):
    points = blocks.shape[1] - SIDE
    total, sizes = half_product(blocks, sums[...], high, low, both)
    total += weighted[...]
    tail = tail_rows(sums[pl.ds(2, 1)] + sizes)
    for block in range(8):
        out[member_at(block), pl.ds(0, points)] = total[block * points : (block + 1) * points]
        out[member_at(block), pl.ds(points, SIDE)] = tail


def summed(blocks):
    total = blocks[0]
    for block in range(1, 8):
        total += blocks[block]
    return total


def sum_kernel(blocks, out, spread):
    out[...] = summed(blocks)
    spread[...] = jnp.broadcast_to(out[...], spread.shape)


def own_kernel(blocks, own, out, part):
    points = own.shape[0]
    out[...] = summed(blocks)
    part[...] = jnp.sum(own[...] * out[pl.ds(0, points)], axis=0, keepdims=True)


def final_kernel(second, cohesion, out):
    points = out.shape[0]
    out[...] = log_softmax_energy(second[pl.ds(0, points)], second[pl.ds(points, 1)], cohesion[...])


PARAMS = pltpu.CompilerParams(vmem_limit_bytes=12 << 20)


def on_chip(kernel, name, shapes, inputs, scratch=(), aliases={}):
    vmem = pl.BlockSpec(memory_space=pltpu.VMEM)
    specs = [vmem] * len(inputs)
    shapes = [jax.ShapeDtypeStruct(*shape) for shape in shapes]
    return pl.pallas_call(
        kernel,
        out_shape=shapes,
        in_specs=specs,
        out_specs=[vmem] * len(shapes),
        scratch_shapes=scratch,
        input_output_aliases=aliases,
        compiler_params=PARAMS,
        name=name,
    )(*inputs)


def copies(x, count):
    return jnp.broadcast_to(x, (count, *x.shape))


def other_core(x):
    return lax.ppermute(x, "core", [(0, 1), (1, 0)])


def log_softmax_energy(attraction, counts, cohesion):
    energy = attraction / counts - cohesion / (2.0 * counts**2)
    logits = -energy / ANNEAL_TEMP_VALUE
    highest = jnp.max(logits, axis=1, keepdims=True)
    return logits - highest - jnp.log(jnp.sum(jnp.exp(logits - highest), axis=1, keepdims=True))


def shards(embedding, seed_cluster):
    points, width = embedding.shape
    lines, tall = points + SIDE, 8 * points
    outside, vmem = pl.BlockSpec(memory_space=pltpu.HBM), pl.BlockSpec(memory_space=pltpu.VMEM)
    block, spread = pl.pallas_call(
        prepare_kernel,
        out_shape=[jax.ShapeDtypeStruct((lines, width), jnp.float32), jax.ShapeDtypeStruct((8, lines, width), jnp.float32)],
        in_specs=[outside, outside],
        out_specs=[vmem, vmem],
        scratch_shapes=[pltpu.VMEM((1, points), jnp.int32), pltpu.SemaphoreType.DMA((2,))],
        name="prepare",
    )(embedding, seed_cluster.reshape(1, points))
    columns = exchange_columns(spread)
    rows = row_peers(block)
    columns, *rows[:6] = lax.optimization_barrier((columns, *rows[:6]))
    kept = ((tall, tall), jnp.bfloat16)
    exchange = ((8, lines, CLUSTER_COUNT), jnp.float32)
    sides = [((tall, 3 * width), jnp.bfloat16), ((SIDE, tall), jnp.float32), ((tall, CLUSTER_COUNT), jnp.bfloat16)]
    lefts = [((EARLY, 3 * width), jnp.bfloat16), ((EARLY, 1), jnp.float32)]
    early = ((EARLY, CLUSTER_COUNT), jnp.float32)
    left, squares, *own_sides, own_high, own_low, weighted = on_chip(
        own_pair_kernel, "own_pairs", [*lefts, *sides, kept, kept, early], [*rows[:6], columns]
    )
    *other_sides, other_high, other_low, weighted = on_chip(
        other_pair_kernel,
        "other_pairs",
        [*sides, kept, kept, early],
        [other_core(columns), left, squares, weighted],
    )
    own_high, own_low, other_high, other_low, weighted = on_chip(
        late_pair_kernel,
        "late_pairs",
        [kept] * 4 + [exchange],
        [*rows, *own_sides, *other_sides, weighted, own_high, own_low, other_high, other_low],
        aliases={15: 0, 16: 1, 17: 2, 18: 3},
    )

    line = ((lines, CLUSTER_COUNT), jnp.float32)
    first, spread = on_chip(sum_kernel, "sum_spread", [line, exchange], [exchange_rows(weighted)])
    tail = ((SIDE, CLUSTER_COUNT), jnp.float32)
    firsts = exchange_columns(spread)
    (sums,) = on_chip(tail_kernel, "tails", [tail], [firsts])
    far_sums = other_core(sums)
    firsts, far_sums = lax.optimization_barrier((firsts, far_sums))
    both = [pltpu.VMEM((tall, 2 * CLUSTER_COUNT), jnp.bfloat16)]
    weighted, sums, own = on_chip(
        own_member_kernel,
        "own_members",
        [((tall, CLUSTER_COUNT), jnp.float32), tail, ((points, CLUSTER_COUNT), jnp.float32)],
        [firsts, sums, far_sums, own_high, own_low, first],
        scratch=both,
    )
    (weighted,) = on_chip(
        other_member_kernel,
        "other_members",
        [exchange],
        [other_core(firsts), sums, other_high, other_low, weighted],
        scratch=both,
    )

    part = ((1, CLUSTER_COUNT), jnp.float32)
    second, part = on_chip(own_kernel, "own_sums", [line, part], [exchange_rows(weighted), own])
    parts = lax.all_to_all(copies(part, 128), EVERY, 0, 0, tiled=True)
    (out,) = on_chip(
        final_kernel,
        "final",
        [((points, CLUSTER_COUNT), jnp.float32)],
        [second, jnp.sum(parts, axis=0)],
    )
    return out


def solution(mesh):
    finer = Mesh(mesh.devices.reshape(SIZES), EVERY)
    return jax.shard_map(
        shards, mesh=finer, in_specs=(P(EVERY, None), P(EVERY)), out_specs=P(EVERY, None), check_vma=False
    )
```

```python
import functools
import itertools

import jax
import jax.numpy as jnp
from jax import lax
from jax.experimental import pallas as pl
from jax.experimental.pallas import tpu as pltpu
from jax.sharding import Mesh
from jax.sharding import PartitionSpec as P

CLUSTER_COUNT = 128
ANNEAL_TEMP_VALUE = 0.02
SIDE = 8

EVERY = ("y_lo", "z", "y_hi", "x", "core")
SIZES = (2, 4, 2, 4, 2)


def place(y_lo, z, y_hi, x, core):
    return (((y_lo * 4 + z) * 2 + y_hi) * 4 + x) * 2 + core


def column_groups():
    groups = []
    for pair, x, core in itertools.product(range(2), range(4), range(2)):
        groups.append([place(lo, z, lo ^ pair, x, core) for lo in range(2) for z in range(4)])
    return groups


COLUMN_GROUPS = column_groups()
ROW_ORDER = ((0, 0), (1, 2), (1, 3), (1, 1), (0, 2), (0, 3), (0, 1), (1, 0))


def exchange_rows(blocks):
    return lax.all_to_all(blocks, ("y_lo", "x"), 0, 0, tiled=True)


def exchange_columns(blocks):
    return lax.all_to_all(blocks, EVERY, 0, 0, axis_index_groups=COLUMN_GROUPS, tiled=True)


def moved(x, flip, step):
    pairs = []
    for lo, z, hi, at, core in itertools.product(*map(range, SIZES)):
        pairs.append((place(lo ^ flip, z, hi, (at + step) % 4, core), place(lo, z, hi, at, core)))
    return lax.ppermute(x, EVERY, pairs)


def row_peers(x):
    return [moved(x, flip, step) if flip or step else x for flip, step in ROW_ORDER]


def member_at(offset):
    y_lo, x = lax.axis_index("y_lo"), lax.axis_index("x")
    flip, step = ROW_ORDER[offset]
    return ((1 - y_lo) if flip else y_lo) * 4 + (x + step) % 4


def halves(x):
    high = x.astype(jnp.bfloat16)
    return high, (x - high.astype(jnp.float32)).astype(jnp.bfloat16)


def product(a, b):
    return jnp.dot(a, b, preferred_element_type=jnp.float32)


def seed_member(seeds):
    labels = lax.broadcasted_iota(jnp.int32, (CLUSTER_COUNT, seeds.shape[1]), 0).astype(jnp.float32)
    return 0.5 * (labels == seeds).astype(jnp.float32).T + 0.5 / CLUSTER_COUNT


def tail_rows(*lines):
    at = lax.broadcasted_iota(jnp.int32, (SIDE, CLUSTER_COUNT), 0)
    tail = jnp.zeros((SIDE, CLUSTER_COUNT), jnp.float32)
    for index, line in enumerate(lines):
        tail = jnp.where(at == index, line, tail)
    return tail


def prepare_kernel(embedding, seeds, block, spread, labels, arrived):
    points, width = embedding.shape
    body, end = pl.ds(0, points), pl.ds(points, SIDE)
    loads = [
        pltpu.make_async_copy(embedding, block.at[body], arrived.at[0]),
        pltpu.make_async_copy(seeds, labels, arrived.at[1]),
    ]
    for load in loads:
        load.start()
    for load in loads:
        load.wait()
    x = block[body]
    side = jnp.concatenate([labels[...].astype(jnp.float32), jnp.sum((x * x).T, axis=0, keepdims=True)], axis=1)
    side = jnp.broadcast_to(side, (SIDE, width))
    block[end] = side
    for copy in range(spread.shape[0]):
        spread[copy, body] = x
        spread[copy, end] = side


CHUNK = 256


def set_columns(columns, right, line, member):
    points, width = columns.shape[1] - SIDE, columns.shape[2]
    for block in range(8):
        at = pl.ds(block * points, points)
        high, low = halves(columns[block, pl.ds(0, points)])
        right[at, pl.ds(0, width)] = high
        right[at, pl.ds(width, width)] = low
        right[at, pl.ds(2 * width, width)] = high
        side = columns[block, pl.ds(points, 1)]
        line[:, at] = jnp.broadcast_to(side[:, points:], (SIDE, points))
        member[at] = seed_member(side[:, :points]).astype(jnp.bfloat16)


def left_rows(x):
    high, low = halves(-2.0 * x)
    return jnp.concatenate([high, high, low], axis=1), jnp.sum(x * x, axis=1, keepdims=True) + 1.0


def distances(left, square, right, line, high_out, low_out, at):
    inner = lax.dot_general(left, right[...], (((1,), (1,)), ((), ())), preferred_element_type=jnp.float32)
    squared = inner + square + line[pl.ds(0, 1)]
    high_out[at], low_out[at] = halves(squared * lax.rsqrt(squared))


def weights(high, low, member, at):
    return product(high[at], member[...]) + product(low[at], member[...])


EARLY = 768


FIRST = (0, 2, 3, 4, 5)


def row_kernel(*refs):
    rows, (left, squares, members) = refs[: len(FIRST)], refs[len(FIRST) :]
    points = rows[0].shape[0] - SIDE
    for offset, block in zip(FIRST, rows):
        at = pl.ds(offset * points, points)
        left[at], squares[at] = left_rows(block[pl.ds(0, points)])
        members[at] = seed_member(block[pl.ds(points, 1)][:, :points])


def own_pair_kernel(last, columns, _, __, left, squares, right, line, member, high, low, out):
    points = last.shape[0] - SIDE
    set_columns(columns, right, line, member)
    at = pl.ds(points, points)
    left[at], squares[at] = left_rows(last[pl.ds(0, points)])
    for start in range(0, EARLY, CHUNK):
        at = pl.ds(start, CHUNK)
        distances(left[at], squares[at], right, line, high, low, at)
    out[...] = weights(high, low, member, pl.ds(0, EARLY))


def other_pair_kernel(columns, left, squares, weighted, right, line, member, high, low, out):
    set_columns(columns, right, line, member)
    for start in range(0, EARLY, CHUNK):
        at = pl.ds(start, CHUNK)
        distances(left[at], squares[at], right, line, high, low, at)
    out[...] = weighted[...] + weights(high, low, member, pl.ds(0, EARLY))


def late_pair_kernel(*refs):
    rows, members, sides, weighted, refs = refs[:3], refs[3], (refs[4:7], refs[7:10]), refs[10], refs[15:]
    (*kept, out) = refs
    points = rows[0].shape[0] - SIDE
    at = pl.ds(EARLY, CHUNK)
    left, square = left_rows(jnp.concatenate([block[pl.ds(0, points)] for block in rows[1:]], axis=0))
    late = 0.0
    for half, (right, line, member) in enumerate(sides):
        high, low = kept[2 * half : 2 * half + 2]
        distances(left, square, right, line, high, low, at)
        late += weights(high, low, member, at)
    cohesion = jnp.zeros((1, CLUSTER_COUNT), jnp.float32)
    for offset in range(8):
        start = offset * points
        part = weighted[pl.ds(start, points)] if start < EARLY else late[start - EARLY : start - EARLY + points]
        out[member_at(offset), pl.ds(0, points)] = part
        if offset in FIRST:
            own = members[pl.ds(start, points)]
        else:
            own = seed_member(rows[{1: 0, 6: 1, 7: 2}[offset]][pl.ds(points, 1)][:, :points])
        cohesion += jnp.sum(own * part, axis=0, keepdims=True)
    counts = jnp.sum(members[pl.ds(0, points)], axis=0, keepdims=True)
    tail = tail_rows(cohesion, counts)
    for target in range(8):
        out[target, pl.ds(points, SIDE)] = tail


def member_kernel(own, other, own_high, own_low, other_high, other_low, first, out, own_member, both):
    points = own.shape[1] - SIDE
    sums = jnp.zeros((SIDE, CLUSTER_COUNT), jnp.float32)
    for block in range(8):
        sums += own[block, pl.ds(points, SIDE)] + other[block, pl.ds(points, SIDE)]
    cohesion, counts = sums[0:1], sums[1:2]
    own_member[...] = jnp.exp(log_softmax_energy(first[pl.ds(0, points)], counts, cohesion))
    sizes = jnp.zeros((1, CLUSTER_COUNT), jnp.float32)
    total = 0.0
    for source, high, low in ((own, own_high, own_low), (other, other_high, other_low)):
        for block in range(8):
            member = jnp.exp(log_softmax_energy(source[block, pl.ds(0, points)], counts, cohesion))
            sizes += jnp.sum(member, axis=0, keepdims=True)
            at = pl.ds(block * points, points)
            both[at, pl.ds(0, CLUSTER_COUNT)], both[at, pl.ds(CLUSTER_COUNT, CLUSTER_COUNT)] = halves(member)
        wide = product(high[...], both[...])
        total += product(low[...], both[:, pl.ds(0, CLUSTER_COUNT)])
        total += wide[:, :CLUSTER_COUNT] + wide[:, CLUSTER_COUNT:]
    tail = tail_rows(sizes)
    for block in range(8):
        out[member_at(block), pl.ds(0, points)] = total[block * points : (block + 1) * points]
        out[member_at(block), pl.ds(points, SIDE)] = tail


def summed(blocks):
    total = blocks[0]
    for block in range(1, 8):
        total += blocks[block]
    return total


def sum_kernel(blocks, out, spread):
    out[...] = summed(blocks)
    spread[...] = jnp.broadcast_to(out[...], spread.shape)


def own_kernel(blocks, own, out, part):
    points = own.shape[0]
    out[...] = summed(blocks)
    part[...] = jnp.sum(own[...] * out[pl.ds(0, points)], axis=0, keepdims=True)


def final_kernel(second, cohesion, out):
    points = out.shape[0]
    out[...] = log_softmax_energy(second[pl.ds(0, points)], second[pl.ds(points, 1)], cohesion[...])


PARAMS = pltpu.CompilerParams(vmem_limit_bytes=12 << 20)


def on_chip(kernel, name, shapes, inputs, scratch=(), aliases={}):
    vmem = pl.BlockSpec(memory_space=pltpu.VMEM)
    specs = [vmem] * len(inputs)
    shapes = [jax.ShapeDtypeStruct(*shape) for shape in shapes]
    return pl.pallas_call(
        kernel,
        out_shape=shapes,
        in_specs=specs,
        out_specs=[vmem] * len(shapes),
        scratch_shapes=scratch,
        input_output_aliases=aliases,
        compiler_params=PARAMS,
        name=name,
    )(*inputs)


def copies(x, count):
    return jnp.broadcast_to(x, (count, *x.shape))


def other_core(x):
    return lax.ppermute(x, "core", [(0, 1), (1, 0)])


def log_softmax_energy(attraction, counts, cohesion):
    energy = attraction / counts - cohesion / (2.0 * counts**2)
    logits = -energy / ANNEAL_TEMP_VALUE
    highest = jnp.max(logits, axis=1, keepdims=True)
    return logits - highest - jnp.log(jnp.sum(jnp.exp(logits - highest), axis=1, keepdims=True))


def shards(embedding, seed_cluster):
    points, width = embedding.shape
    lines, tall = points + SIDE, 8 * points
    outside, vmem = pl.BlockSpec(memory_space=pltpu.HBM), pl.BlockSpec(memory_space=pltpu.VMEM)
    block, spread = pl.pallas_call(
        prepare_kernel,
        out_shape=[jax.ShapeDtypeStruct((lines, width), jnp.float32), jax.ShapeDtypeStruct((8, lines, width), jnp.float32)],
        in_specs=[outside, outside],
        out_specs=[vmem, vmem],
        scratch_shapes=[pltpu.VMEM((1, points), jnp.int32), pltpu.SemaphoreType.DMA((2,))],
        name="prepare",
    )(embedding, seed_cluster.reshape(1, points))
    columns = exchange_columns(spread)
    rows = row_peers(block)
    lefts = [((EARLY, 3 * width), jnp.bfloat16), ((EARLY, 1), jnp.float32)]
    early = ((EARLY, CLUSTER_COUNT), jnp.float32)
    *prepared, members = on_chip(row_kernel, "rows", [*lefts, early], [rows[offset] for offset in FIRST])
    columns, rows[1], *prepared = lax.optimization_barrier((columns, rows[1], *prepared))
    kept = ((tall, tall), jnp.bfloat16)
    exchange = ((8, lines, CLUSTER_COUNT), jnp.float32)
    sides = [((tall, 3 * width), jnp.bfloat16), ((SIDE, tall), jnp.float32), ((tall, CLUSTER_COUNT), jnp.bfloat16)]
    left, squares, *own_sides, own_high, own_low, weighted = on_chip(
        own_pair_kernel,
        "own_pairs",
        [*lefts, *sides, kept, kept, early],
        [rows[1], columns, *prepared],
        aliases={2: 0, 3: 1},
    )
    *other_sides, other_high, other_low, weighted = on_chip(
        other_pair_kernel,
        "other_pairs",
        [*sides, kept, kept, early],
        [other_core(columns), left, squares, weighted],
    )
    own_high, own_low, other_high, other_low, weighted = on_chip(
        late_pair_kernel,
        "late_pairs",
        [kept] * 4 + [exchange],
        [rows[1], *rows[6:], members, *own_sides, *other_sides, weighted, own_high, own_low, other_high, other_low],
        aliases={11: 0, 12: 1, 13: 2, 14: 3},
    )

    line = ((lines, CLUSTER_COUNT), jnp.float32)
    first, spread = on_chip(sum_kernel, "sum_spread", [line, exchange], [exchange_rows(weighted)])
    firsts = exchange_columns(spread)
    weighted, own = on_chip(
        member_kernel,
        "members",
        [exchange, ((points, CLUSTER_COUNT), jnp.float32)],
        [firsts, other_core(firsts), own_high, own_low, other_high, other_low, first],
        scratch=[pltpu.VMEM((tall, 2 * CLUSTER_COUNT), jnp.bfloat16)],
    )

    part = ((1, CLUSTER_COUNT), jnp.float32)
    second, part = on_chip(own_kernel, "own_sums", [line, part], [exchange_rows(weighted), own])
    parts = lax.all_to_all(copies(part, 128), EVERY, 0, 0, tiled=True)
    (out,) = on_chip(
        final_kernel,
        "final",
        [((points, CLUSTER_COUNT), jnp.float32)],
        [second, jnp.sum(parts, axis=0)],
    )
    return out


def solution(mesh):
    finer = Mesh(mesh.devices.reshape(SIZES), EVERY)
    return jax.shard_map(
        shards, mesh=finer, in_specs=(P(EVERY, None), P(EVERY)), out_specs=P(EVERY, None), check_vma=False
    )
```

```python
import functools
import itertools

import jax
import jax.numpy as jnp
from jax import lax
from jax.experimental import pallas as pl
from jax.experimental.pallas import tpu as pltpu
from jax.sharding import Mesh
from jax.sharding import PartitionSpec as P

CLUSTER_COUNT = 128
ANNEAL_TEMP_VALUE = 0.02
SIDE = 8

EVERY = ("y_lo", "z", "y_hi", "x", "core")
SIZES = (2, 4, 2, 4, 2)


def place(y_lo, z, y_hi, x, core):
    return (((y_lo * 4 + z) * 2 + y_hi) * 4 + x) * 2 + core


def column_groups():
    groups = []
    for pair, x, core in itertools.product(range(2), range(4), range(2)):
        groups.append([place(lo, z, lo ^ pair, x, core) for lo in range(2) for z in range(4)])
    return groups


COLUMN_GROUPS = column_groups()
ROW_ORDER = ((0, 0), (1, 2), (1, 3), (1, 1), (0, 2), (0, 3), (0, 1), (1, 0))


def exchange_rows(blocks):
    return lax.all_to_all(blocks, ("y_lo", "x"), 0, 0, tiled=True)


def exchange_columns(blocks):
    return lax.all_to_all(blocks, EVERY, 0, 0, axis_index_groups=COLUMN_GROUPS, tiled=True)


def moved(x, flip, step):
    pairs = []
    for lo, z, hi, at, core in itertools.product(*map(range, SIZES)):
        pairs.append((place(lo ^ flip, z, hi, (at + step) % 4, core), place(lo, z, hi, at, core)))
    return lax.ppermute(x, EVERY, pairs)


def row_peers(x):
    return [moved(x, flip, step) if flip or step else x for flip, step in ROW_ORDER]


def member_at(offset):
    y_lo, x = lax.axis_index("y_lo"), lax.axis_index("x")
    flip, step = ROW_ORDER[offset]
    return ((1 - y_lo) if flip else y_lo) * 4 + (x + step) % 4


def halves(x):
    high = x.astype(jnp.bfloat16)
    return high, (x - high.astype(jnp.float32)).astype(jnp.bfloat16)


def product(a, b):
    return jnp.dot(a, b, preferred_element_type=jnp.float32)


def seed_member(seeds):
    labels = lax.broadcasted_iota(jnp.int32, (CLUSTER_COUNT, seeds.shape[1]), 0).astype(jnp.float32)
    return 0.5 * (labels == seeds).astype(jnp.float32).T + 0.5 / CLUSTER_COUNT


def tail_rows(*lines):
    at = lax.broadcasted_iota(jnp.int32, (SIDE, CLUSTER_COUNT), 0)
    tail = jnp.zeros((SIDE, CLUSTER_COUNT), jnp.float32)
    for index, line in enumerate(lines):
        tail = jnp.where(at == index, line, tail)
    return tail


def prepare_kernel(embedding, seeds, block, spread, labels, arrived):
    points, width = embedding.shape
    body, end = pl.ds(0, points), pl.ds(points, SIDE)
    loads = [
        pltpu.make_async_copy(embedding, block.at[body], arrived.at[0]),
        pltpu.make_async_copy(seeds, labels, arrived.at[1]),
    ]
    for load in loads:
        load.start()
    for load in loads:
        load.wait()
    x = block[body]
    side = jnp.concatenate([labels[...].astype(jnp.float32), jnp.sum((x * x).T, axis=0, keepdims=True)], axis=1)
    side = jnp.broadcast_to(side, (SIDE, width))
    block[end] = side
    for copy in range(spread.shape[0]):
        spread[copy, body] = x
        spread[copy, end] = side


CHUNK = 256


def set_columns(columns, right, line, member):
    points, width = columns.shape[1] - SIDE, columns.shape[2]
    for block in range(8):
        at = pl.ds(block * points, points)
        high, low = halves(columns[block, pl.ds(0, points)])
        right[at, pl.ds(0, width)] = high
        right[at, pl.ds(width, width)] = low
        right[at, pl.ds(2 * width, width)] = high
        side = columns[block, pl.ds(points, 1)]
        line[:, at] = jnp.broadcast_to(side[:, points:], (SIDE, points))
        member[at] = seed_member(side[:, :points]).astype(jnp.bfloat16)


def left_rows(x):
    high, low = halves(-2.0 * x)
    return jnp.concatenate([high, high, low], axis=1), jnp.sum(x * x, axis=1, keepdims=True) + 1.0


def distances(left, square, right, line, high_out, low_out, at):
    inner = lax.dot_general(left, right[...], (((1,), (1,)), ((), ())), preferred_element_type=jnp.float32)
    squared = inner + square + line[pl.ds(0, 1)]
    high_out[at], low_out[at] = halves(squared * lax.rsqrt(squared))


def weights(high, low, member, at):
    return product(high[at], member[...]) + product(low[at], member[...])


EARLY = 512


def own_pair_kernel(*refs):
    rows, (columns, left, squares, right, line, member, high, low, out) = refs[:4], refs[4:]
    points = rows[0].shape[0] - SIDE
    set_columns(columns, right, line, member)
    for offset, block in enumerate(rows):
        at = pl.ds(offset * points, points)
        left[at], squares[at] = left_rows(block[pl.ds(0, points)])
    for start in range(0, EARLY, CHUNK):
        at = pl.ds(start, CHUNK)
        distances(left[at], squares[at], right, line, high, low, at)
    out[...] = weights(high, low, member, pl.ds(0, EARLY))


def other_pair_kernel(columns, left, squares, weighted, right, line, member, high, low, out):
    set_columns(columns, right, line, member)
    for start in range(0, EARLY, CHUNK):
        at = pl.ds(start, CHUNK)
        distances(left[at], squares[at], right, line, high, low, at)
    out[...] = weighted[...] + weights(high, low, member, pl.ds(0, EARLY))


def late_pair_kernel(*refs):
    rows, sides, weighted, refs = refs[:8], (refs[8:11], refs[11:14]), refs[14], refs[19:]
    (*kept, out) = refs
    points = rows[0].shape[0] - SIDE
    late = 0.0
    for half, (right, line, member) in enumerate(sides):
        high, low = kept[2 * half : 2 * half + 2]
        for first in (4, 6):
            pair = rows[first : first + 2]
            left, square = left_rows(jnp.concatenate([block[pl.ds(0, points)] for block in pair], axis=0))
            distances(left, square, right, line, high, low, pl.ds(first * points, CHUNK))
        late += weights(high, low, member, pl.ds(EARLY, EARLY))
    cohesion = jnp.zeros((1, CLUSTER_COUNT), jnp.float32)
    for offset in range(8):
        start = offset * points
        part = weighted[pl.ds(start, points)] if start < EARLY else late[start - EARLY : start - EARLY + points]
        out[member_at(offset), pl.ds(0, points)] = part
        own = seed_member(rows[offset][pl.ds(points, 1)][:, :points])
        cohesion += jnp.sum(own * part, axis=0, keepdims=True)
    counts = jnp.sum(seed_member(rows[0][pl.ds(points, 1)][:, :points]), axis=0, keepdims=True)
    tail = tail_rows(cohesion, counts)
    for target in range(8):
        out[target, pl.ds(points, SIDE)] = tail


def member_kernel(own, other, own_high, own_low, other_high, other_low, first, out, own_member, both):
    points = own.shape[1] - SIDE
    sums = jnp.zeros((SIDE, CLUSTER_COUNT), jnp.float32)
    for block in range(8):
        sums += own[block, pl.ds(points, SIDE)] + other[block, pl.ds(points, SIDE)]
    cohesion, counts = sums[0:1], sums[1:2]
    own_member[...] = jnp.exp(log_softmax_energy(first[pl.ds(0, points)], counts, cohesion))
    sizes = jnp.zeros((1, CLUSTER_COUNT), jnp.float32)
    total = 0.0
    for source, high, low in ((own, own_high, own_low), (other, other_high, other_low)):
        for block in range(8):
            member = jnp.exp(log_softmax_energy(source[block, pl.ds(0, points)], counts, cohesion))
            sizes += jnp.sum(member, axis=0, keepdims=True)
            at = pl.ds(block * points, points)
            both[at, pl.ds(0, CLUSTER_COUNT)], both[at, pl.ds(CLUSTER_COUNT, CLUSTER_COUNT)] = halves(member)
        wide = product(high[...], both[...])
        total += product(low[...], both[:, pl.ds(0, CLUSTER_COUNT)])
        total += wide[:, :CLUSTER_COUNT] + wide[:, CLUSTER_COUNT:]
    tail = tail_rows(sizes)
    for block in range(8):
        out[member_at(block), pl.ds(0, points)] = total[block * points : (block + 1) * points]
        out[member_at(block), pl.ds(points, SIDE)] = tail


def summed(blocks):
    total = blocks[0]
    for block in range(1, 8):
        total += blocks[block]
    return total


def sum_kernel(blocks, out, spread):
    out[...] = summed(blocks)
    spread[...] = jnp.broadcast_to(out[...], spread.shape)


def own_kernel(blocks, own, out, part):
    points = own.shape[0]
    out[...] = summed(blocks)
    part[...] = jnp.sum(own[...] * out[pl.ds(0, points)], axis=0, keepdims=True)


def final_kernel(second, cohesion, out):
    points = out.shape[0]
    out[...] = log_softmax_energy(second[pl.ds(0, points)], second[pl.ds(points, 1)], cohesion[...])


PARAMS = pltpu.CompilerParams(vmem_limit_bytes=12 << 20)


def on_chip(kernel, name, shapes, inputs, scratch=(), aliases={}):
    vmem = pl.BlockSpec(memory_space=pltpu.VMEM)
    specs = [vmem] * len(inputs)
    shapes = [jax.ShapeDtypeStruct(*shape) for shape in shapes]
    return pl.pallas_call(
        kernel,
        out_shape=shapes,
        in_specs=specs,
        out_specs=[vmem] * len(shapes),
        scratch_shapes=scratch,
        input_output_aliases=aliases,
        compiler_params=PARAMS,
        name=name,
    )(*inputs)


def copies(x, count):
    return jnp.broadcast_to(x, (count, *x.shape))


def other_core(x):
    return lax.ppermute(x, "core", [(0, 1), (1, 0)])


def log_softmax_energy(attraction, counts, cohesion):
    energy = attraction / counts - cohesion / (2.0 * counts**2)
    logits = -energy / ANNEAL_TEMP_VALUE
    highest = jnp.max(logits, axis=1, keepdims=True)
    return logits - highest - jnp.log(jnp.sum(jnp.exp(logits - highest), axis=1, keepdims=True))


def shards(embedding, seed_cluster):
    points, width = embedding.shape
    lines, tall = points + SIDE, 8 * points
    outside, vmem = pl.BlockSpec(memory_space=pltpu.HBM), pl.BlockSpec(memory_space=pltpu.VMEM)
    block, spread = pl.pallas_call(
        prepare_kernel,
        out_shape=[jax.ShapeDtypeStruct((lines, width), jnp.float32), jax.ShapeDtypeStruct((8, lines, width), jnp.float32)],
        in_specs=[outside, outside],
        out_specs=[vmem, vmem],
        scratch_shapes=[pltpu.VMEM((1, points), jnp.int32), pltpu.SemaphoreType.DMA((2,))],
        name="prepare",
    )(embedding, seed_cluster.reshape(1, points))
    columns = exchange_columns(spread)
    rows = row_peers(block)
    columns, *rows[:5] = lax.optimization_barrier((columns, *rows[:5]))
    kept = ((tall, tall), jnp.bfloat16)
    exchange = ((8, lines, CLUSTER_COUNT), jnp.float32)
    sides = [((tall, 3 * width), jnp.bfloat16), ((SIDE, tall), jnp.float32), ((tall, CLUSTER_COUNT), jnp.bfloat16)]
    lefts = [((EARLY, 3 * width), jnp.bfloat16), ((EARLY, 1), jnp.float32)]
    early = ((EARLY, CLUSTER_COUNT), jnp.float32)
    left, squares, *own_sides, own_high, own_low, weighted = on_chip(
        own_pair_kernel, "own_pairs", [*lefts, *sides, kept, kept, early], [*rows[:4], columns]
    )
    *other_sides, other_high, other_low, weighted = on_chip(
        other_pair_kernel,
        "other_pairs",
        [*sides, kept, kept, early],
        [other_core(columns), left, squares, weighted],
    )
    own_high, own_low, other_high, other_low, weighted = on_chip(
        late_pair_kernel,
        "late_pairs",
        [kept] * 4 + [exchange],
        [*rows, *own_sides, *other_sides, weighted, own_high, own_low, other_high, other_low],
        aliases={15: 0, 16: 1, 17: 2, 18: 3},
    )

    line = ((lines, CLUSTER_COUNT), jnp.float32)
    first, spread = on_chip(sum_kernel, "sum_spread", [line, exchange], [exchange_rows(weighted)])
    firsts = exchange_columns(spread)
    weighted, own = on_chip(
        member_kernel,
        "members",
        [exchange, ((points, CLUSTER_COUNT), jnp.float32)],
        [firsts, other_core(firsts), own_high, own_low, other_high, other_low, first],
        scratch=[pltpu.VMEM((tall, 2 * CLUSTER_COUNT), jnp.bfloat16)],
    )

    part = ((1, CLUSTER_COUNT), jnp.float32)
    second, part = on_chip(own_kernel, "own_sums", [line, part], [exchange_rows(weighted), own])
    parts = lax.all_to_all(copies(part, 128), EVERY, 0, 0, tiled=True)
    (out,) = on_chip(
        final_kernel,
        "final",
        [((points, CLUSTER_COUNT), jnp.float32)],
        [second, jnp.sum(parts, axis=0)],
    )
    return out


def solution(mesh):
    finer = Mesh(mesh.devices.reshape(SIZES), EVERY)
    return jax.shard_map(
        shards, mesh=finer, in_specs=(P(EVERY, None), P(EVERY)), out_specs=P(EVERY, None), check_vma=False
    )
```

```python
import functools
import itertools

import jax
import jax.numpy as jnp
from jax import lax
from jax.experimental import pallas as pl
from jax.experimental.pallas import tpu as pltpu
from jax.sharding import Mesh
from jax.sharding import PartitionSpec as P

CLUSTER_COUNT = 128
ANNEAL_TEMP_VALUE = 0.02
SIDE = 8

EVERY = ("y_lo", "z", "y_hi", "x", "core")
SIZES = (2, 4, 2, 4, 2)


def place(y_lo, z, y_hi, x, core):
    return (((y_lo * 4 + z) * 2 + y_hi) * 4 + x) * 2 + core


def column_groups():
    groups = []
    for pair, x, core in itertools.product(range(2), range(4), range(2)):
        groups.append([place(lo, z, lo ^ pair, x, core) for lo in range(2) for z in range(4)])
    return groups


COLUMN_GROUPS = column_groups()
ROW_ORDER = ((0, 0), (1, 2), (1, 3), (1, 0), (0, 2), (0, 1), (0, 3), (1, 1))


def exchange_rows(blocks):
    return lax.all_to_all(blocks, ("y_lo", "x"), 0, 0, tiled=True)


def exchange_columns(blocks):
    return lax.all_to_all(blocks, EVERY, 0, 0, axis_index_groups=COLUMN_GROUPS, tiled=True)


def moved(x, flip, step):
    pairs = []
    for lo, z, hi, at, core in itertools.product(*map(range, SIZES)):
        pairs.append((place(lo ^ flip, z, hi, (at + step) % 4, core), place(lo, z, hi, at, core)))
    return lax.ppermute(x, EVERY, pairs)


def row_peers(x):
    return [moved(x, flip, step) if flip or step else x for flip, step in ROW_ORDER]


def member_at(offset):
    y_lo, x = lax.axis_index("y_lo"), lax.axis_index("x")
    flip, step = ROW_ORDER[offset]
    return ((1 - y_lo) if flip else y_lo) * 4 + (x + step) % 4


def halves(x):
    high = x.astype(jnp.bfloat16)
    return high, (x - high.astype(jnp.float32)).astype(jnp.bfloat16)


def product(a, b):
    return jnp.dot(a, b, preferred_element_type=jnp.float32)


def seed_member(seeds):
    labels = lax.broadcasted_iota(jnp.int32, (CLUSTER_COUNT, seeds.shape[1]), 0).astype(jnp.float32)
    return 0.5 * (labels == seeds).astype(jnp.float32).T + 0.5 / CLUSTER_COUNT


def tail_rows(*lines):
    at = lax.broadcasted_iota(jnp.int32, (SIDE, CLUSTER_COUNT), 0)
    tail = jnp.zeros((SIDE, CLUSTER_COUNT), jnp.float32)
    for index, line in enumerate(lines):
        tail = jnp.where(at == index, line, tail)
    return tail


def prepare_kernel(embedding, seeds, block, spread, labels, arrived):
    points, width = embedding.shape
    body, end = pl.ds(0, points), pl.ds(points, SIDE)
    loads = [
        pltpu.make_async_copy(embedding, block.at[body], arrived.at[0]),
        pltpu.make_async_copy(seeds, labels, arrived.at[1]),
    ]
    for load in loads:
        load.start()
    for load in loads:
        load.wait()
    x = block[body]
    side = jnp.concatenate([labels[...].astype(jnp.float32), jnp.sum((x * x).T, axis=0, keepdims=True)], axis=1)
    side = jnp.broadcast_to(side, (SIDE, width))
    block[end] = side
    for copy in range(spread.shape[0]):
        spread[copy, body] = x
        spread[copy, end] = side


CHUNK = 256


def set_columns(columns, right, line, member):
    points, width = columns.shape[1] - SIDE, columns.shape[2]
    for block in range(8):
        at = pl.ds(block * points, points)
        high, low = halves(columns[block, pl.ds(0, points)])
        right[at, pl.ds(0, width)] = high
        right[at, pl.ds(width, width)] = low
        right[at, pl.ds(2 * width, width)] = high
        side = columns[block, pl.ds(points, 1)]
        line[:, at] = jnp.broadcast_to(side[:, points:], (SIDE, points))
        member[at] = seed_member(side[:, :points]).astype(jnp.bfloat16)


def left_rows(x):
    high, low = halves(-2.0 * x)
    return jnp.concatenate([high, high, low], axis=1), jnp.sum(x * x, axis=1, keepdims=True) + 1.0


def distances(left, square, right, line, high_out, low_out, at):
    inner = lax.dot_general(left, right[...], (((1,), (1,)), ((), ())), preferred_element_type=jnp.float32)
    squared = inner + square + line[pl.ds(0, 1)]
    high_out[at], low_out[at] = halves(squared * lax.rsqrt(squared))


def weights(high, low, member, at):
    return product(high[at], member[...]) + product(low[at], member[...])


EARLY = 768


def own_pair_kernel(*refs):
    rows, (columns, left, squares, right, line, member, high, low, out) = refs[:6], refs[6:]
    points = rows[0].shape[0] - SIDE
    set_columns(columns, right, line, member)
    for offset, block in enumerate(rows):
        at = pl.ds(offset * points, points)
        left[at], squares[at] = left_rows(block[pl.ds(0, points)])
    for start in range(0, EARLY, CHUNK):
        at = pl.ds(start, CHUNK)
        distances(left[at], squares[at], right, line, high, low, at)
    out[...] = weights(high, low, member, pl.ds(0, EARLY))


def other_pair_kernel(columns, left, squares, weighted, right, line, member, high, low, out):
    set_columns(columns, right, line, member)
    for start in range(0, EARLY, CHUNK):
        at = pl.ds(start, CHUNK)
        distances(left[at], squares[at], right, line, high, low, at)
    out[...] = weighted[...] + weights(high, low, member, pl.ds(0, EARLY))


def late_pair_kernel(*refs):
    rows, sides, weighted, refs = refs[:8], (refs[8:11], refs[11:14]), refs[14], refs[19:]
    (*kept, out) = refs
    points = rows[0].shape[0] - SIDE
    at = pl.ds(EARLY, CHUNK)
    left, square = left_rows(jnp.concatenate([block[pl.ds(0, points)] for block in rows[6:]], axis=0))
    late = 0.0
    for half, (right, line, member) in enumerate(sides):
        high, low = kept[2 * half : 2 * half + 2]
        distances(left, square, right, line, high, low, at)
        late += weights(high, low, member, at)
    cohesion = jnp.zeros((1, CLUSTER_COUNT), jnp.float32)
    for offset in range(8):
        start = offset * points
        part = weighted[pl.ds(start, points)] if start < EARLY else late[start - EARLY : start - EARLY + points]
        out[member_at(offset), pl.ds(0, points)] = part
        own = seed_member(rows[offset][pl.ds(points, 1)][:, :points])
        cohesion += jnp.sum(own * part, axis=0, keepdims=True)
    counts = jnp.sum(seed_member(rows[0][pl.ds(points, 1)][:, :points]), axis=0, keepdims=True)
    tail = tail_rows(cohesion, counts)
    for target in range(8):
        out[target, pl.ds(points, SIDE)] = tail


def member_kernel(own, other, own_high, own_low, other_high, other_low, first, out, own_member, both):
    points = own.shape[1] - SIDE
    sums = jnp.zeros((SIDE, CLUSTER_COUNT), jnp.float32)
    for block in range(8):
        sums += own[block, pl.ds(points, SIDE)] + other[block, pl.ds(points, SIDE)]
    cohesion, counts = sums[0:1], sums[1:2]
    own_member[...] = jnp.exp(log_softmax_energy(first[pl.ds(0, points)], counts, cohesion))
    sizes = jnp.zeros((1, CLUSTER_COUNT), jnp.float32)
    total = 0.0
    for source, high, low in ((own, own_high, own_low), (other, other_high, other_low)):
        for block in range(8):
            member = jnp.exp(log_softmax_energy(source[block, pl.ds(0, points)], counts, cohesion))
            sizes += jnp.sum(member, axis=0, keepdims=True)
            at = pl.ds(block * points, points)
            both[at, pl.ds(0, CLUSTER_COUNT)], both[at, pl.ds(CLUSTER_COUNT, CLUSTER_COUNT)] = halves(member)
        wide = product(high[...], both[...])
        total += product(low[...], both[:, pl.ds(0, CLUSTER_COUNT)])
        total += wide[:, :CLUSTER_COUNT] + wide[:, CLUSTER_COUNT:]
    tail = tail_rows(sizes)
    for block in range(8):
        out[member_at(block), pl.ds(0, points)] = total[block * points : (block + 1) * points]
        out[member_at(block), pl.ds(points, SIDE)] = tail


def summed(blocks):
    total = blocks[0]
    for block in range(1, 8):
        total += blocks[block]
    return total


def sum_kernel(blocks, out, spread):
    out[...] = summed(blocks)
    spread[...] = jnp.broadcast_to(out[...], spread.shape)


def own_kernel(blocks, own, out, part):
    points = own.shape[0]
    out[...] = summed(blocks)
    part[...] = jnp.sum(own[...] * out[pl.ds(0, points)], axis=0, keepdims=True)


def final_kernel(second, cohesion, out):
    points = out.shape[0]
    out[...] = log_softmax_energy(second[pl.ds(0, points)], second[pl.ds(points, 1)], cohesion[...])


PARAMS = pltpu.CompilerParams(vmem_limit_bytes=12 << 20)


def on_chip(kernel, name, shapes, inputs, scratch=(), aliases={}):
    vmem = pl.BlockSpec(memory_space=pltpu.VMEM)
    specs = [vmem] * len(inputs)
    shapes = [jax.ShapeDtypeStruct(*shape) for shape in shapes]
    return pl.pallas_call(
        kernel,
        out_shape=shapes,
        in_specs=specs,
        out_specs=[vmem] * len(shapes),
        scratch_shapes=scratch,
        input_output_aliases=aliases,
        compiler_params=PARAMS,
        name=name,
    )(*inputs)


def copies(x, count):
    return jnp.broadcast_to(x, (count, *x.shape))


def other_core(x):
    return lax.ppermute(x, "core", [(0, 1), (1, 0)])


def log_softmax_energy(attraction, counts, cohesion):
    energy = attraction / counts - cohesion / (2.0 * counts**2)
    logits = -energy / ANNEAL_TEMP_VALUE
    highest = jnp.max(logits, axis=1, keepdims=True)
    return logits - highest - jnp.log(jnp.sum(jnp.exp(logits - highest), axis=1, keepdims=True))


def shards(embedding, seed_cluster):
    points, width = embedding.shape
    lines, tall = points + SIDE, 8 * points
    outside, vmem = pl.BlockSpec(memory_space=pltpu.HBM), pl.BlockSpec(memory_space=pltpu.VMEM)
    block, spread = pl.pallas_call(
        prepare_kernel,
        out_shape=[jax.ShapeDtypeStruct((lines, width), jnp.float32), jax.ShapeDtypeStruct((8, lines, width), jnp.float32)],
        in_specs=[outside, outside],
        out_specs=[vmem, vmem],
        scratch_shapes=[pltpu.VMEM((1, points), jnp.int32), pltpu.SemaphoreType.DMA((2,))],
        name="prepare",
    )(embedding, seed_cluster.reshape(1, points))
    columns = exchange_columns(spread)
    rows = row_peers(block)
    columns, *rows[:6] = lax.optimization_barrier((columns, *rows[:6]))
    kept = ((tall, tall), jnp.bfloat16)
    exchange = ((8, lines, CLUSTER_COUNT), jnp.float32)
    sides = [((tall, 3 * width), jnp.bfloat16), ((SIDE, tall), jnp.float32), ((tall, CLUSTER_COUNT), jnp.bfloat16)]
    lefts = [((EARLY, 3 * width), jnp.bfloat16), ((EARLY, 1), jnp.float32)]
    early = ((EARLY, CLUSTER_COUNT), jnp.float32)
    left, squares, *own_sides, own_high, own_low, weighted = on_chip(
        own_pair_kernel, "own_pairs", [*lefts, *sides, kept, kept, early], [*rows[:6], columns]
    )
    *other_sides, other_high, other_low, weighted = on_chip(
        other_pair_kernel,
        "other_pairs",
        [*sides, kept, kept, early],
        [other_core(columns), left, squares, weighted],
    )
    own_high, own_low, other_high, other_low, weighted = on_chip(
        late_pair_kernel,
        "late_pairs",
        [kept] * 4 + [exchange],
        [*rows, *own_sides, *other_sides, weighted, own_high, own_low, other_high, other_low],
        aliases={15: 0, 16: 1, 17: 2, 18: 3},
    )

    line = ((lines, CLUSTER_COUNT), jnp.float32)
    first, spread = on_chip(sum_kernel, "sum_spread", [line, exchange], [exchange_rows(weighted)])
    firsts = exchange_columns(spread)
    weighted, own = on_chip(
        member_kernel,
        "members",
        [exchange, ((points, CLUSTER_COUNT), jnp.float32)],
        [firsts, other_core(firsts), own_high, own_low, other_high, other_low, first],
        scratch=[pltpu.VMEM((tall, 2 * CLUSTER_COUNT), jnp.bfloat16)],
    )

    part = ((1, CLUSTER_COUNT), jnp.float32)
    second, part = on_chip(own_kernel, "own_sums", [line, part], [exchange_rows(weighted), own])
    parts = lax.all_to_all(copies(part, 128), EVERY, 0, 0, tiled=True)
    (out,) = on_chip(
        final_kernel,
        "final",
        [((points, CLUSTER_COUNT), jnp.float32)],
        [second, jnp.sum(parts, axis=0)],
    )
    return out


def solution(mesh):
    finer = Mesh(mesh.devices.reshape(SIZES), EVERY)
    return jax.shard_map(
        shards, mesh=finer, in_specs=(P(EVERY, None), P(EVERY)), out_specs=P(EVERY, None), check_vma=False
    )
```

```python
import functools
import itertools

import jax
import jax.numpy as jnp
from jax import lax
from jax.experimental import pallas as pl
from jax.experimental.pallas import tpu as pltpu
from jax.sharding import Mesh
from jax.sharding import PartitionSpec as P

CLUSTER_COUNT = 128
ANNEAL_TEMP_VALUE = 0.02
SIDE = 8

EVERY = ("y_lo", "z", "y_hi", "x", "core")
SIZES = (2, 4, 2, 4, 2)


def place(y_lo, z, y_hi, x, core):
    return (((y_lo * 4 + z) * 2 + y_hi) * 4 + x) * 2 + core


def column_groups():
    groups = []
    for pair, x, core in itertools.product(range(2), range(4), range(2)):
        groups.append([place(lo, z, lo ^ pair, x, core) for lo in range(2) for z in range(4)])
    return groups


COLUMN_GROUPS = column_groups()
ROW_ORDER = ((0, 0), (1, 2), (1, 3), (1, 0), (0, 2), (0, 1), (0, 3), (1, 1))


def exchange_rows(blocks):
    return lax.all_to_all(blocks, ("y_lo", "x"), 0, 0, tiled=True)


def exchange_columns(blocks):
    return lax.all_to_all(blocks, EVERY, 0, 0, axis_index_groups=COLUMN_GROUPS, tiled=True)


def moved(x, flip, step):
    pairs = []
    for lo, z, hi, at, core in itertools.product(*map(range, SIZES)):
        pairs.append((place(lo ^ flip, z, hi, (at + step) % 4, core), place(lo, z, hi, at, core)))
    return lax.ppermute(x, EVERY, pairs)


def row_peers(x):
    return [moved(x, flip, step) if flip or step else x for flip, step in ROW_ORDER]


def member_at(offset):
    y_lo, x = lax.axis_index("y_lo"), lax.axis_index("x")
    flip, step = ROW_ORDER[offset]
    return ((1 - y_lo) if flip else y_lo) * 4 + (x + step) % 4


def halves(x):
    high = x.astype(jnp.bfloat16)
    return high, (x - high.astype(jnp.float32)).astype(jnp.bfloat16)


def product(a, b):
    return jnp.dot(a, b, preferred_element_type=jnp.float32)


def seed_member(seeds):
    labels = lax.broadcasted_iota(jnp.int32, (CLUSTER_COUNT, seeds.shape[1]), 0).astype(jnp.float32)
    return 0.5 * (labels == seeds).astype(jnp.float32).T + 0.5 / CLUSTER_COUNT


def tail_rows(*lines):
    at = lax.broadcasted_iota(jnp.int32, (SIDE, CLUSTER_COUNT), 0)
    tail = jnp.zeros((SIDE, CLUSTER_COUNT), jnp.float32)
    for index, line in enumerate(lines):
        tail = jnp.where(at == index, line, tail)
    return tail


def prepare_kernel(embedding, seeds, block, spread, labels, arrived):
    points, width = embedding.shape
    body, end = pl.ds(0, points), pl.ds(points, SIDE)
    loads = [
        pltpu.make_async_copy(embedding, block.at[body], arrived.at[0]),
        pltpu.make_async_copy(seeds, labels, arrived.at[1]),
    ]
    for load in loads:
        load.start()
    for load in loads:
        load.wait()
    x = block[body]
    side = jnp.concatenate([labels[...].astype(jnp.float32), jnp.sum((x * x).T, axis=0, keepdims=True)], axis=1)
    side = jnp.broadcast_to(side, (SIDE, width))
    block[end] = side
    for copy in range(spread.shape[0]):
        spread[copy, body] = x
        spread[copy, end] = side


CHUNK = 256


def set_columns(columns, right, line, member):
    points, width = columns.shape[1] - SIDE, columns.shape[2]
    for block in range(8):
        at = pl.ds(block * points, points)
        high, low = halves(columns[block, pl.ds(0, points)])
        right[at, pl.ds(0, width)] = high
        right[at, pl.ds(width, width)] = low
        right[at, pl.ds(2 * width, width)] = high
        side = columns[block, pl.ds(points, 1)]
        line[:, at] = jnp.broadcast_to(side[:, points:], (SIDE, points))
        member[at] = seed_member(side[:, :points]).astype(jnp.bfloat16)


def left_rows(x):
    high, low = halves(-2.0 * x)
    return jnp.concatenate([high, high, low], axis=1), jnp.sum(x * x, axis=1, keepdims=True) + 1.0


def distances(left, square, right, line, high_out, low_out, at):
    inner = lax.dot_general(left, right[...], (((1,), (1,)), ((), ())), preferred_element_type=jnp.float32)
    squared = inner + square + line[pl.ds(0, 1)]
    high_out[at], low_out[at] = halves(squared * lax.rsqrt(squared))


def weights(high, low, member, at):
    return product(high[at], member[...]) + product(low[at], member[...])


EARLY = 768


def own_pair_kernel(*refs):
    rows, (columns, left, squares, right, line, member, high, low, out) = refs[:6], refs[6:]
    points = rows[0].shape[0] - SIDE
    set_columns(columns, right, line, member)
    for offset, block in enumerate(rows):
        at = pl.ds(offset * points, points)
        left[at], squares[at] = left_rows(block[pl.ds(0, points)])
    for start in range(0, EARLY, CHUNK):
        at = pl.ds(start, CHUNK)
        distances(left[at], squares[at], right, line, high, low, at)
    out[...] = weights(high, low, member, pl.ds(0, EARLY))


def other_pair_kernel(columns, left, squares, weighted, right, line, member, high, low, out):
    set_columns(columns, right, line, member)
    for start in range(0, EARLY, CHUNK):
        at = pl.ds(start, CHUNK)
        distances(left[at], squares[at], right, line, high, low, at)
    out[...] = weighted[...] + weights(high, low, member, pl.ds(0, EARLY))


def late_pair_kernel(*refs):
    rows, sides, weighted, refs = refs[:8], (refs[8:11], refs[11:14]), refs[14], refs[19:]
    (*kept, out) = refs
    points = rows[0].shape[0] - SIDE
    at = pl.ds(EARLY, CHUNK)
    left, square = left_rows(jnp.concatenate([block[pl.ds(0, points)] for block in rows[6:]], axis=0))
    late = 0.0
    for half, (right, line, member) in enumerate(sides):
        high, low = kept[2 * half : 2 * half + 2]
        distances(left, square, right, line, high, low, at)
        late += weights(high, low, member, at)
    cohesion = jnp.zeros((1, CLUSTER_COUNT), jnp.float32)
    for offset in range(8):
        start = offset * points
        part = weighted[pl.ds(start, points)] if start < EARLY else late[start - EARLY : start - EARLY + points]
        out[member_at(offset), pl.ds(0, points)] = part
        own = seed_member(rows[offset][pl.ds(points, 1)][:, :points])
        cohesion += jnp.sum(own * part, axis=0, keepdims=True)
    counts = jnp.sum(seed_member(rows[0][pl.ds(points, 1)][:, :points]), axis=0, keepdims=True)
    tail = tail_rows(cohesion, counts)
    for target in range(8):
        out[target, pl.ds(points, SIDE)] = tail


def tail_kernel(blocks, out):
    points = blocks.shape[1] - SIDE
    out[...] = sum(blocks[block, pl.ds(points, SIDE)] for block in range(8))


def half_product(source, sums, high, low, both):
    points = source.shape[1] - SIDE
    sizes = jnp.zeros((1, CLUSTER_COUNT), jnp.float32)
    for block in range(8):
        member = jnp.exp(log_softmax_energy(source[block, pl.ds(0, points)], sums[1:2], sums[0:1]))
        sizes += jnp.sum(member, axis=0, keepdims=True)
        at = pl.ds(block * points, points)
        both[at, pl.ds(0, CLUSTER_COUNT)], both[at, pl.ds(CLUSTER_COUNT, CLUSTER_COUNT)] = halves(member)
    wide = product(high[...], both[...])
    total = product(low[...], both[:, pl.ds(0, CLUSTER_COUNT)])
    return total + wide[:, :CLUSTER_COUNT] + wide[:, CLUSTER_COUNT:], sizes


def own_member_kernel(blocks, tail, far_tail, high, low, first, out, sums, own_member, both):
    points = own_member.shape[0]
    both_tails = tail[...] + far_tail[...]
    own_member[...] = jnp.exp(log_softmax_energy(first[pl.ds(0, points)], both_tails[1:2], both_tails[0:1]))
    out[...], sizes = half_product(blocks, both_tails, high, low, both)
    sums[...] = tail_rows(both_tails[0:1], both_tails[1:2], sizes)


def other_member_kernel(blocks, sums, high, low, weighted, out, both):
    points = blocks.shape[1] - SIDE
    total, sizes = half_product(blocks, sums[...], high, low, both)
    total += weighted[...]
    tail = tail_rows(sums[pl.ds(2, 1)] + sizes)
    for block in range(8):
        out[member_at(block), pl.ds(0, points)] = total[block * points : (block + 1) * points]
        out[member_at(block), pl.ds(points, SIDE)] = tail


def summed(blocks):
    total = blocks[0]
    for block in range(1, 8):
        total += blocks[block]
    return total


def sum_kernel(blocks, out, spread):
    out[...] = summed(blocks)
    spread[...] = jnp.broadcast_to(out[...], spread.shape)


def own_kernel(blocks, own, out, part):
    points = own.shape[0]
    out[...] = summed(blocks)
    part[...] = jnp.sum(own[...] * out[pl.ds(0, points)], axis=0, keepdims=True)


def final_kernel(second, cohesion, out):
    points = out.shape[0]
    out[...] = log_softmax_energy(second[pl.ds(0, points)], second[pl.ds(points, 1)], cohesion[...])


PARAMS = pltpu.CompilerParams(vmem_limit_bytes=12 << 20)


def on_chip(kernel, name, shapes, inputs, scratch=(), aliases={}):
    vmem = pl.BlockSpec(memory_space=pltpu.VMEM)
    specs = [vmem] * len(inputs)
    shapes = [jax.ShapeDtypeStruct(*shape) for shape in shapes]
    return pl.pallas_call(
        kernel,
        out_shape=shapes,
        in_specs=specs,
        out_specs=[vmem] * len(shapes),
        scratch_shapes=scratch,
        input_output_aliases=aliases,
        compiler_params=PARAMS,
        name=name,
    )(*inputs)


def copies(x, count):
    return jnp.broadcast_to(x, (count, *x.shape))


def other_core(x):
    return lax.ppermute(x, "core", [(0, 1), (1, 0)])


def log_softmax_energy(attraction, counts, cohesion):
    energy = attraction / counts - cohesion / (2.0 * counts**2)
    logits = -energy / ANNEAL_TEMP_VALUE
    highest = jnp.max(logits, axis=1, keepdims=True)
    return logits - highest - jnp.log(jnp.sum(jnp.exp(logits - highest), axis=1, keepdims=True))


def shards(embedding, seed_cluster):
    points, width = embedding.shape
    lines, tall = points + SIDE, 8 * points
    outside, vmem = pl.BlockSpec(memory_space=pltpu.HBM), pl.BlockSpec(memory_space=pltpu.VMEM)
    block, spread = pl.pallas_call(
        prepare_kernel,
        out_shape=[jax.ShapeDtypeStruct((lines, width), jnp.float32), jax.ShapeDtypeStruct((8, lines, width), jnp.float32)],
        in_specs=[outside, outside],
        out_specs=[vmem, vmem],
        scratch_shapes=[pltpu.VMEM((1, points), jnp.int32), pltpu.SemaphoreType.DMA((2,))],
        name="prepare",
    )(embedding, seed_cluster.reshape(1, points))
    columns = exchange_columns(spread)
    rows = row_peers(block)
    columns, *rows[:6] = lax.optimization_barrier((columns, *rows[:6]))
    kept = ((tall, tall), jnp.bfloat16)
    exchange = ((8, lines, CLUSTER_COUNT), jnp.float32)
    sides = [((tall, 3 * width), jnp.bfloat16), ((SIDE, tall), jnp.float32), ((tall, CLUSTER_COUNT), jnp.bfloat16)]
    lefts = [((EARLY, 3 * width), jnp.bfloat16), ((EARLY, 1), jnp.float32)]
    early = ((EARLY, CLUSTER_COUNT), jnp.float32)
    left, squares, *own_sides, own_high, own_low, weighted = on_chip(
        own_pair_kernel, "own_pairs", [*lefts, *sides, kept, kept, early], [*rows[:6], columns]
    )
    *other_sides, other_high, other_low, weighted = on_chip(
        other_pair_kernel,
        "other_pairs",
        [*sides, kept, kept, early],
        [other_core(columns), left, squares, weighted],
    )
    own_high, own_low, other_high, other_low, weighted = on_chip(
        late_pair_kernel,
        "late_pairs",
        [kept] * 4 + [exchange],
        [*rows, *own_sides, *other_sides, weighted, own_high, own_low, other_high, other_low],
        aliases={15: 0, 16: 1, 17: 2, 18: 3},
    )

    line = ((lines, CLUSTER_COUNT), jnp.float32)
    first, spread = on_chip(sum_kernel, "sum_spread", [line, exchange], [exchange_rows(weighted)])
    tail = ((SIDE, CLUSTER_COUNT), jnp.float32)
    firsts = exchange_columns(spread)
    (sums,) = on_chip(tail_kernel, "tails", [tail], [firsts])
    far_sums = other_core(sums)
    firsts, far_sums = lax.optimization_barrier((firsts, far_sums))
    both = [pltpu.VMEM((tall, 2 * CLUSTER_COUNT), jnp.bfloat16)]
    weighted, sums, own = on_chip(
        own_member_kernel,
        "own_members",
        [((tall, CLUSTER_COUNT), jnp.float32), tail, ((points, CLUSTER_COUNT), jnp.float32)],
        [firsts, sums, far_sums, own_high, own_low, first],
        scratch=both,
    )
    (weighted,) = on_chip(
        other_member_kernel,
        "other_members",
        [exchange],
        [other_core(firsts), sums, other_high, other_low, weighted],
        scratch=both,
    )

    part = ((1, CLUSTER_COUNT), jnp.float32)
    second, part = on_chip(own_kernel, "own_sums", [line, part], [exchange_rows(weighted), own])
    parts = lax.all_to_all(copies(part, 128), EVERY, 0, 0, tiled=True)
    (out,) = on_chip(
        final_kernel,
        "final",
        [((points, CLUSTER_COUNT), jnp.float32)],
        [second, jnp.sum(parts, axis=0)],
    )
    return out


def solution(mesh):
    finer = Mesh(mesh.devices.reshape(SIZES), EVERY)
    return jax.shard_map(
        shards, mesh=finer, in_specs=(P(EVERY, None), P(EVERY)), out_specs=P(EVERY, None), check_vma=False
    )
```

```python
import functools
import itertools

import jax
import jax.numpy as jnp
from jax import lax
from jax.experimental import pallas as pl
from jax.experimental.pallas import tpu as pltpu
from jax.sharding import Mesh
from jax.sharding import PartitionSpec as P

CLUSTER_COUNT = 128
ANNEAL_TEMP_VALUE = 0.02
SIDE = 8

EVERY = ("y_lo", "z", "y_hi", "x", "core")
SIZES = (2, 4, 2, 4, 2)


def place(y_lo, z, y_hi, x, core):
    return (((y_lo * 4 + z) * 2 + y_hi) * 4 + x) * 2 + core


def column_groups():
    groups = []
    for pair, x, core in itertools.product(range(2), range(4), range(2)):
        groups.append([place(lo, z, lo ^ pair, x, core) for lo in range(2) for z in range(4)])
    return groups


COLUMN_GROUPS = column_groups()
ROW_ORDER = ((0, 0), (1, 2), (1, 3), (1, 1), (0, 2), (0, 3), (1, 0), (0, 1))


def exchange_rows(blocks):
    return lax.all_to_all(blocks, ("y_lo", "x"), 0, 0, tiled=True)


def exchange_columns(blocks):
    return lax.all_to_all(blocks, EVERY, 0, 0, axis_index_groups=COLUMN_GROUPS, tiled=True)


def moved(x, flip, step):
    pairs = []
    for lo, z, hi, at, core in itertools.product(*map(range, SIZES)):
        pairs.append((place(lo ^ flip, z, hi, (at + step) % 4, core), place(lo, z, hi, at, core)))
    return lax.ppermute(x, EVERY, pairs)


def row_peers(x):
    return [moved(x, flip, step) if flip or step else x for flip, step in ROW_ORDER]


def member_at(offset):
    y_lo, x = lax.axis_index("y_lo"), lax.axis_index("x")
    flip, step = ROW_ORDER[offset]
    return ((1 - y_lo) if flip else y_lo) * 4 + (x + step) % 4


def halves(x):
    high = x.astype(jnp.bfloat16)
    return high, (x - high.astype(jnp.float32)).astype(jnp.bfloat16)


def product(a, b):
    return jnp.dot(a, b, preferred_element_type=jnp.float32)


def seed_member(seeds):
    labels = lax.broadcasted_iota(jnp.int32, (CLUSTER_COUNT, seeds.shape[1]), 0).astype(jnp.float32)
    return 0.5 * (labels == seeds).astype(jnp.float32).T + 0.5 / CLUSTER_COUNT


def tail_rows(*lines):
    at = lax.broadcasted_iota(jnp.int32, (SIDE, CLUSTER_COUNT), 0)
    tail = jnp.zeros((SIDE, CLUSTER_COUNT), jnp.float32)
    for index, line in enumerate(lines):
        tail = jnp.where(at == index, line, tail)
    return tail


def prepare_kernel(embedding, seeds, block, spread, labels, arrived):
    points, width = embedding.shape
    body, end = pl.ds(0, points), pl.ds(points, SIDE)
    loads = [
        pltpu.make_async_copy(embedding, block.at[body], arrived.at[0]),
        pltpu.make_async_copy(seeds, labels, arrived.at[1]),
    ]
    for load in loads:
        load.start()
    for load in loads:
        load.wait()
    x = block[body]
    side = jnp.concatenate([labels[...].astype(jnp.float32), jnp.sum((x * x).T, axis=0, keepdims=True)], axis=1)
    side = jnp.broadcast_to(side, (SIDE, width))
    block[end] = side
    for copy in range(spread.shape[0]):
        spread[copy, body] = x
        spread[copy, end] = side


CHUNK = 256


def set_columns(columns, right, line, member):
    points, width = columns.shape[1] - SIDE, columns.shape[2]
    for block in range(8):
        at = pl.ds(block * points, points)
        high, low = halves(columns[block, pl.ds(0, points)])
        right[at, pl.ds(0, width)] = high
        right[at, pl.ds(width, width)] = low
        right[at, pl.ds(2 * width, width)] = high
        side = columns[block, pl.ds(points, 1)]
        line[:, at] = jnp.broadcast_to(side[:, points:], (SIDE, points))
        member[at] = seed_member(side[:, :points]).astype(jnp.bfloat16)


def left_rows(x):
    high, low = halves(-2.0 * x)
    return jnp.concatenate([high, high, low], axis=1), jnp.sum(x * x, axis=1, keepdims=True) + 1.0


def distances(left, square, right, line, high_out, low_out, at):
    inner = lax.dot_general(left, right[...], (((1,), (1,)), ((), ())), preferred_element_type=jnp.float32)
    squared = inner + square + line[pl.ds(0, 1)]
    high_out[at], low_out[at] = halves(squared * lax.rsqrt(squared))


def weights(high, low, member, at):
    return product(high[at], member[...]) + product(low[at], member[...])


EARLY = 768


def own_pair_kernel(*refs):
    rows, (columns, left, squares, right, line, member, high, low, out) = refs[:6], refs[6:]
    points = rows[0].shape[0] - SIDE
    set_columns(columns, right, line, member)
    for offset, block in enumerate(rows):
        at = pl.ds(offset * points, points)
        left[at], squares[at] = left_rows(block[pl.ds(0, points)])
    for start in range(0, EARLY, CHUNK):
        at = pl.ds(start, CHUNK)
        distances(left[at], squares[at], right, line, high, low, at)
    out[...] = weights(high, low, member, pl.ds(0, EARLY))


def other_pair_kernel(columns, left, squares, weighted, right, line, member, high, low, out):
    set_columns(columns, right, line, member)
    for start in range(0, EARLY, CHUNK):
        at = pl.ds(start, CHUNK)
        distances(left[at], squares[at], right, line, high, low, at)
    out[...] = weighted[...] + weights(high, low, member, pl.ds(0, EARLY))


def late_pair_kernel(*refs):
    rows, sides, weighted, refs = refs[:8], (refs[8:11], refs[11:14]), refs[14], refs[19:]
    (*kept, out) = refs
    points = rows[0].shape[0] - SIDE
    at = pl.ds(EARLY, CHUNK)
    left, square = left_rows(jnp.concatenate([block[pl.ds(0, points)] for block in rows[6:]], axis=0))
    late = 0.0
    for half, (right, line, member) in enumerate(sides):
        high, low = kept[2 * half : 2 * half + 2]
        distances(left, square, right, line, high, low, at)
        late += weights(high, low, member, at)
    cohesion = jnp.zeros((1, CLUSTER_COUNT), jnp.float32)
    for offset in range(8):
        start = offset * points
        part = weighted[pl.ds(start, points)] if start < EARLY else late[start - EARLY : start - EARLY + points]
        out[member_at(offset), pl.ds(0, points)] = part
        own = seed_member(rows[offset][pl.ds(points, 1)][:, :points])
        cohesion += jnp.sum(own * part, axis=0, keepdims=True)
    counts = jnp.sum(seed_member(rows[0][pl.ds(points, 1)][:, :points]), axis=0, keepdims=True)
    tail = tail_rows(cohesion, counts)
    for target in range(8):
        out[target, pl.ds(points, SIDE)] = tail


def member_kernel(own, other, own_high, own_low, other_high, other_low, first, out, own_member, both):
    points = own.shape[1] - SIDE
    sums = jnp.zeros((SIDE, CLUSTER_COUNT), jnp.float32)
    for block in range(8):
        sums += own[block, pl.ds(points, SIDE)] + other[block, pl.ds(points, SIDE)]
    cohesion, counts = sums[0:1], sums[1:2]
    own_member[...] = jnp.exp(log_softmax_energy(first[pl.ds(0, points)], counts, cohesion))
    sizes = jnp.zeros((1, CLUSTER_COUNT), jnp.float32)
    total = 0.0
    for source, high, low in ((own, own_high, own_low), (other, other_high, other_low)):
        for block in range(8):
            member = jnp.exp(log_softmax_energy(source[block, pl.ds(0, points)], counts, cohesion))
            sizes += jnp.sum(member, axis=0, keepdims=True)
            at = pl.ds(block * points, points)
            both[at, pl.ds(0, CLUSTER_COUNT)], both[at, pl.ds(CLUSTER_COUNT, CLUSTER_COUNT)] = halves(member)
        wide = product(high[...], both[...])
        total += product(low[...], both[:, pl.ds(0, CLUSTER_COUNT)])
        total += wide[:, :CLUSTER_COUNT] + wide[:, CLUSTER_COUNT:]
    tail = tail_rows(sizes)
    for block in range(8):
        out[member_at(block), pl.ds(0, points)] = total[block * points : (block + 1) * points]
        out[member_at(block), pl.ds(points, SIDE)] = tail


def summed(blocks):
    total = blocks[0]
    for block in range(1, 8):
        total += blocks[block]
    return total


def sum_kernel(blocks, out, spread):
    out[...] = summed(blocks)
    spread[...] = jnp.broadcast_to(out[...], spread.shape)


def own_kernel(blocks, own, out, part):
    points = own.shape[0]
    out[...] = summed(blocks)
    part[...] = jnp.sum(own[...] * out[pl.ds(0, points)], axis=0, keepdims=True)


def final_kernel(second, cohesion, out):
    points = out.shape[0]
    out[...] = log_softmax_energy(second[pl.ds(0, points)], second[pl.ds(points, 1)], cohesion[...])


PARAMS = pltpu.CompilerParams(vmem_limit_bytes=12 << 20)


def on_chip(kernel, name, shapes, inputs, scratch=(), aliases={}):
    vmem = pl.BlockSpec(memory_space=pltpu.VMEM)
    specs = [vmem] * len(inputs)
    shapes = [jax.ShapeDtypeStruct(*shape) for shape in shapes]
    return pl.pallas_call(
        kernel,
        out_shape=shapes,
        in_specs=specs,
        out_specs=[vmem] * len(shapes),
        scratch_shapes=scratch,
        input_output_aliases=aliases,
        compiler_params=PARAMS,
        name=name,
    )(*inputs)


def copies(x, count):
    return jnp.broadcast_to(x, (count, *x.shape))


def other_core(x):
    return lax.ppermute(x, "core", [(0, 1), (1, 0)])


def log_softmax_energy(attraction, counts, cohesion):
    energy = attraction / counts - cohesion / (2.0 * counts**2)
    logits = -energy / ANNEAL_TEMP_VALUE
    highest = jnp.max(logits, axis=1, keepdims=True)
    return logits - highest - jnp.log(jnp.sum(jnp.exp(logits - highest), axis=1, keepdims=True))


def shards(embedding, seed_cluster):
    points, width = embedding.shape
    lines, tall = points + SIDE, 8 * points
    outside, vmem = pl.BlockSpec(memory_space=pltpu.HBM), pl.BlockSpec(memory_space=pltpu.VMEM)
    block, spread = pl.pallas_call(
        prepare_kernel,
        out_shape=[jax.ShapeDtypeStruct((lines, width), jnp.float32), jax.ShapeDtypeStruct((8, lines, width), jnp.float32)],
        in_specs=[outside, outside],
        out_specs=[vmem, vmem],
        scratch_shapes=[pltpu.VMEM((1, points), jnp.int32), pltpu.SemaphoreType.DMA((2,))],
        name="prepare",
    )(embedding, seed_cluster.reshape(1, points))
    columns = exchange_columns(spread)
    rows = row_peers(block)
    columns, *rows[:6] = lax.optimization_barrier((columns, *rows[:6]))
    kept = ((tall, tall), jnp.bfloat16)
    exchange = ((8, lines, CLUSTER_COUNT), jnp.float32)
    sides = [((tall, 3 * width), jnp.bfloat16), ((SIDE, tall), jnp.float32), ((tall, CLUSTER_COUNT), jnp.bfloat16)]
    lefts = [((EARLY, 3 * width), jnp.bfloat16), ((EARLY, 1), jnp.float32)]
    early = ((EARLY, CLUSTER_COUNT), jnp.float32)
    left, squares, *own_sides, own_high, own_low, weighted = on_chip(
        own_pair_kernel, "own_pairs", [*lefts, *sides, kept, kept, early], [*rows[:6], columns]
    )
    *other_sides, other_high, other_low, weighted = on_chip(
        other_pair_kernel,
        "other_pairs",
        [*sides, kept, kept, early],
        [other_core(columns), left, squares, weighted],
    )
    own_high, own_low, other_high, other_low, weighted = on_chip(
        late_pair_kernel,
        "late_pairs",
        [kept] * 4 + [exchange],
        [*rows, *own_sides, *other_sides, weighted, own_high, own_low, other_high, other_low],
        aliases={15: 0, 16: 1, 17: 2, 18: 3},
    )

    line = ((lines, CLUSTER_COUNT), jnp.float32)
    first, spread = on_chip(sum_kernel, "sum_spread", [line, exchange], [exchange_rows(weighted)])
    firsts = exchange_columns(spread)
    weighted, own = on_chip(
        member_kernel,
        "members",
        [exchange, ((points, CLUSTER_COUNT), jnp.float32)],
        [firsts, other_core(firsts), own_high, own_low, other_high, other_low, first],
        scratch=[pltpu.VMEM((tall, 2 * CLUSTER_COUNT), jnp.bfloat16)],
    )

    part = ((1, CLUSTER_COUNT), jnp.float32)
    second, part = on_chip(own_kernel, "own_sums", [line, part], [exchange_rows(weighted), own])
    parts = lax.all_to_all(copies(part, 128), EVERY, 0, 0, tiled=True)
    (out,) = on_chip(
        final_kernel,
        "final",
        [((points, CLUSTER_COUNT), jnp.float32)],
        [second, jnp.sum(parts, axis=0)],
    )
    return out


def solution(mesh):
    finer = Mesh(mesh.devices.reshape(SIZES), EVERY)
    return jax.shard_map(
        shards, mesh=finer, in_specs=(P(EVERY, None), P(EVERY)), out_specs=P(EVERY, None), check_vma=False
    )
```
